256 devices in a mesh: section: 8 (over z_lo, x), dp: 32 (over y, z_hi, core).
Axes of the slice: x: 4, y: 4, z: 8 (z_hi: 4, z_lo: 2; z = z_hi * 2 + z_lo), core: 2. Of those that a mesh axis runs over, the one named last changes fastest.
Arguments:
- hidden: bfloat16 [8, 4096, 8192], P('section', 'dp'), may hold values from -6 to 6
- gain_table: bfloat16 [40, 8192], replicated, may hold values from 0.099609375 to 1.8984375
- layer_counts: int32 [8], P('section'), may hold values from 1 to 8, 40 in all
- positions: int32 [8, 4096], P('section', 'dp'), may hold values from 0 to 8191, as said below
- queries: bfloat16 [8, 4096, 4096], P('section', 'dp'), may hold values from -35 to 35
- keys: bfloat16 [8, 4096, 512], P('section', 'dp'), may hold values from -10 to 10
- value_weight: bfloat16 [8, 8192, 512], P('section', 'dp'), may hold values from -0.0625 to 0.0625
- out_grad: bfloat16 [8, 4096, 4096], P('section', 'dp'), may hold values from -6 to 6
Outputs:
- query_grad: bfloat16 [8, 4096, 4096], P('section', 'dp')
- key_grad: bfloat16 [8, 4096, 512], P('section', 'dp')
- value_weight_grad: bfloat16 [8, 8192, 512], P('section', 'dp')
- upstream_grad: bfloat16 [8, 4096, 8192], P('section', 'dp')
The draws below stay inside these ranges and needn't reach their ends.
Inputs may be any that keep to these rules, and one draw needn't show every extreme that they name: Within each device's block of 128 tokens the positions rise by 1 to 3 from token to token.
All inputs are finite; a program needn't handle non-finite values. No bound on the sum of `layer_counts` on one device may be relied on, other than what follows from the above.
Results may differ from the reference program's by a relative error of at most 0.02.
Values may be sent and summed in bfloat16 or wider, within the bound.
A program may use at most 128 MiB of HBM per device.

```python
import math
import jax
import jax.numpy as jnp
import numpy as np
from jax import lax

D = 8192
HQ = 32
HK = 4
HD = 128
TOK_DEV = 128
MOST_LAYERS = 8
MAXPOS = 8192
SECTIONS = 8
TOKENS = 4096
LAYERS = 40


def draw_pair(key):
    base = jax.random.fold_in(key, 11)
    key_keys, key_queries = jax.random.split(base, 2)
    share = HQ // HK
    keys_raw = jnp.clip(jax.random.normal(key_keys, (SECTIONS, TOKENS, HK, HD), jnp.float32), -4.0, 4.0)
    queries_raw = jnp.clip(jax.random.normal(key_queries, (SECTIONS, TOKENS, HK, share, HD), jnp.float32), -4.0, 4.0)
    return (queries_raw.reshape(SECTIONS, TOKENS, HQ * HD), keys_raw.reshape(SECTIONS, TOKENS, HK * HD))


def draw_queries(key, part):
    return draw_pair(key)[0].astype(jnp.bfloat16)


def draw_keys(key, part):
    return draw_pair(key)[1].astype(jnp.bfloat16)


def draw_positions(key, part):
    blocks = TOKENS // TOK_DEV
    key_step, key_start = jax.random.split(jax.random.fold_in(key, 5), 2)
    steps = jax.random.randint(key_step, (SECTIONS, blocks, TOK_DEV), 1, 4, jnp.int32)
    steps = steps.at[:, :, 0].set(0)
    offsets = jnp.cumsum(steps, axis=2).astype(jnp.int32)
    span = offsets[:, :, TOK_DEV - 1]
    room = (MAXPOS - span).astype(jnp.int32)
    drawn = jax.random.randint(key_start, (SECTIONS, blocks), 0, 1048576, jnp.int32)
    starts = (drawn % room).astype(jnp.int32)
    starts = starts.at[0, 0].set(room[0, 0] - 1)
    starts = starts.at[0, blocks - 1].set(0)
    return (starts[:, :, None] + offsets).reshape(SECTIONS, TOKENS).astype(jnp.int32)


def with_spikes(result, key, source, target, blocks, factor):
    owner, partner = [(jnp.arange(result.shape[axis_at]) // (result.shape[axis_at] // blocks)).reshape([-1 if axis == axis_at else 1 for axis in range(result.ndim)]) for axis_at in (source, target)]
    chosen = jax.random.permutation(key, blocks)[partner]
    strong = (owner == chosen) | (owner == (partner + blocks // 2) % blocks)
    return jnp.where(strong, factor * result, result)


def steps_of(own_key, shape, cuts, low, top_value):
    level, own = 1.0, jax.random.fold_in(own_key, 6)
    for dim, shards_of in cuts:
        draws = jnp.exp(jax.random.uniform(jax.random.fold_in(own, dim), (shards_of,), jnp.float32, low / len(cuts), top_value / len(cuts)))
        level = level * jnp.repeat(draws, shape[dim] // shards_of).reshape([-1 if axis == dim else 1 for axis in range(len(shape))])
    return level


def length_profile(number_of, total, limit, skew):
    portions = [(1 << 20) // math.isqrt(grade ** skew) + 1 for grade in range(2, number_of + 1)]
    surplus, counts = total - limit - (number_of - 1), [1] * (number_of - 1)
    while surplus > 0:
        free = [i for i in range(number_of - 1) if counts[i] < limit]
        whole, left = sum([portions[i] for i in free]), surplus
        for i in free:
            addition = min(limit - counts[i], max(1, left * portions[i] // whole), surplus)
            counts[i] = counts[i] + addition
            surplus = surplus - addition
    return np.array([limit] + counts)


def ragged_sizes(own_key, amount, total, most, slope):
    if amount == 2:
        one = jax.random.randint(own_key, (), max(1, total - most), min(most, total - 1) + 1)
        return jnp.stack([one, total - one])
    tallies = jnp.asarray(length_profile(amount, total, most, slope), jnp.int32)
    twos = (amount - 1) // 2
    source_of, taker = tallies[1:1 + 2 * twos:2], tallies[2:2 + 2 * twos:2]
    slack = jnp.minimum(source_of - 1, most - taker)
    shifted = jax.random.randint(jax.random.fold_in(own_key, 1), (twos,), 0, 1 << 20) % (slack + 1)
    tallies = tallies.at[1:1 + 2 * twos:2].set(source_of - shifted).at[2:2 + 2 * twos:2].set(taker + shifted)
    return tallies[jax.random.permutation(jax.random.fold_in(own_key, 2), amount)]


def centred(key, extent, scale, reach, pieces=(), kind=jnp.bfloat16):
    values = scale * jax.random.normal(key, extent, jnp.float32)
    if pieces:
        values = values * steps_of(key, extent, pieces, -0.22, 0.18)
    return jnp.clip(values, -reach, reach).astype(kind)


def bell_draw_with(key, dims, deviation, limit, cuts, heavy, held_as=jnp.bfloat16):
    values = deviation * jax.random.normal(key, dims, jnp.float32)
    if cuts:
        values = values * steps_of(key, dims, cuts, -0.22, 0.18)
    return jnp.clip(with_spikes(values, jax.random.fold_in(key, 3), *heavy), -limit, limit).astype(held_as)


def setup_inputs(seed: int = 0) -> dict:
    key_list = jax.random.split(jax.random.key(seed), 9)
    return {
        "hidden": bell_draw_with(key_list[0], (SECTIONS, TOKENS, D), 1.0, 6.0, ((0, 8), (1, 32)), (1, 2, 32, 2.75)),
        "gain_table": jnp.clip(1.0 + 0.18 * jax.random.normal(key_list[1], (LAYERS, D), jnp.float32), 0.099609375, 1.8984375).astype(jnp.bfloat16),
        "layer_counts": ragged_sizes(key_list[2], SECTIONS, LAYERS, MOST_LAYERS, 2).astype(jnp.int32),
        "positions": draw_positions(jax.random.fold_in(key_list[8], 71), 0),
        "queries": draw_queries(jax.random.fold_in(key_list[8], 71), 0),
        "keys": draw_keys(jax.random.fold_in(key_list[8], 71), 0),
        "value_weight": centred(key_list[6], (SECTIONS, D, HK * HD), D ** -0.5, 0.0625, ((0, 8), (1, 32))),
        "out_grad": centred(key_list[7], (SECTIONS, TOKENS, HQ * HD), 1.0, 6.0, ((0, 8), (1, 32))),
    }


def rope_angles(places, width):
    half = width // 2
    steps = jnp.arange(half, dtype=jnp.float32)
    freq = jnp.exp(steps * (-2.0 * math.log(500000.0) / width))
    angle = places.astype(jnp.float32)[:, None] * freq[None, :]
    return (jnp.cos(angle), jnp.sin(angle))

def rotate(values, cosine, sine, heads, width):
    rows_here = values.shape[0]
    split = values.reshape(rows_here, heads, 2, width // 2)
    first = split[:, :, 0, :]
    second = split[:, :, 1, :]
    cosine = cosine[:, None, :]
    sine = sine[:, None, :]
    turned = jnp.stack([first * cosine - second * sine, first * sine + second * cosine], axis=2)
    return turned.reshape(rows_here, heads * width)

def attend_back(q_rot, k_rot, v_low, d_out, heads, groups, width):
    rows_here = q_rot.shape[0]
    share = heads // groups
    scale = width ** (-0.5)
    q_four = q_rot.astype(jnp.float32).reshape(rows_here, groups, share, width)
    k_three = k_rot.astype(jnp.float32).reshape(rows_here, groups, width)
    v_three = v_low.astype(jnp.float32).reshape(rows_here, groups, width)
    d_four = d_out.astype(jnp.float32).reshape(rows_here, groups, share, width)
    scores = jnp.einsum('tgrd,ugd->grtu', q_four, k_three) * scale
    later = jnp.arange(rows_here)[:, None] >= jnp.arange(rows_here)[None, :]
    scores = jnp.where(later, scores, -1e+30)
    top = lax.optimization_barrier(jnp.max(scores, axis=-1, keepdims=True))
    expo = jnp.exp(scores - top)
    probs = expo / lax.optimization_barrier(jnp.sum(expo, axis=-1, keepdims=True))
    probs_low = lax.optimization_barrier(probs.astype(jnp.bfloat16)).astype(jnp.float32)
    attended = jnp.einsum('grtu,ugd->tgrd', probs_low, v_three)
    delta = lax.optimization_barrier(jnp.sum(d_four * attended, axis=-1))
    delta = jnp.transpose(delta, (1, 2, 0))[..., None]
    d_probs = jnp.einsum('tgrd,ugd->grtu', d_four, v_three)
    d_scores = (probs * (d_probs - delta) * scale).astype(jnp.bfloat16)
    d_scores = lax.optimization_barrier(d_scores).astype(jnp.float32)
    dq_rot = jnp.einsum('grtu,ugd->tgrd', d_scores, k_three).reshape(rows_here, heads * width)
    dk_rot = jnp.einsum('grtu,tgrd->ugd', d_scores, q_four).reshape(rows_here, groups * width)
    d_values = jnp.einsum('grtu,tgrd->ugd', probs_low, d_four).reshape(rows_here, groups * width)
    return (dq_rot, dk_rot, d_values)

def section_terms(hidden, gain, places, queries, keys, weight, out_grad):
    hidden_f = hidden.astype(jnp.float32)
    gain_f = gain.astype(jnp.float32)
    inverse = lax.rsqrt(lax.optimization_barrier(jnp.mean(hidden_f * hidden_f, axis=-1, keepdims=True)) + 1e-05)
    normed = (hidden_f * inverse * gain_f).astype(jnp.bfloat16)
    values = jnp.dot(normed, weight, preferred_element_type=jnp.float32).astype(jnp.bfloat16)

    def one_sequence(block):
        place_b, query_b, key_b, value_b, grad_b = block
        cosine, sine = rope_angles(place_b, HD)
        q_rot = rotate(query_b.astype(jnp.float32), cosine, sine, HQ, HD).astype(jnp.bfloat16)
        k_rot = rotate(key_b.astype(jnp.float32), cosine, sine, HK, HD).astype(jnp.bfloat16)
        dq_rot, dk_rot, d_values = attend_back(q_rot, k_rot, value_b, grad_b, HQ, HK, HD)
        query_grad = rotate(dq_rot, cosine, -sine, HQ, HD).astype(jnp.bfloat16)
        key_grad = rotate(dk_rot, cosine, -sine, HK, HD).astype(jnp.bfloat16)
        return (query_grad, key_grad, d_values.astype(jnp.bfloat16))
    seqs_here = hidden.shape[0] // TOK_DEV
    blocks = (places.reshape(seqs_here, TOK_DEV), queries.reshape(seqs_here, TOK_DEV, HQ * HD), keys.reshape(seqs_here, TOK_DEV, HK * HD), values.reshape(seqs_here, TOK_DEV, HK * HD), out_grad.reshape(seqs_here, TOK_DEV, HQ * HD))
    query_grad, key_grad, values_grad = lax.map(one_sequence, blocks)
    query_grad = query_grad.reshape(-1, HQ * HD)
    key_grad = key_grad.reshape(-1, HK * HD)
    values_grad = values_grad.reshape(-1, HK * HD)
    weight_grad = jnp.dot(normed.T, values_grad, preferred_element_type=jnp.float32).astype(jnp.bfloat16)
    d_normed = jnp.dot(values_grad, weight.T, preferred_element_type=jnp.float32)
    scaled = gain_f * d_normed
    local_grad = inverse * scaled - hidden_f * inverse ** 3 * lax.optimization_barrier(jnp.mean(hidden_f * scaled, axis=-1, keepdims=True))
    return (query_grad, key_grad, weight_grad, local_grad.astype(jnp.bfloat16))

def reference(hidden, gain_table, layer_counts, positions, queries, keys, value_weight, out_grad):
    last = (jnp.cumsum(layer_counts) - 1).astype(jnp.int32)
    gains = jnp.take(gain_table, last, axis=0)

    def one_section(block):
        return section_terms(*block)
    query_grad, key_grad, weight_grad, local_grad = lax.map(one_section, (hidden, gains, positions, queries, keys, value_weight, out_grad))
    upstream = jnp.concatenate([local_grad[1:], jnp.zeros_like(local_grad[:1])], axis=0)
    return (query_grad, key_grad, weight_grad, upstream)
```

```python
import functools
import math

import jax
import jax.numpy as jnp
from jax import lax
from jax.experimental import pallas as pl
from jax.experimental.pallas import tpu as pltpu
from jax.sharding import PartitionSpec as P

HQ = 32
HK = 4
HD = 128
SHARE = HQ // HK
SCALE = HD ** (-0.5)
T = 128
D = 8192
E = HK * HD
SH = 256
NS = 8
MESH = pl.DeviceIdType.MESH
F32 = jnp.float32
BF16 = jnp.bfloat16

COLOURS = (("z", "y", 0, 384), ("y", "z", 384, 128))
OFFS = (0, 3, 1, 2)
RS_OFFS = (2, 1, 3, 0)
NT = (((1,), (1,)), ((), ()))
TN = (((0,), (0,)), ((), ()))


def dot(a, b, dims=(((1,), (0,)), ((), ()))):
    return lax.dot_general(a, b, dims, preferred_element_type=F32)


def turn(x, cosine, sine):
    return x * cosine + pltpu.roll(x, HD // 2, 1) * sine


def kernel(
    hid_hbm, gt_hbm, cnt_ref, cos_ref, sin_ref, q_hbm, k_hbm, w_hbm, og_hbm,
    qg_hbm, kg_hbm, wg_hbm, up_hbm,
    hid, gt, q, k, og, wf, normed, pnorm, gain, krot, qrot, probs, vg2, vals, lg, stg,
    rl_a, rl_b, fin_a, fin_b, rl2_a, rl2_b, fin2_a, fin2_b, wacc, wgo, qgo, kgo, cbuf, col,
    loc, ssem, rf, rs, rp, cs, cr, ps, pr, lss, lsr, rrl, rfin, rrl2, rfin2,
):
    sec = lax.axis_index("section")
    dp = lax.axis_index("dp")
    core = lax.rem(dp, 2)
    y = dp // 8
    z = lax.rem(dp // 2, 4)
    other = 1 - core
    coord = {"y": y, "z": z}

    def at(yy, zz, cc):
        return (sec, (yy * 4 + zz) * 2 + cc)

    def near(axis, step):
        if axis == "y":
            return at(lax.rem(y + step + 4, 4), z, core)
        return at(y, lax.rem(z + step + 4, 4), core)

    partner = at(y, z, other)

    def place(first, fo, so):
        yo, zo = (fo, so) if first == "y" else (so, fo)
        return lax.rem(y + yo, 4) * 4 + lax.rem(z + zo, 4)

    here = y * 4 + z

    loads = [
        pltpu.make_async_copy(k_hbm, k, loc.at[0]),
        pltpu.make_async_copy(q_hbm, q, loc.at[1]),
        pltpu.make_async_copy(og_hbm, og, loc.at[2]),
        pltpu.make_async_copy(hid_hbm, hid, loc.at[3]),
        pltpu.make_async_copy(gt_hbm, gt, loc.at[4]),
        pltpu.make_async_copy(w_hbm, wf.at[here, core], loc.at[5]),
    ]
    loads[0].start()
    loads[1].start()
    loads[2].start()
    cbuf[0] = jnp.full((8, 128), cnt_ref[0], jnp.int32)

    barrier = pltpu.get_barrier_semaphore()
    ids = [near("y", 1), near("y", -1), near("z", 1), near("z", -1), partner]
    ids += [(lax.rem(sec + i, NS), dp) for i in range(1, NS)]
    for one in ids:
        pl.semaphore_signal(barrier, inc=1, device_id=one, device_id_type=MESH)
    pl.semaphore_wait(barrier, len(ids))

    sent = []

    def send(src, dst, recv, device):
        copy = pltpu.make_async_remote_copy(
            src_ref=src, dst_ref=dst, send_sem=ssem.at[len(sent)], recv_sem=recv,
            device_id=device, device_id_type=MESH,
        )
        sent.append(copy)
        copy.start()

    def arrived(dst, recv):
        pltpu.make_async_remote_copy(
            src_ref=dst, dst_ref=dst, send_sem=ssem.at[0], recv_sem=recv,
            device_id=partner, device_id_type=MESH,
        ).wait_recv()

    HALF = (pl.ds(0, 128), pl.ds(128, 128))
    FULL = pl.ds(0, SH)

    def piece(c, fo, so, rows):
        first, _, c0, cw = COLOURS[c]
        return wf.at[place(first, fo, so), core, rows, pl.ds(c0, cw)]

    def to_second(c, fi):
        first, second, c0, cw = COLOURS[c]
        src = w_hbm.at[:, pl.ds(c0, cw)] if fi == 0 else piece(c, OFFS[fi], 0, FULL)
        dst = piece(c, OFFS[fi], 0, FULL)
        send(src, dst, rs.at[c, fi, 0], near(second, 1))
        send(src, dst, rs.at[c, fi, 1], near(second, -1))

    def to_partner(c, fi, si):
        first, second, c0, cw = COLOURS[c]
        dst = piece(c, OFFS[fi], OFFS[si], FULL)
        src = w_hbm.at[:, pl.ds(c0, cw)] if fi == 0 and si == 0 else dst
        send(src, dst, rp.at[c, fi, si], partner)

    def own(c):
        first, second, c0, cw = COLOURS[c]
        src, dst = w_hbm.at[:, pl.ds(c0, cw)], piece(c, 0, 0, FULL)
        send(src, dst, rf.at[c, 0], near(first, 1))
        send(src, dst, rf.at[c, 1], near(first, -1))
        to_second(c, 0)
        to_partner(c, 0, 0)

    def first12(c):
        first = COLOURS[c][0]
        for fi, (step, half) in ((1, (1, 0)), (2, (-1, 1))):
            arrived(piece(c, OFFS[fi], 0, FULL), rf.at[c, fi - 1])
            part = piece(c, OFFS[fi], 0, HALF[half])
            send(part, part, rf.at[c, 2 + half], near(first, step))
            to_second(c, fi)
            to_partner(c, fi, 0)

    def first3(c):
        for half in (0, 1):
            arrived(piece(c, 2, 0, HALF[half]), rf.at[c, 2 + half])
        to_second(c, 3)
        to_partner(c, 3, 0)

    def second12(c, fi):
        second = COLOURS[c][1]
        for si, (step, half) in ((1, (1, 0)), (2, (-1, 1))):
            arrived(piece(c, OFFS[fi], OFFS[si], FULL), rs.at[c, fi, si - 1])
            part = piece(c, OFFS[fi], OFFS[si], HALF[half])
            send(part, part, rs.at[c, fi, 2 + half], near(second, step))
            to_partner(c, fi, si)

    def second3(c, fi):
        for half in (0, 1):
            arrived(piece(c, OFFS[fi], 2, HALF[half]), rs.at[c, fi, 2 + half])
        to_partner(c, fi, 3)

    def from_partner(c, fi, si):
        first, _, c0, cw = COLOURS[c]
        arrived(
            wf.at[place(first, OFFS[fi], OFFS[si]), other, FULL, pl.ds(c0, cw)], rp.at[c, fi, si]
        )

    def multiply(c, fi, si, cc):
        first, _, c0, cw = COLOURS[c]
        p = place(first, OFFS[fi], OFFS[si])
        vals[:, c0 : c0 + cw] += dot(normed[p, cc], wf[p, cc, :, c0 : c0 + cw])

    own(0)
    own(1)
    counts = []
    for i in range(1, NS):
        copy = pltpu.make_async_remote_copy(
            src_ref=cbuf.at[0], dst_ref=cbuf.at[i], send_sem=cs.at[i - 1], recv_sem=cr.at[i - 1],
            device_id=(lax.rem(sec + i, NS), dp), device_id_type=MESH,
        )
        copy.start()
        counts.append(copy)
    loads[3].start()
    loads[4].start()
    loads[5].start()

    cosine, sine = cos_ref, sin_ref
    loads[0].wait()
    loads[1].wait()
    loads[2].wait()
    for g in range(HK):
        krot[g] = turn(k[:, g * HD : (g + 1) * HD].astype(F32), cosine[...], sine[...]).astype(BF16)

    def attend(g):
        for r in range(SHARE):
            h = g * SHARE + r
            qrot[g, r * T : (r + 1) * T] = turn(
                q[:, h * HD : (h + 1) * HD].astype(F32), cosine[...], sine[...]
            ).astype(BF16)
        total = jnp.zeros((T, HD), F32)
        for r in range(0, SHARE, 2):
            rows = slice(r * T, (r + 2) * T)
            scores = dot(qrot[g, rows], krot[g], NT) * SCALE
            row = lax.broadcasted_iota(jnp.int32, (2 * T, T), 0)
            row = jnp.where(row >= T, row - T, row)
            lane = lax.broadcasted_iota(jnp.int32, (2 * T, T), 1)
            scores = jnp.where(row >= lane, scores, -1e30)
            expo = jnp.exp(scores - jnp.max(scores, axis=-1, keepdims=True))
            p = expo / jnp.sum(expo, axis=-1, keepdims=True)
            probs[g, rows] = p
            h = g * SHARE + r
            d_out = jnp.concatenate(
                [og[:, h * HD : (h + 1) * HD], og[:, (h + 1) * HD : (h + 2) * HD]], axis=0
            )
            total = total + dot(p.astype(BF16), d_out, TN)
        vg2[0, :, g * HD : (g + 1) * HD] = total.astype(BF16)

    attend(0)
    second12(0, 0)
    first12(1)
    attend(1)
    first12(0)
    second3(0, 0)
    first3(1)
    attend(2)
    second12(1, 0)
    first3(0)

    for copy in counts:
        copy.wait_recv()
    last = cbuf[0] - 1
    for i in range(1, NS):
        last = last + jnp.where(sec >= i, cbuf[i], 0)
    loads[3].wait()
    loads[4].wait()

    @pl.loop(0, 8)
    def _(i):
        cols = pl.ds(pl.multiple_of(i * 1024, 1024), 1024)
        rows = lax.broadcasted_iota(jnp.int32, (40, 1024), 0)
        same = rows == jnp.broadcast_to(last[0:1, 0:1], (40, 1024))
        gain[:, cols] = jnp.sum(jnp.where(same, gt[:, cols].astype(F32), 0.0), axis=0, keepdims=True)

    def squares(i, acc):
        x = hid[:, pl.ds(pl.multiple_of(i * SH, SH), SH)].astype(F32)
        return acc + x * x

    acc = lax.fori_loop(0, 32, squares, jnp.zeros((T, SH), F32))
    inverse = lax.rsqrt(jnp.sum(acc, axis=-1, keepdims=True) * (1.0 / D) + 1e-05)
    col[0] = jnp.broadcast_to(inverse, (T, 128))

    @pl.loop(0, 16)
    def _(i):
        for c in range(2):
            cols = pl.ds(pl.multiple_of(i * 512 + c * SH, SH), SH)
            x = hid[:, cols].astype(F32)
            inv = jnp.concatenate([col[0]] * 2, axis=1)
            normed[i, c] = (x * inv * gain[:, cols]).astype(BF16)

    pair = pltpu.make_async_remote_copy(
        src_ref=normed.at[:, other], dst_ref=pnorm, send_sem=ps.at[0], recv_sem=pr.at[0],
        device_id=partner, device_id_type=MESH,
    )
    pair.start()
    vals[...] = jnp.zeros((T, E), F32)

    second12(0, 1)
    second12(0, 2)
    attend(3)
    pair_vg = pltpu.make_async_remote_copy(
        src_ref=vg2.at[0], dst_ref=vg2.at[1], send_sem=ps.at[1], recv_sem=pr.at[1],
        device_id=partner, device_id_type=MESH,
    )
    pair_vg.start()
    second3(1, 0)
    second12(1, 1)
    second12(1, 2)
    second3(0, 1)
    second3(0, 2)
    second12(0, 3)

    loads[5].wait()
    pair.wait_recv()
    pair_vg.wait_recv()

    def weight_part(i):
        left = jnp.concatenate([normed[i, core], pnorm[i]], axis=0)
        right = jnp.concatenate([vg2[0], vg2[1]], axis=0)
        stg[i] = dot(left, right, TN).astype(BF16)

    @pl.loop(0, 16)
    def _(i):
        weight_part(i)

    second3(1, 1)
    second3(1, 2)
    second12(1, 3)
    for c in range(2):
        for fi in range(3):
            for si in range(4):
                from_partner(c, fi, si)
                multiply(c, fi, si, core)
                multiply(c, fi, si, other)

    rl, fin, rl2, fin2 = (rl_a, rl_b), (fin_a, fin_b), (rl2_a, rl2_b), (fin2_a, fin2_b)

    def part(c, fo, so, rows):
        _, first, c0, cw = COLOURS[c]
        return stg.at[place(first, fo, so), rows, pl.ds(c0, cw)]

    def free_sends(c, oi):
        first, so = COLOURS[c][1], RS_OFFS[oi]
        up, down = near(first, 1), near(first, -1)
        send(part(c, 2, so, HALF[0]), rl[c].at[oi, 0], rrl.at[c, oi, 0], up)
        send(part(c, 2, so, HALF[1]), rl[c].at[oi, 1], rrl.at[c, oi, 1], down)
        send(part(c, 1, so, HALF[1]), fin[c].at[oi, 0, HALF[1]], rfin.at[c, oi, 0, 1], up)
        send(part(c, 3, so, HALF[0]), fin[c].at[oi, 1, HALF[0]], rfin.at[c, oi, 1, 0], down)

    def relay(c, oi):
        _, first, c0, cw = COLOURS[c]
        so = RS_OFFS[oi]
        for side, (fo, step) in enumerate(((1, 1), (3, -1))):
            arrived(rl[c].at[oi, side], rrl.at[c, oi, side])
            p = place(first, fo, so)
            rows, cols = slice(side * 128, side * 128 + 128), slice(c0, c0 + cw)
            both = stg[p, rows, cols].astype(F32) + rl[c][oi, side].astype(F32)
            stg[p, rows, cols] = both.astype(BF16)
            send(
                part(c, fo, so, HALF[side]), fin[c].at[oi, side, HALF[side]],
                rfin.at[c, oi, side, side], near(first, step),
            )

    def finish(c, oi):
        _, first, c0, cw = COLOURS[c]
        so = RS_OFFS[oi]
        for side in range(2):
            for half in range(2):
                arrived(fin[c].at[oi, side, HALF[half]], rfin.at[c, oi, side, half])
        p, cols = place(first, 0, so), slice(c0, c0 + cw)
        total = stg[p, :, cols].astype(F32) + fin[c][oi, 0].astype(F32) + fin[c][oi, 1].astype(F32)
        if so == 0:
            wacc[:, cols] = total
        else:
            stg[p, :, cols] = total.astype(BF16)
            second = COLOURS[c][0]
            up, down = near(second, 1), near(second, -1)
            if so == 2:
                send(part(c, 0, 2, HALF[0]), rl2[c].at[0], rrl2.at[c, 0], up)
                send(part(c, 0, 2, HALF[1]), rl2[c].at[1], rrl2.at[c, 1], down)
            elif so == 1:
                send(part(c, 0, 1, HALF[1]), fin2[c].at[0, HALF[1]], rfin2.at[c, 0, 1], up)
            else:
                send(part(c, 0, 3, HALF[0]), fin2[c].at[1, HALF[0]], rfin2.at[c, 1, 0], down)

    def relay2(c, side):
        second, first, c0, cw = COLOURS[c]
        so, step = ((1, 1), (3, -1))[side]
        arrived(rl2[c].at[side], rrl2.at[c, side])
        p = place(first, 0, so)
        rows, cols = slice(side * 128, side * 128 + 128), slice(c0, c0 + cw)
        both = stg[p, rows, cols].astype(F32) + rl2[c][side].astype(F32)
        stg[p, rows, cols] = both.astype(BF16)
        send(
            part(c, 0, so, HALF[side]), fin2[c].at[side, HALF[side]],
            rfin2.at[c, side, side], near(second, step),
        )

    def finish2(c):
        _, _, c0, cw = COLOURS[c]
        cols = slice(c0, c0 + cw)
        for side in range(2):
            for half in range(2):
                arrived(fin2[c].at[side, HALF[half]], rfin2.at[c, side, half])
        total = wacc[:, cols] + fin2[c][0].astype(F32) + fin2[c][1].astype(F32)
        wgo[:, cols] = total.astype(BF16)

    for oi in range(2):
        free_sends(0, oi)
        free_sends(1, oi)

    second3(0, 3)
    second3(1, 3)
    for c in range(2):
        for si in range(4):
            from_partner(c, 3, si)
            multiply(c, 3, si, core)
            multiply(c, 3, si, other)

    inverse = col[0][:, 0:1]
    mean = jnp.sum(vg2[0].astype(F32) * vals[...], axis=-1, keepdims=True) * (1.0 / D)
    col[1] = jnp.broadcast_to(inverse * inverse * mean, (T, 128))

    def chunk(ref, i):
        return ref.at[:, pl.ds(pl.multiple_of(i * 512, 512), 512)]

    def passing(i):
        return pltpu.make_async_remote_copy(
            src_ref=chunk(lg, i), dst_ref=chunk(up_hbm, i), send_sem=lss.at[i], recv_sem=lsr.at[i],
            device_id=(lax.rem(sec + NS - 1, NS), dp), device_id_type=MESH,
        )

    @pl.when(sec > 0)
    def _():
        @pl.loop(0, 16)
        def _(i):
            cols = pl.ds(pl.multiple_of(i * 512, 512), 512)
            d_normed = dot(vg2[0], wf[i].reshape(512, E), NT)
            inv = jnp.concatenate([col[0]] * 4, axis=1)
            fix = jnp.concatenate([col[1]] * 4, axis=1)
            out = inv * (gain[:, cols] * d_normed) - hid[:, cols].astype(F32) * fix
            lg[:, cols] = out.astype(BF16)
            passing(i).start()

    values_low = vals[...].astype(BF16)
    vg2[1] = values_low

    def attend_back(g):
        value = vg2[1, :, g * HD : (g + 1) * HD]
        total = jnp.zeros((T, HD), F32)
        for r in range(0, SHARE, 2):
            h = g * SHARE + r
            rows = slice(r * T, (r + 2) * T)
            d_out = jnp.concatenate(
                [og[:, h * HD : (h + 1) * HD], og[:, (h + 1) * HD : (h + 2) * HD]], axis=0
            )
            d_probs = dot(d_out, value, NT)
            p = probs[g, rows]
            low = p.astype(BF16).astype(F32)
            delta = jnp.sum(low * d_probs, axis=-1, keepdims=True)
            d_scores = (p * (d_probs - delta) * SCALE).astype(BF16)
            total = total + dot(d_scores, qrot[g, rows], TN)
            dq = dot(d_scores, krot[g])
            for i in range(2):
                one = turn(dq[i * T : (i + 1) * T], cosine[...], -sine[...])
                qgo[:, (h + i) * HD : (h + i + 1) * HD] = one.astype(BF16)
        kgo[:, g * HD : (g + 1) * HD] = turn(total, cosine[...], -sine[...]).astype(BF16)

    relay(0, 0)
    relay(1, 0)
    free_sends(0, 2)
    free_sends(1, 2)
    attend_back(0)
    relay(0, 1)
    relay(1, 1)
    free_sends(0, 3)
    free_sends(1, 3)
    finish(0, 0)
    finish(1, 0)
    attend_back(1)
    relay(0, 2)
    relay(1, 2)
    finish(0, 1)
    finish(1, 1)
    relay2(0, 0)
    relay2(1, 0)
    attend_back(2)
    relay(0, 3)
    relay(1, 3)
    finish(0, 2)
    finish(1, 2)
    relay2(0, 1)
    relay2(1, 1)
    attend_back(3)
    outs = [
        pltpu.make_async_copy(qgo, qg_hbm, loc.at[0]),
        pltpu.make_async_copy(kgo, kg_hbm, loc.at[1]),
    ]
    for one in outs:
        one.start()
    finish(0, 3)
    finish(1, 3)
    finish2(0)
    finish2(1)
    outs.append(pltpu.make_async_copy(wgo, wg_hbm, loc.at[2]))
    outs[2].start()

    @pl.when(sec == NS - 1)
    def _():
        hid[...] = jnp.zeros((T, D), BF16)
        blank = pltpu.make_async_copy(hid, up_hbm, loc.at[3])
        blank.start()
        blank.wait()

    @pl.when(sec < NS - 1)
    def _():
        @pl.loop(0, 16)
        def _(i):
            passing(i).wait_recv()

    @pl.when(sec > 0)
    def _():
        @pl.loop(0, 16)
        def _(i):
            passing(i).wait_send()

    for copy in sent:
        copy.wait_send()
    for copy in counts:
        copy.wait_send()
    pair.wait_send()
    pair_vg.wait_send()
    for one in outs:
        one.wait()


def shards(hidden, gain_table, layer_counts, positions, queries, keys, value_weight, out_grad):
    half = HD // 2
    freq = jnp.exp(jnp.arange(half, dtype=F32) * (-2.0 * math.log(500000.0) / HD))
    angle = positions[0].astype(F32)[:, None] * freq[None, :]
    cosine, sine = jnp.cos(angle), jnp.sin(angle)
    cosine = jnp.concatenate([cosine, cosine], axis=1)
    sine = jnp.concatenate([-sine, sine], axis=1)
    anywhere = pl.BlockSpec(memory_space=pl.ANY)
    vmem = pl.BlockSpec(memory_space=pltpu.VMEM)
    smem = pl.BlockSpec(memory_space=pltpu.SMEM)
    dma = pltpu.SemaphoreType.DMA
    widths = [one[3] for one in COLOURS]
    scratch = [
        pltpu.VMEM((T, D), BF16),
        pltpu.VMEM((40, D), BF16),
        pltpu.VMEM((T, HQ * HD), BF16),
        pltpu.VMEM((T, HK * HD), BF16),
        pltpu.VMEM((T, HQ * HD), BF16),
        pltpu.VMEM((16, 2, SH, E), BF16),
        pltpu.VMEM((16, 2, T, SH), BF16),
        pltpu.VMEM((16, T, SH), BF16),
        pltpu.VMEM((1, D), F32),
        pltpu.VMEM((HK, T, HD), BF16),
        pltpu.VMEM((HK, SHARE * T, HD), BF16),
        pltpu.VMEM((HK, SHARE * T, T), F32),
        pltpu.VMEM((2, T, E), BF16),
        pltpu.VMEM((T, E), F32),
        pltpu.VMEM((T, D), BF16),
        pltpu.VMEM((16, SH, E), BF16),
    ]
    scratch += [pltpu.VMEM((4, 2, 128, w), BF16) for w in widths]
    scratch += [pltpu.VMEM((4, 2, SH, w), BF16) for w in widths]
    scratch += [pltpu.VMEM((2, 128, w), BF16) for w in widths]
    scratch += [pltpu.VMEM((2, SH, w), BF16) for w in widths]
    scratch += [
        pltpu.VMEM((SH, E), F32),
        pltpu.VMEM((SH, E), BF16),
        pltpu.VMEM((T, HQ * HD), BF16),
        pltpu.VMEM((T, HK * HD), BF16),
        pltpu.VMEM((NS, 8, 128), jnp.int32),
        pltpu.VMEM((2, T, 128), F32),
        dma((6,)),
        dma((136,)),
        dma((2, 4)),
        dma((2, 4, 4)),
        dma((2, 4, 4)),
        dma((7,)),
        dma((7,)),
        dma((2,)),
        dma((2,)),
        dma((16,)),
        dma((16,)),
        dma((2, 4, 2)),
        dma((2, 4, 2, 2)),
        dma((2, 2)),
        dma((2, 2, 2)),
    ]
    query_grad, key_grad, weight_grad, upstream = pl.pallas_call(
        kernel,
        out_shape=(
            jax.ShapeDtypeStruct((T, HQ * HD), BF16),
            jax.ShapeDtypeStruct((T, HK * HD), BF16),
            jax.ShapeDtypeStruct((SH, E), BF16),
            jax.ShapeDtypeStruct((T, D), BF16),
        ),
        in_specs=[anywhere, anywhere, smem, vmem, vmem] + [anywhere] * 4,
        out_specs=(anywhere,) * 4,
        scratch_shapes=scratch,
        compiler_params=pltpu.CompilerParams(
            collective_id=0, has_side_effects=True, vmem_limit_bytes=56 << 20
        ),
    )(
        hidden[0], gain_table, layer_counts, cosine, sine, queries[0], keys[0], value_weight[0],
        out_grad[0],
    )
    return (query_grad[None], key_grad[None], weight_grad[None], upstream[None])


def solution(mesh):
    rows = P("section", "dp", None)
    in_specs = (rows, P(), P("section"), P("section", "dp"), rows, rows, rows, rows)
    return jax.shard_map(
        shards, mesh=mesh, in_specs=in_specs, out_specs=(rows,) * 4, check_vma=False
    )
```

```python
import functools
import math

import jax
import jax.numpy as jnp
from jax import lax
from jax.experimental import pallas as pl
from jax.experimental.pallas import tpu as pltpu
from jax.sharding import PartitionSpec as P

HQ = 32
HK = 4
HD = 128
SHARE = HQ // HK
SCALE = HD ** (-0.5)
T = 128
D = 8192
E = HK * HD
SH = 256
NS = 8
MESH = pl.DeviceIdType.MESH
F32 = jnp.float32
BF16 = jnp.bfloat16

COLOURS = (("z", "y", 0, 384), ("y", "z", 384, 128))
OFFS = (0, 3, 1, 2)
INDEX = {0: 0, 3: 1, 1: 2, 2: 3}
EARLY = ((0, 0), (1, 0), (3, 0), (0, 1), (0, 3), (2, 0), (0, 2))
RS_OFFS = (2, 1, 3, 0)
NT = (((1,), (1,)), ((), ()))
TN = (((0,), (0,)), ((), ()))


def dot(a, b, dims=(((1,), (0,)), ((), ()))):
    return lax.dot_general(a, b, dims, preferred_element_type=F32)


def turn(x, cosine, sine):
    return x * cosine + pltpu.roll(x, HD // 2, 1) * sine


def kernel(
    hid_hbm, gt_hbm, cnt_ref, cos_ref, sin_ref, q_hbm, k_hbm, w_hbm, og_hbm,
    qgo, kgo, wgo, up,
    hid, gt, q, k, og, wf, normed, pnorm, gain, krot, qrot, probs, vg2, vals, lg, stg,
    rl, fin, rl2, fin2, wacc, cbuf, col, hin, fixr, rb,
    loc, ssem, rf, rs, rp, cs, cr, ps, pr, lss, lsr, rrl, rfin, rrl2, rfin2, hs, hr, fx, rbs, rbr,
):
    sec = lax.axis_index("section")
    dp = lax.axis_index("dp")
    core = lax.rem(dp, 2)
    y = dp // 8
    z = lax.rem(dp // 2, 4)
    other = 1 - core

    def at(yy, zz, cc):
        return (sec, (yy * 4 + zz) * 2 + cc)

    def near(axis, step):
        if axis == "y":
            return at(lax.rem(y + step + 4, 4), z, core)
        return at(y, lax.rem(z + step + 4, 4), core)

    partner = at(y, z, other)

    def spot(yo, zo):
        return lax.rem(y + yo, 4) * 4 + lax.rem(z + zo, 4)

    def place(first, fo, so):
        return spot(fo, so) if first == "y" else spot(so, fo)

    gives_early = jnp.logical_and(sec != 0, sec != 4)
    gets_early = jnp.logical_and(sec != NS - 1, sec != 3)
    below = lax.rem(sec + NS - 1, NS)

    here = y * 4 + z

    loads = [
        pltpu.make_async_copy(k_hbm, k, loc.at[0]),
        pltpu.make_async_copy(q_hbm, q, loc.at[1]),
        pltpu.make_async_copy(og_hbm, og, loc.at[2]),
        pltpu.make_async_copy(hid_hbm, hid, loc.at[3]),
        pltpu.make_async_copy(gt_hbm, gt, loc.at[4]),
        pltpu.make_async_copy(w_hbm, wf.at[here, core], loc.at[5]),
    ]
    loads[0].start()
    loads[1].start()
    loads[2].start()
    cbuf[0] = jnp.full((8, 128), cnt_ref[0], jnp.int32)

    barrier = pltpu.get_barrier_semaphore()
    ids = [near("y", 1), near("y", -1), near("z", 1), near("z", -1), partner]
    ids += [(lax.rem(sec + i, NS), dp) for i in range(1, NS)]
    for one in ids:
        pl.semaphore_signal(barrier, inc=1, device_id=one, device_id_type=MESH)
    pl.semaphore_wait(barrier, len(ids))

    sent = []

    def send(src, dst, recv, device):
        copy = pltpu.make_async_remote_copy(
            src_ref=src, dst_ref=dst, send_sem=ssem.at[len(sent)], recv_sem=recv,
            device_id=device, device_id_type=MESH,
        )
        sent.append(copy)
        copy.start()

    def arrived(dst, recv):
        pltpu.make_async_remote_copy(
            src_ref=dst, dst_ref=dst, send_sem=ssem.at[0], recv_sem=recv,
            device_id=partner, device_id_type=MESH,
        ).wait_recv()

    HALF = (pl.ds(0, 128), pl.ds(128, 128))
    FULL = pl.ds(0, SH)

    def piece(c, fo, so, rows):
        first, _, c0, cw = COLOURS[c]
        return wf.at[place(first, fo, so), core, rows, pl.ds(c0, cw)]

    def to_second(c, fi):
        first, second, c0, cw = COLOURS[c]
        src = w_hbm.at[:, pl.ds(c0, cw)] if fi == 0 else piece(c, OFFS[fi], 0, FULL)
        dst = piece(c, OFFS[fi], 0, FULL)
        send(src, dst, rs.at[c, fi, 0], near(second, 1))
        send(src, dst, rs.at[c, fi, 1], near(second, -1))

    def to_partner(c, fi, si):
        first, second, c0, cw = COLOURS[c]
        dst = piece(c, OFFS[fi], OFFS[si], FULL)
        src = w_hbm.at[:, pl.ds(c0, cw)] if fi == 0 and si == 0 else dst
        send(src, dst, rp.at[c, fi, si], partner)

    def own(c):
        first, second, c0, cw = COLOURS[c]
        src, dst = w_hbm.at[:, pl.ds(c0, cw)], piece(c, 0, 0, FULL)
        send(src, dst, rf.at[c, 0], near(first, 1))
        send(src, dst, rf.at[c, 1], near(first, -1))
        to_second(c, 0)
        to_partner(c, 0, 0)

    def first12(c):
        first = COLOURS[c][0]
        for fi, (step, half) in ((1, (1, 0)), (2, (-1, 1))):
            arrived(piece(c, OFFS[fi], 0, FULL), rf.at[c, fi - 1])
            part = piece(c, OFFS[fi], 0, HALF[half])
            send(part, part, rf.at[c, 2 + half], near(first, step))
            to_second(c, fi)
            to_partner(c, fi, 0)

    def first3(c):
        for half in (0, 1):
            arrived(piece(c, 2, 0, HALF[half]), rf.at[c, 2 + half])
        to_second(c, 3)
        to_partner(c, 3, 0)

    def second12(c, fi):
        second = COLOURS[c][1]
        for si, (step, half) in ((1, (1, 0)), (2, (-1, 1))):
            arrived(piece(c, OFFS[fi], OFFS[si], FULL), rs.at[c, fi, si - 1])
            part = piece(c, OFFS[fi], OFFS[si], HALF[half])
            send(part, part, rs.at[c, fi, 2 + half], near(second, step))
            to_partner(c, fi, si)

    def second3(c, fi):
        for half in (0, 1):
            arrived(piece(c, OFFS[fi], 2, HALF[half]), rs.at[c, fi, 2 + half])
        to_partner(c, fi, 3)

    def from_partner(c, fi, si):
        first, _, c0, cw = COLOURS[c]
        arrived(
            wf.at[place(first, OFFS[fi], OFFS[si]), other, FULL, pl.ds(c0, cw)], rp.at[c, fi, si]
        )

    def multiply(yo, zo):
        from_partner(0, INDEX[zo], INDEX[yo])
        from_partner(1, INDEX[yo], INDEX[zo])
        p = spot(yo, zo)
        vals[...] += dot(normed[p, 0], wf[p, 0]) + dot(normed[p, 1], wf[p, 1])

    def chunk(ref, i):
        return ref.at[:, pl.ds(pl.multiple_of(i * 512, 512), 512)]

    def ahead(i):
        p = spot(*EARLY[i])
        return pltpu.make_async_remote_copy(
            src_ref=chunk(hid_hbm, p), dst_ref=hin.at[i], send_sem=hs.at[i], recv_sem=hr.at[i],
            device_id=(below, dp), device_id_type=MESH,
        )

    def passing(i):
        return pltpu.make_async_remote_copy(
            src_ref=chunk(lg, i), dst_ref=chunk(up, i), send_sem=lss.at[i], recv_sem=lsr.at[i],
            device_id=(below, dp), device_id_type=MESH,
        )

    def first_term(p):
        cols = pl.ds(pl.multiple_of(p * 512, 512), 512)
        d_normed = dot(vg2[0], wf[p].reshape(512, E), NT)
        inv = jnp.concatenate([col[0]] * 4, axis=1)
        return cols, inv * (gain[:, cols] * d_normed)

    def leave_early(i):
        p = spot(*EARLY[i])

        @pl.when(gives_early)
        def _():
            cols, term = first_term(p)
            lg[:, cols] = term.astype(BF16)
            passing(p).start()

    def fixing():
        return pltpu.make_async_remote_copy(
            src_ref=col.at[1], dst_ref=fixr, send_sem=fx.at[0], recv_sem=fx.at[1],
            device_id=(below, dp), device_id_type=MESH,
        )

    def whole_term(p):
        cols, term = first_term(p)
        fix = jnp.concatenate([col[1]] * 4, axis=1)
        lg[:, cols] = (term - hid[:, cols].astype(F32) * fix).astype(BF16)

    own(0)
    own(1)
    counts = []
    for i in range(1, NS):
        copy = pltpu.make_async_remote_copy(
            src_ref=cbuf.at[0], dst_ref=cbuf.at[i], send_sem=cs.at[i - 1], recv_sem=cr.at[i - 1],
            device_id=(lax.rem(sec + i, NS), dp), device_id_type=MESH,
        )
        copy.start()
        counts.append(copy)
    loads[3].start()
    loads[4].start()
    loads[5].start()

    @pl.when(gives_early)
    def _():
        for i in range(len(EARLY)):
            ahead(i).start()

    cosine, sine = cos_ref, sin_ref
    loads[0].wait()
    loads[1].wait()
    loads[2].wait()
    for g in range(HK):
        krot[g] = turn(k[:, g * HD : (g + 1) * HD].astype(F32), cosine[...], sine[...]).astype(BF16)

    def attend(g):
        for r in range(SHARE):
            h = g * SHARE + r
            qrot[g, r * T : (r + 1) * T] = turn(
                q[:, h * HD : (h + 1) * HD].astype(F32), cosine[...], sine[...]
            ).astype(BF16)
        total = jnp.zeros((T, HD), F32)
        for r in range(0, SHARE, 2):
            rows = slice(r * T, (r + 2) * T)
            scores = dot(qrot[g, rows], krot[g], NT) * SCALE
            row = lax.broadcasted_iota(jnp.int32, (2 * T, T), 0)
            row = jnp.where(row >= T, row - T, row)
            lane = lax.broadcasted_iota(jnp.int32, (2 * T, T), 1)
            scores = jnp.where(row >= lane, scores, -1e30)
            expo = jnp.exp(scores - jnp.max(scores, axis=-1, keepdims=True))
            p = expo / jnp.sum(expo, axis=-1, keepdims=True)
            probs[g, rows] = p
            h = g * SHARE + r
            d_out = jnp.concatenate(
                [og[:, h * HD : (h + 1) * HD], og[:, (h + 1) * HD : (h + 2) * HD]], axis=0
            )
            total = total + dot(p.astype(BF16), d_out, TN)
        vg2[0, :, g * HD : (g + 1) * HD] = total.astype(BF16)

    attend(0)
    second12(0, 0)
    first12(1)
    attend(1)
    first12(0)
    second3(0, 0)
    first3(1)
    attend(2)
    second12(1, 0)
    first3(0)
    attend(3)
    pair_vg = pltpu.make_async_remote_copy(
        src_ref=vg2.at[0], dst_ref=vg2.at[1], send_sem=ps.at[1], recv_sem=pr.at[1],
        device_id=partner, device_id_type=MESH,
    )
    pair_vg.start()

    for copy in counts:
        copy.wait_recv()
    last = cbuf[0] - 1
    for i in range(1, NS):
        last = last + jnp.where(sec >= i, cbuf[i], 0)
    loads[3].wait()
    loads[4].wait()

    @pl.loop(0, 8)
    def _(i):
        cols = pl.ds(pl.multiple_of(i * 1024, 1024), 1024)
        rows = lax.broadcasted_iota(jnp.int32, (40, 1024), 0)
        same = rows == jnp.broadcast_to(last[0:1, 0:1], (40, 1024))
        gain[:, cols] = jnp.sum(jnp.where(same, gt[:, cols].astype(F32), 0.0), axis=0, keepdims=True)

    def squares(i, acc):
        x = hid[:, pl.ds(pl.multiple_of(i * SH, SH), SH)].astype(F32)
        return acc + x * x

    acc = lax.fori_loop(0, 32, squares, jnp.zeros((T, SH), F32))
    inverse = lax.rsqrt(jnp.sum(acc, axis=-1, keepdims=True) * (1.0 / D) + 1e-05)
    col[0] = jnp.broadcast_to(inverse, (T, 128))

    @pl.loop(0, 16)
    def _(i):
        for c in range(2):
            cols = pl.ds(pl.multiple_of(i * 512 + c * SH, SH), SH)
            x = hid[:, cols].astype(F32)
            inv = jnp.concatenate([col[0]] * 2, axis=1)
            normed[i, c] = (x * inv * gain[:, cols]).astype(BF16)

    pair = pltpu.make_async_remote_copy(
        src_ref=normed.at[:, other], dst_ref=pnorm, send_sem=ps.at[0], recv_sem=pr.at[0],
        device_id=partner, device_id_type=MESH,
    )
    pair.start()
    vals[...] = jnp.zeros((T, E), F32)

    def weight_part(p):
        left = jnp.concatenate([normed[p, core], pnorm[p]], axis=0)
        right = jnp.concatenate([vg2[0], vg2[1]], axis=0)
        stg[p] = dot(left, right, TN).astype(BF16)

    def weight_parts(yo):
        @pl.loop(0, 4)
        def _(i):
            weight_part(lax.rem(y + yo, 4) * 4 + i)

    second12(0, 1)
    second12(0, 2)
    loads[5].wait()
    for i in range(3):
        multiply(*EARLY[i])
        leave_early(i)
    second3(1, 0)
    second12(1, 1)
    second12(1, 2)
    for i in range(3, 5):
        multiply(*EARLY[i])
        leave_early(i)
    second3(0, 1)
    second3(0, 2)
    for i in range(5, 7):
        multiply(*EARLY[i])
        leave_early(i)
    pair.wait_recv()
    pair_vg.wait_recv()
    weight_parts(2)
    weight_parts(1)
    second12(0, 3)
    weight_parts(3)
    second12(1, 3)
    weight_parts(0)
    for yo in (1, 3):
        for zo in (1, 3):
            multiply(yo, zo)
    second3(1, 1)
    second3(1, 2)

    def part(yo, zo, rows):
        return stg.at[spot(yo, zo), rows]

    def free_sends(oi):
        zo = RS_OFFS[oi]
        up1, down1 = near("y", 1), near("y", -1)
        send(part(2, zo, HALF[0]), rl.at[oi, 0], rrl.at[oi, 0], up1)
        send(part(2, zo, HALF[1]), rl.at[oi, 1], rrl.at[oi, 1], down1)
        send(part(1, zo, HALF[1]), fin.at[oi, 0, HALF[1]], rfin.at[oi, 0, 1], up1)
        send(part(3, zo, HALF[0]), fin.at[oi, 1, HALF[0]], rfin.at[oi, 1, 0], down1)

    def relay(oi):
        for side, (yo, step) in enumerate(((1, 1), (3, -1))):
            arrived(rl.at[oi, side], rrl.at[oi, side])
            p, rows = spot(yo, RS_OFFS[oi]), slice(side * 128, side * 128 + 128)
            stg[p, rows] = (stg[p, rows].astype(F32) + rl[oi, side].astype(F32)).astype(BF16)
            send(
                stg.at[p, HALF[side]], fin.at[oi, side, HALF[side]], rfin.at[oi, side, side],
                near("y", step),
            )

    def finish(oi):
        zo = RS_OFFS[oi]
        for side in range(2):
            for half in range(2):
                arrived(fin.at[oi, side, HALF[half]], rfin.at[oi, side, half])
        p = spot(0, zo)
        total = stg[p].astype(F32) + fin[oi, 0].astype(F32) + fin[oi, 1].astype(F32)
        if zo == 0:
            wacc[...] = total
            return
        stg[p] = total.astype(BF16)
        up1, down1 = near("z", 1), near("z", -1)
        if zo == 2:
            send(part(0, 2, HALF[0]), rl2.at[0], rrl2.at[0], up1)
            send(part(0, 2, HALF[1]), rl2.at[1], rrl2.at[1], down1)
        elif zo == 1:
            send(part(0, 1, HALF[1]), fin2.at[0, HALF[1]], rfin2.at[0, 1], up1)
        else:
            send(part(0, 3, HALF[0]), fin2.at[1, HALF[0]], rfin2.at[1, 0], down1)

    def relay2(side):
        zo, step = ((1, 1), (3, -1))[side]
        arrived(rl2.at[side], rrl2.at[side])
        p, rows = spot(0, zo), slice(side * 128, side * 128 + 128)
        stg[p, rows] = (stg[p, rows].astype(F32) + rl2[side].astype(F32)).astype(BF16)
        send(
            stg.at[p, HALF[side]], fin2.at[side, HALF[side]], rfin2.at[side, side],
            near("z", step),
        )

    def finish2():
        for side in range(2):
            for half in range(2):
                arrived(fin2.at[side, HALF[half]], rfin2.at[side, half])
        total = wacc[...] + fin2[0].astype(F32) + fin2[1].astype(F32)
        wgo[...] = total.astype(BF16)

    free_sends(0)
    free_sends(1)
    multiply(2, 1)
    multiply(2, 3)
    multiply(1, 2)
    multiply(3, 2)
    second3(0, 3)
    second3(1, 3)
    multiply(2, 2)

    inverse = col[0][:, 0:1]
    mean = jnp.sum(vg2[0].astype(F32) * vals[...], axis=-1, keepdims=True) * (1.0 / D)
    col[1] = jnp.broadcast_to(inverse * inverse * mean, (T, 128))

    @pl.when(gives_early)
    def _():
        fixing().start()

        @pl.loop(0, 9)
        def _(i):
            p = spot(i // 3 + 1, lax.rem(i, 3) + 1)
            whole_term(p)
            passing(p).start()

    @pl.when(sec == 4)
    def _():
        @pl.loop(0, 16)
        def _(n):
            p = spot(n // 4, lax.rem(n, 4))
            whole_term(p)
            pltpu.make_async_remote_copy(
                src_ref=chunk(lg, p), dst_ref=rb.at[n // 2], send_sem=lss.at[p],
                recv_sem=rbr.at[n // 2], device_id=(lax.rem(n, 2) * 7, dp), device_id_type=MESH,
            ).start()

    relays = jnp.logical_or(sec == 0, sec == NS - 1)

    def handing(j):
        n = 2 * j + sec // 7
        p = spot(n // 4, lax.rem(n, 4))
        return pltpu.make_async_remote_copy(
            src_ref=rb.at[j], dst_ref=chunk(up, p), send_sem=rbs.at[j], recv_sem=lsr.at[p],
            device_id=(3, dp), device_id_type=MESH,
        )

    def hand_on(*js):
        @pl.when(relays)
        def _():
            for j in js:
                arrived(rb.at[j], rbr.at[j])
                handing(j).start()

    values_low = vals[...].astype(BF16)
    vg2[1] = values_low

    def attend_back(g):
        value = vg2[1, :, g * HD : (g + 1) * HD]
        total = jnp.zeros((T, HD), F32)
        for r in range(0, SHARE, 2):
            h = g * SHARE + r
            rows = slice(r * T, (r + 2) * T)
            d_out = jnp.concatenate(
                [og[:, h * HD : (h + 1) * HD], og[:, (h + 1) * HD : (h + 2) * HD]], axis=0
            )
            d_probs = dot(d_out, value, NT)
            p = probs[g, rows]
            low = p.astype(BF16).astype(F32)
            delta = jnp.sum(low * d_probs, axis=-1, keepdims=True)
            d_scores = (p * (d_probs - delta) * SCALE).astype(BF16)
            total = total + dot(d_scores, qrot[g, rows], TN)
            dq = dot(d_scores, krot[g])
            for i in range(2):
                one = turn(dq[i * T : (i + 1) * T], cosine[...], -sine[...])
                qgo[:, (h + i) * HD : (h + i + 1) * HD] = one.astype(BF16)
        kgo[:, g * HD : (g + 1) * HD] = turn(total, cosine[...], -sine[...]).astype(BF16)

    relay(0)
    free_sends(2)
    hand_on(0)
    attend_back(0)
    relay(1)
    free_sends(3)
    hand_on(1, 2)
    finish(0)
    attend_back(1)
    hand_on(3)
    relay(2)
    finish(1)
    relay2(0)
    hand_on(4, 5)
    attend_back(2)
    relay(3)
    finish(2)
    relay2(1)
    hand_on(6, 7)
    attend_back(3)

    @pl.when(sec == NS - 1)
    def _():
        up[...] = jnp.zeros((T, D), BF16)

    finish(3)
    finish2()

    @pl.when(gets_early)
    def _():
        fixing().wait_recv()
        fix = jnp.concatenate([fixr[...]] * 4, axis=1)
        for i in range(len(EARLY)):
            p = spot(*EARLY[i])
            ahead(i).wait_recv()
            passing(p).wait_recv()
            cols = pl.ds(pl.multiple_of(p * 512, 512), 512)
            up[:, cols] = (up[:, cols].astype(F32) - hin[i].astype(F32) * fix).astype(BF16)

        @pl.loop(0, 9)
        def _(i):
            passing(spot(i // 3 + 1, lax.rem(i, 3) + 1)).wait_recv()

    @pl.when(sec == 3)
    def _():
        @pl.loop(0, 16)
        def _(i):
            passing(i).wait_recv()

    @pl.when(relays)
    def _():
        for j in range(8):
            handing(j).wait_send()

    @pl.when(gives_early)
    def _():
        fixing().wait_send()
        for i in range(len(EARLY)):
            ahead(i).wait_send()

    @pl.when(sec > 0)
    def _():
        @pl.loop(0, 16)
        def _(i):
            passing(i).wait_send()

    for copy in sent:
        copy.wait_send()
    for copy in counts:
        copy.wait_send()
    pair.wait_send()
    pair_vg.wait_send()


def shards(hidden, gain_table, layer_counts, positions, queries, keys, value_weight, out_grad):
    half = HD // 2
    freq = jnp.exp(jnp.arange(half, dtype=F32) * (-2.0 * math.log(500000.0) / HD))
    angle = positions[0].astype(F32)[:, None] * freq[None, :]
    cosine, sine = jnp.cos(angle), jnp.sin(angle)
    cosine = jnp.concatenate([cosine, cosine], axis=1)
    sine = jnp.concatenate([-sine, sine], axis=1)
    anywhere = pl.BlockSpec(memory_space=pl.ANY)
    vmem = pl.BlockSpec(memory_space=pltpu.VMEM)
    smem = pl.BlockSpec(memory_space=pltpu.SMEM)
    dma = pltpu.SemaphoreType.DMA
    scratch = [
        pltpu.VMEM((T, D), BF16),
        pltpu.VMEM((40, D), BF16),
        pltpu.VMEM((T, HQ * HD), BF16),
        pltpu.VMEM((T, HK * HD), BF16),
        pltpu.VMEM((T, HQ * HD), BF16),
        pltpu.VMEM((16, 2, SH, E), BF16),
        pltpu.VMEM((16, 2, T, SH), BF16),
        pltpu.VMEM((16, T, SH), BF16),
        pltpu.VMEM((1, D), F32),
        pltpu.VMEM((HK, T, HD), BF16),
        pltpu.VMEM((HK, SHARE * T, HD), BF16),
        pltpu.VMEM((HK, SHARE * T, T), F32),
        pltpu.VMEM((2, T, E), BF16),
        pltpu.VMEM((T, E), F32),
        pltpu.VMEM((T, D), BF16),
        pltpu.VMEM((16, SH, E), BF16),
    ]
    scratch += [
        pltpu.VMEM((4, 2, 128, E), BF16),
        pltpu.VMEM((4, 2, SH, E), BF16),
        pltpu.VMEM((2, 128, E), BF16),
        pltpu.VMEM((2, SH, E), BF16),
        pltpu.VMEM((SH, E), F32),
        pltpu.VMEM((NS, 8, 128), jnp.int32),
        pltpu.VMEM((2, T, 128), F32),
        pltpu.VMEM((len(EARLY), T, 512), BF16),
        pltpu.VMEM((T, 128), F32),
        pltpu.VMEM((8, T, 512), BF16),
        dma((6,)),
        dma((104,)),
        dma((2, 4)),
        dma((2, 4, 4)),
        dma((2, 4, 4)),
        dma((7,)),
        dma((7,)),
        dma((2,)),
        dma((2,)),
        dma((16,)),
        dma((16,)),
        dma((4, 2)),
        dma((4, 2, 2)),
        dma((2,)),
        dma((2, 2)),
        dma((len(EARLY),)),
        dma((len(EARLY),)),
        dma((2,)),
        dma((8,)),
        dma((8,)),
    ]
    query_grad, key_grad, weight_grad, upstream = pl.pallas_call(
        kernel,
        out_shape=(
            pltpu.VMEM((T, HQ * HD), BF16),
            pltpu.VMEM((T, HK * HD), BF16),
            pltpu.VMEM((SH, E), BF16),
            pltpu.VMEM((T, D), BF16),
        ),
        in_specs=[anywhere, anywhere, smem, vmem, vmem] + [anywhere] * 4,
        out_specs=(vmem,) * 4,
        scratch_shapes=scratch,
        compiler_params=pltpu.CompilerParams(
            collective_id=0, has_side_effects=True, vmem_limit_bytes=56 << 20
        ),
    )(
        hidden[0], gain_table, layer_counts, cosine, sine, queries[0], keys[0], value_weight[0],
        out_grad[0],
    )
    return (query_grad[None], key_grad[None], weight_grad[None], upstream[None])


def solution(mesh):
    rows = P("section", "dp", None)
    in_specs = (rows, P(), P("section"), P("section", "dp"), rows, rows, rows, rows)
    return jax.shard_map(
        shards, mesh=mesh, in_specs=in_specs, out_specs=(rows,) * 4, check_vma=False
    )
```

```python
import functools
import math

import jax
import jax.numpy as jnp
from jax import lax
from jax.experimental import pallas as pl
from jax.experimental.pallas import tpu as pltpu
from jax.sharding import PartitionSpec as P

HQ = 32
HK = 4
HD = 128
SHARE = HQ // HK
SCALE = HD ** (-0.5)
T = 128
D = 8192
E = HK * HD
SH = 256
NS = 8
MESH = pl.DeviceIdType.MESH
F32 = jnp.float32
BF16 = jnp.bfloat16

COLOURS = (("z", "y", 0, 384), ("y", "z", 384, 128))
OFFS = (0, 3, 1, 2)
INDEX = {0: 0, 3: 1, 1: 2, 2: 3}
EARLY = ((0, 0), (1, 0), (3, 0), (0, 1), (0, 3), (2, 0), (0, 2))
LATE = tuple((i, j) for i in range(4) for j in range(4) if (i, j) not in EARLY)
ORDER = (
    ("oF", 0), ("oF", 1), ("oS", 0), ("hid",), ("att", 3), ("att", 0), ("att", 1), ("att", 2),
    ("rF", 1, 2), ("rF", 1, 1), ("norm",), ("rS", 0, 0), ("oS", 1), ("rF", 0, 1), ("sF", 0, 1),
    ("mul", 0, 0), ("rF", 0, 2), ("rS", 1, 0), ("sF", 1, 2), ("sF", 0, 2), ("mul", 0, 1),
    ("rS", 0, 1), ("sF", 1, 1), ("le", 0), ("mul", 0, 3), ("f3", 0), ("s3", 1, 0), ("s3", 0, 0),
    ("mul", 3, 0), ("rS", 1, 2), ("le", 4), ("le", 2), ("s3", 0, 1), ("wp", 2), ("f3", 1),
    ("wp", 0), ("rS", 0, 2), ("wp", 1), ("le", 3), ("rS", 1, 1), ("wp", 3), ("s3", 1, 2),
    ("rS", 0, 3), ("s3", 0, 2), ("rS", 1, 3), ("mul", 3, 1), ("mul", 1, 1), ("free", 0),
    ("mul", 1, 0), ("s3", 1, 1), ("mul", 2, 0), ("s3", 0, 3), ("free", 2), ("s3", 1, 3),
    ("mul", 3, 3), ("free", 1), ("mul", 1, 3), ("mul", 0, 2), ("mul", 3, 2), ("mul", 2, 1),
    ("mul", 2, 3), ("mul", 1, 2), ("mul", 2, 2), ("lg",), ("ab", 2), ("relay", 0), ("le", 5),
    ("relay", 1), ("relay", 2), ("ab", 3), ("fin", 0), ("ab", 1), ("hand", 2), ("ab", 0),
    ("free", 3), ("hand", 5), ("hand", 6), ("le", 6), ("le", 1), ("hand", 0), ("hand", 3),
    ("fin", 1), ("fin", 2), ("r2", 0), ("r2", 1), ("hand", 7), ("hand", 4), ("hand", 1),
    ("relay", 3), ("fin", 3), ("f2",),
)
RS_OFFS = (2, 1, 3, 0)
NT = (((1,), (1,)), ((), ()))
TN = (((0,), (0,)), ((), ()))


def dot(a, b, dims=(((1,), (0,)), ((), ()))):
    return lax.dot_general(a, b, dims, preferred_element_type=F32)


def turn(x, cosine, sine):
    return x * cosine + pltpu.roll(x, HD // 2, 1) * sine


def kernel(
    hid_hbm, gt_hbm, cnt_ref, cos_ref, sin_ref, q_hbm, k_hbm, w_hbm, og_hbm,
    qgo, kgo, wgo, up,
    hid, gt, q, k, og, wf, normed, pnorm, gain, krot, qrot, probs, vg2, vals, lg, stg,
    rl, fin, rl2, fin2, wacc, cbuf, col, hin, fixr, rb, vlow,
    loc, ssem, rf, rs, rp, cs, cr, ps, pr, lss, lsr, rrl, rfin, rrl2, rfin2, hs, hr, fx, rbs, rbr,
):
    sec = lax.axis_index("section")
    dp = lax.axis_index("dp")
    core = lax.rem(dp, 2)
    y = dp // 8
    z = lax.rem(dp // 2, 4)
    other = 1 - core

    def at(yy, zz, cc):
        return (sec, (yy * 4 + zz) * 2 + cc)

    def near(axis, step):
        if axis == "y":
            return at(lax.rem(y + step + 4, 4), z, core)
        return at(y, lax.rem(z + step + 4, 4), core)

    partner = at(y, z, other)

    def spot(yo, zo):
        return lax.rem(y + yo, 4) * 4 + lax.rem(z + zo, 4)

    def place(first, fo, so):
        return spot(fo, so) if first == "y" else spot(so, fo)

    gives_early = jnp.logical_and(sec != 0, sec != 4)
    gets_early = jnp.logical_and(sec != NS - 1, sec != 3)
    below = lax.rem(sec + NS - 1, NS)

    here = y * 4 + z

    loads = [
        pltpu.make_async_copy(k_hbm, k, loc.at[0]),
        pltpu.make_async_copy(q_hbm, q, loc.at[1]),
        pltpu.make_async_copy(og_hbm, og, loc.at[2]),
        pltpu.make_async_copy(hid_hbm, hid, loc.at[3]),
        pltpu.make_async_copy(gt_hbm, gt, loc.at[4]),
        pltpu.make_async_copy(w_hbm, wf.at[here, core], loc.at[5]),
    ]
    loads[0].start()
    loads[1].start()
    loads[2].start()
    cbuf[0] = jnp.full((8, 128), cnt_ref[0], jnp.int32)

    barrier = pltpu.get_barrier_semaphore()
    ids = [near("y", 1), near("y", -1), near("z", 1), near("z", -1), partner]
    ids += [(lax.rem(sec + i, NS), dp) for i in range(1, NS)]
    for one in ids:
        pl.semaphore_signal(barrier, inc=1, device_id=one, device_id_type=MESH)
    pl.semaphore_wait(barrier, len(ids))

    sent = []

    def send(src, dst, recv, device):
        copy = pltpu.make_async_remote_copy(
            src_ref=src, dst_ref=dst, send_sem=ssem.at[len(sent)], recv_sem=recv,
            device_id=device, device_id_type=MESH,
        )
        sent.append(copy)
        copy.start()

    def arrived(dst, recv):
        pltpu.make_async_remote_copy(
            src_ref=dst, dst_ref=dst, send_sem=ssem.at[0], recv_sem=recv,
            device_id=partner, device_id_type=MESH,
        ).wait_recv()

    HALF = (pl.ds(0, 128), pl.ds(128, 128))
    FULL = pl.ds(0, SH)

    def piece(c, fo, so, rows):
        first, _, c0, cw = COLOURS[c]
        return wf.at[place(first, fo, so), core, rows, pl.ds(c0, cw)]

    def to_second(c, fi):
        first, second, c0, cw = COLOURS[c]
        src = w_hbm.at[:, pl.ds(c0, cw)] if fi == 0 else piece(c, OFFS[fi], 0, FULL)
        dst = piece(c, OFFS[fi], 0, FULL)
        send(src, dst, rs.at[c, fi, 0], near(second, 1))
        send(src, dst, rs.at[c, fi, 1], near(second, -1))

    def to_partner(c, fi, si):
        first, second, c0, cw = COLOURS[c]
        dst = piece(c, OFFS[fi], OFFS[si], FULL)
        src = w_hbm.at[:, pl.ds(c0, cw)] if fi == 0 and si == 0 else dst
        send(src, dst, rp.at[c, fi, si], partner)

    def first_own(c):
        _, _, c0, cw = COLOURS[c]
        first, src, dst = COLOURS[c][0], w_hbm.at[:, pl.ds(c0, cw)], piece(c, 0, 0, FULL)
        send(src, dst, rf.at[c, 0], near(first, 1))
        send(src, dst, rf.at[c, 1], near(first, -1))
        to_partner(c, 0, 0)

    def first12(c, fi):
        step, half = ((1, 0), (-1, 1))[fi - 1]
        arrived(piece(c, OFFS[fi], 0, FULL), rf.at[c, fi - 1])
        part = piece(c, OFFS[fi], 0, HALF[half])
        send(part, part, rf.at[c, 2 + half], near(COLOURS[c][0], step))
        to_partner(c, fi, 0)

    def first3(c):
        for half in (0, 1):
            arrived(piece(c, 2, 0, HALF[half]), rf.at[c, 2 + half])
        to_second(c, 3)
        to_partner(c, 3, 0)

    def second12(c, fi):
        second = COLOURS[c][1]
        for si, (step, half) in ((1, (1, 0)), (2, (-1, 1))):
            arrived(piece(c, OFFS[fi], OFFS[si], FULL), rs.at[c, fi, si - 1])
            part = piece(c, OFFS[fi], OFFS[si], HALF[half])
            send(part, part, rs.at[c, fi, 2 + half], near(second, step))
            to_partner(c, fi, si)

    def second3(c, fi):
        for half in (0, 1):
            arrived(piece(c, OFFS[fi], 2, HALF[half]), rs.at[c, fi, 2 + half])
        to_partner(c, fi, 3)

    def from_partner(c, fi, si):
        first, _, c0, cw = COLOURS[c]
        arrived(
            wf.at[place(first, OFFS[fi], OFFS[si]), other, FULL, pl.ds(c0, cw)], rp.at[c, fi, si]
        )

    def multiply(yo, zo):
        from_partner(0, INDEX[zo], INDEX[yo])
        from_partner(1, INDEX[yo], INDEX[zo])
        p = spot(yo, zo)
        vals[...] += dot(normed[p, 0], wf[p, 0]) + dot(normed[p, 1], wf[p, 1])

    def chunk(ref, i):
        return ref.at[:, pl.ds(pl.multiple_of(i * 512, 512), 512)]

    def ahead(i):
        p = spot(*EARLY[i])
        return pltpu.make_async_remote_copy(
            src_ref=chunk(hid_hbm, p), dst_ref=hin.at[i], send_sem=hs.at[i], recv_sem=hr.at[i],
            device_id=(below, dp), device_id_type=MESH,
        )

    def passing(i):
        return pltpu.make_async_remote_copy(
            src_ref=chunk(lg, i), dst_ref=chunk(up, i), send_sem=lss.at[i], recv_sem=lsr.at[i],
            device_id=(below, dp), device_id_type=MESH,
        )

    def first_term(p):
        cols = pl.ds(pl.multiple_of(p * 512, 512), 512)
        d_normed = dot(vg2[0], wf[p].reshape(512, E), NT)
        inv = jnp.concatenate([col[0]] * 4, axis=1)
        return cols, inv * (gain[:, cols] * d_normed)

    def leave_early(i):
        p = spot(*EARLY[i])

        @pl.when(gives_early)
        def _():
            cols, term = first_term(p)
            lg[:, cols] = term.astype(BF16)
            passing(p).start()

    def fixing():
        return pltpu.make_async_remote_copy(
            src_ref=col.at[1], dst_ref=fixr, send_sem=fx.at[0], recv_sem=fx.at[1],
            device_id=(below, dp), device_id_type=MESH,
        )

    def whole_term(p):
        cols, term = first_term(p)
        fix = jnp.concatenate([col[1]] * 4, axis=1)
        lg[:, cols] = (term - hid[:, cols].astype(F32) * fix).astype(BF16)

    def counting(i):
        return pltpu.make_async_remote_copy(
            src_ref=cbuf.at[0], dst_ref=cbuf.at[i], send_sem=cs.at[i - 1], recv_sem=cr.at[i - 1],
            device_id=(lax.rem(sec + i, NS), dp), device_id_type=MESH,
        )

    def hidden_ahead():
        for i in range(1, NS):
            counting(i).start()
        for load in loads[3:]:
            load.start()

        @pl.when(gives_early)
        def _():
            for i in range(len(EARLY)):
                ahead(i).start()

        for load in loads[:3]:
            load.wait()
        for g in range(HK):
            k_g = k[:, g * HD : (g + 1) * HD].astype(F32)
            krot[g] = turn(k_g, cosine[...], sine[...]).astype(BF16)

    cosine, sine = cos_ref, sin_ref

    def attend(g):
        for r in range(SHARE):
            h = g * SHARE + r
            qrot[g, r * T : (r + 1) * T] = turn(
                q[:, h * HD : (h + 1) * HD].astype(F32), cosine[...], sine[...]
            ).astype(BF16)
        total = jnp.zeros((T, HD), F32)
        for r in range(0, SHARE, 2):
            rows = slice(r * T, (r + 2) * T)
            scores = dot(qrot[g, rows], krot[g], NT) * SCALE
            row = lax.broadcasted_iota(jnp.int32, (2 * T, T), 0)
            row = jnp.where(row >= T, row - T, row)
            lane = lax.broadcasted_iota(jnp.int32, (2 * T, T), 1)
            scores = jnp.where(row >= lane, scores, -1e30)
            expo = jnp.exp(scores - jnp.max(scores, axis=-1, keepdims=True))
            p = expo / jnp.sum(expo, axis=-1, keepdims=True)
            probs[g, rows] = p
            h = g * SHARE + r
            d_out = jnp.concatenate(
                [og[:, h * HD : (h + 1) * HD], og[:, (h + 1) * HD : (h + 2) * HD]], axis=0
            )
            total = total + dot(p.astype(BF16), d_out, TN)
        vg2[0, :, g * HD : (g + 1) * HD] = total.astype(BF16)

    pair = pltpu.make_async_remote_copy(
        src_ref=normed.at[:, other], dst_ref=pnorm, send_sem=ps.at[0], recv_sem=pr.at[0],
        device_id=partner, device_id_type=MESH,
    )
    pair_vg = pltpu.make_async_remote_copy(
        src_ref=vg2.at[0], dst_ref=vg2.at[1], send_sem=ps.at[1], recv_sem=pr.at[1],
        device_id=partner, device_id_type=MESH,
    )

    def norm():
        pair_vg.start()
        for i in range(1, NS):
            counting(i).wait_recv()
        last = cbuf[0] - 1
        for i in range(1, NS):
            last = last + jnp.where(sec >= i, cbuf[i], 0)
        loads[3].wait()
        loads[4].wait()

        @pl.loop(0, 8)
        def _(i):
            cols = pl.ds(pl.multiple_of(i * 1024, 1024), 1024)
            rows = lax.broadcasted_iota(jnp.int32, (40, 1024), 0)
            table = gt[:, cols].astype(F32)
            same = rows == jnp.broadcast_to(last[0:1, 0:1], (40, 1024))
            gain[:, cols] = jnp.sum(jnp.where(same, table, 0.0), axis=0, keepdims=True)

        def squares(i, acc):
            x = hid[:, pl.ds(pl.multiple_of(i * SH, SH), SH)].astype(F32)
            return acc + x * x

        acc = lax.fori_loop(0, 32, squares, jnp.zeros((T, SH), F32))
        inverse = lax.rsqrt(jnp.sum(acc, axis=-1, keepdims=True) * (1.0 / D) + 1e-05)
        col[0] = jnp.broadcast_to(inverse, (T, 128))

        @pl.loop(0, 16)
        def _(i):
            for c in range(2):
                cols = pl.ds(pl.multiple_of(i * 512 + c * SH, SH), SH)
                x = hid[:, cols].astype(F32)
                inv = jnp.concatenate([col[0]] * 2, axis=1)
                normed[i, c] = (x * inv * gain[:, cols]).astype(BF16)

        pair.start()
        vals[...] = jnp.zeros((T, E), F32)
        loads[5].wait()

    def weight_part(p):
        left = jnp.concatenate([normed[p, core], pnorm[p]], axis=0)
        right = jnp.concatenate([vg2[0], vg2[1]], axis=0)
        stg[p] = dot(left, right, TN).astype(BF16)

    def weight_parts(yo):
        if not paired:
            paired.append(True)
            pair.wait_recv()
            pair_vg.wait_recv()

        @pl.loop(0, 4)
        def _(i):
            weight_part(lax.rem(y + yo, 4) * 4 + i)

    paired = []

    def part(yo, zo, rows):
        return stg.at[spot(yo, zo), rows]

    def free_sends(oi):
        zo = RS_OFFS[oi]
        up1, down1 = near("y", 1), near("y", -1)
        send(part(2, zo, HALF[0]), rl.at[oi, 0], rrl.at[oi, 0], up1)
        send(part(2, zo, HALF[1]), rl.at[oi, 1], rrl.at[oi, 1], down1)
        send(part(1, zo, HALF[1]), fin.at[oi, 0, HALF[1]], rfin.at[oi, 0, 1], up1)
        send(part(3, zo, HALF[0]), fin.at[oi, 1, HALF[0]], rfin.at[oi, 1, 0], down1)

    def relay(oi):
        for side, (yo, step) in enumerate(((1, 1), (3, -1))):
            arrived(rl.at[oi, side], rrl.at[oi, side])
            p, rows = spot(yo, RS_OFFS[oi]), slice(side * 128, side * 128 + 128)
            stg[p, rows] = (stg[p, rows].astype(F32) + rl[oi, side].astype(F32)).astype(BF16)
            send(
                stg.at[p, HALF[side]], fin.at[oi, side, HALF[side]], rfin.at[oi, side, side],
                near("y", step),
            )

    def finish(oi):
        zo = RS_OFFS[oi]
        for side in range(2):
            for half in range(2):
                arrived(fin.at[oi, side, HALF[half]], rfin.at[oi, side, half])
        p = spot(0, zo)
        total = stg[p].astype(F32) + fin[oi, 0].astype(F32) + fin[oi, 1].astype(F32)
        if zo == 0:
            wacc[...] = total
            return
        stg[p] = total.astype(BF16)
        up1, down1 = near("z", 1), near("z", -1)
        if zo == 2:
            send(part(0, 2, HALF[0]), rl2.at[0], rrl2.at[0], up1)
            send(part(0, 2, HALF[1]), rl2.at[1], rrl2.at[1], down1)
        elif zo == 1:
            send(part(0, 1, HALF[1]), fin2.at[0, HALF[1]], rfin2.at[0, 1], up1)
        else:
            send(part(0, 3, HALF[0]), fin2.at[1, HALF[0]], rfin2.at[1, 0], down1)

    def relay2(side):
        zo, step = ((1, 1), (3, -1))[side]
        arrived(rl2.at[side], rrl2.at[side])
        p, rows = spot(0, zo), slice(side * 128, side * 128 + 128)
        stg[p, rows] = (stg[p, rows].astype(F32) + rl2[side].astype(F32)).astype(BF16)
        send(
            stg.at[p, HALF[side]], fin2.at[side, HALF[side]], rfin2.at[side, side],
            near("z", step),
        )

    def finish2():
        for side in range(2):
            for half in range(2):
                arrived(fin2.at[side, HALF[half]], rfin2.at[side, half])
        total = wacc[...] + fin2[0].astype(F32) + fin2[1].astype(F32)
        wgo[...] = total.astype(BF16)

    def late_terms():
        inverse = col[0][:, 0:1]
        mean = jnp.sum(vg2[0].astype(F32) * vals[...], axis=-1, keepdims=True) * (1.0 / D)
        col[1] = jnp.broadcast_to(inverse * inverse * mean, (T, 128))

        @pl.when(gives_early)
        def _():
            fixing().start()

            for yo, zo in LATE:
                p = spot(yo, zo)
                whole_term(p)
                passing(p).start()

        @pl.when(sec == 4)
        def _():
            @pl.loop(0, 16)
            def _(n):
                p = spot(n // 4, lax.rem(n, 4))
                whole_term(p)
                pltpu.make_async_remote_copy(
                    src_ref=chunk(lg, p), dst_ref=rb.at[n // 2], send_sem=lss.at[p],
                    recv_sem=rbr.at[n // 2], device_id=(lax.rem(n, 2) * 7, dp),
                    device_id_type=MESH,
                ).start()

        vlow[...] = vals[...].astype(BF16)

    relays = jnp.logical_or(sec == 0, sec == NS - 1)

    def handing(j):
        n = 2 * j + sec // 7
        p = spot(n // 4, lax.rem(n, 4))
        return pltpu.make_async_remote_copy(
            src_ref=rb.at[j], dst_ref=chunk(up, p), send_sem=rbs.at[j], recv_sem=lsr.at[p],
            device_id=(3, dp), device_id_type=MESH,
        )

    def hand_on(*js):
        @pl.when(relays)
        def _():
            for j in js:
                arrived(rb.at[j], rbr.at[j])
                handing(j).start()

    def attend_back(g):
        value = vlow[:, g * HD : (g + 1) * HD]
        total = jnp.zeros((T, HD), F32)
        for r in range(0, SHARE, 2):
            h = g * SHARE + r
            rows = slice(r * T, (r + 2) * T)
            d_out = jnp.concatenate(
                [og[:, h * HD : (h + 1) * HD], og[:, (h + 1) * HD : (h + 2) * HD]], axis=0
            )
            d_probs = dot(d_out, value, NT)
            p = probs[g, rows]
            low = p.astype(BF16).astype(F32)
            delta = jnp.sum(low * d_probs, axis=-1, keepdims=True)
            d_scores = (p * (d_probs - delta) * SCALE).astype(BF16)
            total = total + dot(d_scores, qrot[g, rows], TN)
            dq = dot(d_scores, krot[g])
            for i in range(2):
                one = turn(dq[i * T : (i + 1) * T], cosine[...], -sine[...])
                qgo[:, (h + i) * HD : (h + i + 1) * HD] = one.astype(BF16)
        kgo[:, g * HD : (g + 1) * HD] = turn(total, cosine[...], -sine[...]).astype(BF16)

    @pl.when(sec == NS - 1)
    def _():
        up[...] = jnp.zeros((T, D), BF16)

    steps = {
        "oF": first_own, "oS": lambda c: to_second(c, 0), "rF": first12, "sF": to_second,
        "f3": first3, "rS": second12, "s3": second3, "hid": hidden_ahead, "att": attend,
        "norm": norm, "wp": weight_parts, "mul": multiply, "le": leave_early, "lg": late_terms,
        "free": free_sends, "relay": relay, "fin": finish, "r2": relay2, "f2": finish2,
        "ab": attend_back, "hand": hand_on,
    }
    for step in ORDER:
        steps[step[0]](*step[1:])

    @pl.when(gets_early)
    def _():
        fixing().wait_recv()
        fix = jnp.concatenate([fixr[...]] * 4, axis=1)
        for i in range(len(EARLY)):
            p = spot(*EARLY[i])
            ahead(i).wait_recv()
            passing(p).wait_recv()
            cols = pl.ds(pl.multiple_of(p * 512, 512), 512)
            up[:, cols] = (up[:, cols].astype(F32) - hin[i].astype(F32) * fix).astype(BF16)

        for yo, zo in LATE:
            passing(spot(yo, zo)).wait_recv()

    @pl.when(sec == 3)
    def _():
        @pl.loop(0, 16)
        def _(i):
            passing(i).wait_recv()

    @pl.when(relays)
    def _():
        for j in range(8):
            handing(j).wait_send()

    @pl.when(gives_early)
    def _():
        fixing().wait_send()
        for i in range(len(EARLY)):
            ahead(i).wait_send()

    @pl.when(sec > 0)
    def _():
        @pl.loop(0, 16)
        def _(i):
            passing(i).wait_send()

    for copy in sent:
        copy.wait_send()
    for i in range(1, NS):
        counting(i).wait_send()
    pair.wait_send()
    pair_vg.wait_send()


def shards(hidden, gain_table, layer_counts, positions, queries, keys, value_weight, out_grad):
    half = HD // 2
    freq = jnp.exp(jnp.arange(half, dtype=F32) * (-2.0 * math.log(500000.0) / HD))
    angle = positions[0].astype(F32)[:, None] * freq[None, :]
    cosine, sine = jnp.cos(angle), jnp.sin(angle)
    cosine = jnp.concatenate([cosine, cosine], axis=1)
    sine = jnp.concatenate([-sine, sine], axis=1)
    anywhere = pl.BlockSpec(memory_space=pl.ANY)
    vmem = pl.BlockSpec(memory_space=pltpu.VMEM)
    smem = pl.BlockSpec(memory_space=pltpu.SMEM)
    dma = pltpu.SemaphoreType.DMA
    scratch = [
        pltpu.VMEM((T, D), BF16),
        pltpu.VMEM((40, D), BF16),
        pltpu.VMEM((T, HQ * HD), BF16),
        pltpu.VMEM((T, HK * HD), BF16),
        pltpu.VMEM((T, HQ * HD), BF16),
        pltpu.VMEM((16, 2, SH, E), BF16),
        pltpu.VMEM((16, 2, T, SH), BF16),
        pltpu.VMEM((16, T, SH), BF16),
        pltpu.VMEM((1, D), F32),
        pltpu.VMEM((HK, T, HD), BF16),
        pltpu.VMEM((HK, SHARE * T, HD), BF16),
        pltpu.VMEM((HK, SHARE * T, T), F32),
        pltpu.VMEM((2, T, E), BF16),
        pltpu.VMEM((T, E), F32),
        pltpu.VMEM((T, D), BF16),
        pltpu.VMEM((16, SH, E), BF16),
    ]
    scratch += [
        pltpu.VMEM((4, 2, 128, E), BF16),
        pltpu.VMEM((4, 2, SH, E), BF16),
        pltpu.VMEM((2, 128, E), BF16),
        pltpu.VMEM((2, SH, E), BF16),
        pltpu.VMEM((SH, E), F32),
        pltpu.VMEM((NS, 8, 128), jnp.int32),
        pltpu.VMEM((2, T, 128), F32),
        pltpu.VMEM((len(EARLY), T, 512), BF16),
        pltpu.VMEM((T, 128), F32),
        pltpu.VMEM((8, T, 512), BF16),
        pltpu.VMEM((T, E), BF16),
        dma((6,)),
        dma((104,)),
        dma((2, 4)),
        dma((2, 4, 4)),
        dma((2, 4, 4)),
        dma((7,)),
        dma((7,)),
        dma((2,)),
        dma((2,)),
        dma((16,)),
        dma((16,)),
        dma((4, 2)),
        dma((4, 2, 2)),
        dma((2,)),
        dma((2, 2)),
        dma((len(EARLY),)),
        dma((len(EARLY),)),
        dma((2,)),
        dma((8,)),
        dma((8,)),
    ]
    query_grad, key_grad, weight_grad, upstream = pl.pallas_call(
        kernel,
        out_shape=(
            pltpu.VMEM((T, HQ * HD), BF16),
            pltpu.VMEM((T, HK * HD), BF16),
            pltpu.VMEM((SH, E), BF16),
            pltpu.VMEM((T, D), BF16),
        ),
        in_specs=[anywhere, anywhere, smem, vmem, vmem] + [anywhere] * 4,
        out_specs=(vmem,) * 4,
        scratch_shapes=scratch,
        compiler_params=pltpu.CompilerParams(
            collective_id=0, has_side_effects=True, vmem_limit_bytes=56 << 20
        ),
    )(
        hidden[0], gain_table, layer_counts, cosine, sine, queries[0], keys[0], value_weight[0],
        out_grad[0],
    )
    return (query_grad[None], key_grad[None], weight_grad[None], upstream[None])


def solution(mesh):
    rows = P("section", "dp", None)
    in_specs = (rows, P(), P("section"), P("section", "dp"), rows, rows, rows, rows)
    return jax.shard_map(
        shards, mesh=mesh, in_specs=in_specs, out_specs=(rows,) * 4, check_vma=False
    )
```

```python
import functools
import math

import jax
import jax.numpy as jnp
from jax import lax
from jax.experimental import pallas as pl
from jax.experimental.pallas import tpu as pltpu
from jax.sharding import PartitionSpec as P

HQ = 32
HK = 4
HD = 128
SHARE = HQ // HK
SCALE = HD ** (-0.5)
T = 128
D = 8192
E = HK * HD
SH = 256
NS = 8
MESH = pl.DeviceIdType.MESH
F32 = jnp.float32
BF16 = jnp.bfloat16

COLOURS = (("z", "y", 0, 384), ("y", "z", 384, 128))
SUMS = (("y", "z", 0, 224), ("z", "y", 224, 32))
OFFS = (0, 3, 1, 2)
INDEX = {0: 0, 3: 1, 1: 2, 2: 3}
EARLY = ((0, 0), (1, 0), (3, 0), (0, 1), (0, 3), (2, 0), (0, 2))
LATE = tuple((i, j) for i in range(4) for j in range(4) if (i, j) not in EARLY)
ORDER = (
    ("oF", 0), ("oF", 1), ("oS", 0), ("hid",), ("att", 3), ("att", 0), ("att", 1), ("att", 2),
    ("rF", 1, 2), ("rF", 1, 1), ("norm",), ("rS", 0, 0), ("oS", 1), ("rF", 0, 1), ("sF", 0, 1),
    ("mul", 0, 0), ("le", 0), ("rF", 0, 2), ("rS", 1, 0), ("sF", 1, 2), ("sF", 0, 2), ("mul", 0, 1),
    ("le", 3), ("rS", 0, 1), ("sF", 1, 1), ("mul", 0, 3), ("le", 4), ("f3", 0), ("s3", 1, 0),
    ("s3", 0, 0), ("mul", 3, 0), ("le", 2), ("rS", 1, 2), ("s3", 0, 1), ("wp", 2), ("f3", 1),
    ("wp", 0), ("rS", 0, 2), ("wp", 1), ("rS", 1, 1), ("wp", 3), ("s3", 1, 2), ("rS", 0, 3),
    ("s3", 0, 2), ("rS", 1, 3), ("mul", 3, 1), ("mul", 1, 1), ("mul", 1, 0), ("le", 1),
    ("s3", 1, 1), ("mul", 2, 0), ("le", 5), ("free", 0, 0), ("free", 1, 0), ("s3", 0, 3),
    ("free", 0, 1), ("free", 1, 1), ("s3", 1, 3), ("mul", 3, 3), ("free", 0, 2), ("free", 1, 2),
    ("mul", 1, 3), ("mul", 0, 2), ("le", 6), ("mul", 3, 2), ("mul", 2, 1), ("mul", 2, 3),
    ("mul", 1, 2), ("mul", 2, 2), ("lg",), ("relay", 0, 0), ("relay", 1, 0), ("ab", 0),
    ("hand", 0, 5, 0, 7), ("free", 0, 3), ("free", 1, 3), ("relay", 0, 1), ("relay", 1, 1),
    ("hand", 1, 0, 7), ("ab", 1), ("fin", 0, 0), ("fin", 1, 0), ("hand", 0, 1, 6), ("relay", 0, 2),
    ("relay", 1, 2), ("hand", 1, 5), ("hand", 2, 0, 7), ("ab", 2), ("hand", 0, 2), ("fin", 0, 1),
    ("fin", 1, 1), ("hand", 1, 1, 6), ("hand", 3, 0, 7), ("r2", 0, 0), ("r2", 1, 0), ("hand", 2, 5),
    ("hand", 4, 0, 7), ("relay", 0, 3), ("relay", 1, 3), ("hand", 1, 2), ("ab", 3),
    ("hand", 2, 1, 6), ("fin", 0, 2), ("fin", 1, 2), ("r2", 0, 1), ("r2", 1, 1), ("hand", 2, 2),
    ("fin", 0, 3), ("fin", 1, 3), ("f2", 0), ("f2", 1),
)
RS_OFFS = (2, 1, 3, 0)
NT = (((1,), (1,)), ((), ()))
TN = (((0,), (0,)), ((), ()))


def dot(a, b, dims=(((1,), (0,)), ((), ()))):
    return lax.dot_general(a, b, dims, preferred_element_type=F32)


def turn(x, cosine, sine):
    return x * cosine + pltpu.roll(x, HD // 2, 1) * sine


def kernel(
    hid_hbm, gt_hbm, cnt_ref, cos_ref, sin_ref, q_hbm, k_hbm, w_hbm, og_hbm,
    qgo, kgo, wgo, up,
    hid, gt, q, k, og, wf, normed, pnorm, gain, krot, qrot, probs, vg2, vals, lg, stg,
    rl, fin, rl2, fin2, wacc, cbuf, col, hin, fixr, rb, vlow,
    loc, ssem, rf, rs, rp, cs, cr, ps, pr, lss, lsr, rrl, rfin, rrl2, rfin2, hs, hr, fx, rbs, rbr,
):
    sec = lax.axis_index("section")
    dp = lax.axis_index("dp")
    core = lax.rem(dp, 2)
    y = dp // 8
    z = lax.rem(dp // 2, 4)
    other = 1 - core

    def at(yy, zz, cc):
        return (sec, (yy * 4 + zz) * 2 + cc)

    def near(axis, step):
        if axis == "y":
            return at(lax.rem(y + step + 4, 4), z, core)
        return at(y, lax.rem(z + step + 4, 4), core)

    partner = at(y, z, other)

    def spot(yo, zo):
        return lax.rem(y + yo, 4) * 4 + lax.rem(z + zo, 4)

    def place(first, fo, so):
        return spot(fo, so) if first == "y" else spot(so, fo)

    gives_early = jnp.logical_and(sec != 0, sec != 4)
    gets_early = jnp.logical_and(sec != NS - 1, sec != 3)
    below = lax.rem(sec + NS - 1, NS)

    here = y * 4 + z

    loads = [
        pltpu.make_async_copy(k_hbm, k, loc.at[0]),
        pltpu.make_async_copy(q_hbm, q, loc.at[1]),
        pltpu.make_async_copy(og_hbm, og, loc.at[2]),
        pltpu.make_async_copy(hid_hbm, hid, loc.at[3]),
        pltpu.make_async_copy(gt_hbm, gt, loc.at[4]),
        pltpu.make_async_copy(w_hbm, wf.at[here, core], loc.at[5]),
    ]
    loads[0].start()
    loads[1].start()
    loads[2].start()
    cbuf[0] = jnp.full((8, 128), cnt_ref[0], jnp.int32)

    barrier = pltpu.get_barrier_semaphore()
    ids = [near("y", 1), near("y", -1), near("z", 1), near("z", -1), partner]
    ids += [(lax.rem(sec + i, NS), dp) for i in range(1, NS)]
    for one in ids:
        pl.semaphore_signal(barrier, inc=1, device_id=one, device_id_type=MESH)
    pl.semaphore_wait(barrier, len(ids))

    sent = []

    def send(src, dst, recv, device):
        copy = pltpu.make_async_remote_copy(
            src_ref=src, dst_ref=dst, send_sem=ssem.at[len(sent)], recv_sem=recv,
            device_id=device, device_id_type=MESH,
        )
        sent.append(copy)
        copy.start()

    def arrived(dst, recv):
        pltpu.make_async_remote_copy(
            src_ref=dst, dst_ref=dst, send_sem=ssem.at[0], recv_sem=recv,
            device_id=partner, device_id_type=MESH,
        ).wait_recv()

    HALF = (pl.ds(0, 128), pl.ds(128, 128))
    FULL = pl.ds(0, SH)

    def piece(c, fo, so, rows):
        first, _, c0, cw = COLOURS[c]
        return wf.at[place(first, fo, so), core, rows, pl.ds(c0, cw)]

    def to_second(c, fi):
        first, second, c0, cw = COLOURS[c]
        src = w_hbm.at[:, pl.ds(c0, cw)] if fi == 0 else piece(c, OFFS[fi], 0, FULL)
        dst = piece(c, OFFS[fi], 0, FULL)
        send(src, dst, rs.at[c, fi, 0], near(second, 1))
        send(src, dst, rs.at[c, fi, 1], near(second, -1))

    def to_partner(c, fi, si):
        first, second, c0, cw = COLOURS[c]
        dst = piece(c, OFFS[fi], OFFS[si], FULL)
        src = w_hbm.at[:, pl.ds(c0, cw)] if fi == 0 and si == 0 else dst
        send(src, dst, rp.at[c, fi, si], partner)

    def first_own(c):
        _, _, c0, cw = COLOURS[c]
        first, src, dst = COLOURS[c][0], w_hbm.at[:, pl.ds(c0, cw)], piece(c, 0, 0, FULL)
        send(src, dst, rf.at[c, 0], near(first, 1))
        send(src, dst, rf.at[c, 1], near(first, -1))
        to_partner(c, 0, 0)

    def first12(c, fi):
        step, half = ((1, 0), (-1, 1))[fi - 1]
        arrived(piece(c, OFFS[fi], 0, FULL), rf.at[c, fi - 1])
        part = piece(c, OFFS[fi], 0, HALF[half])
        send(part, part, rf.at[c, 2 + half], near(COLOURS[c][0], step))
        to_partner(c, fi, 0)

    def first3(c):
        for half in (0, 1):
            arrived(piece(c, 2, 0, HALF[half]), rf.at[c, 2 + half])
        to_second(c, 3)
        to_partner(c, 3, 0)

    def second12(c, fi):
        second = COLOURS[c][1]
        for si, (step, half) in ((1, (1, 0)), (2, (-1, 1))):
            arrived(piece(c, OFFS[fi], OFFS[si], FULL), rs.at[c, fi, si - 1])
            part = piece(c, OFFS[fi], OFFS[si], HALF[half])
            send(part, part, rs.at[c, fi, 2 + half], near(second, step))
            to_partner(c, fi, si)

    def second3(c, fi):
        for half in (0, 1):
            arrived(piece(c, OFFS[fi], 2, HALF[half]), rs.at[c, fi, 2 + half])
        to_partner(c, fi, 3)

    def from_partner(c, fi, si):
        first, _, c0, cw = COLOURS[c]
        arrived(
            wf.at[place(first, OFFS[fi], OFFS[si]), other, FULL, pl.ds(c0, cw)], rp.at[c, fi, si]
        )

    def multiply(yo, zo):
        from_partner(0, INDEX[zo], INDEX[yo])
        from_partner(1, INDEX[yo], INDEX[zo])
        p = spot(yo, zo)
        vals[...] += dot(normed[p, 0], wf[p, 0]) + dot(normed[p, 1], wf[p, 1])

    def chunk(ref, i):
        return ref.at[:, pl.ds(pl.multiple_of(i * 512, 512), 512)]

    def ahead(i):
        p = spot(*EARLY[i])
        return pltpu.make_async_remote_copy(
            src_ref=chunk(hid_hbm, p), dst_ref=hin.at[i], send_sem=hs.at[i], recv_sem=hr.at[i],
            device_id=(below, dp), device_id_type=MESH,
        )

    def passing(i):
        return pltpu.make_async_remote_copy(
            src_ref=chunk(lg, i), dst_ref=chunk(up, i), send_sem=lss.at[i], recv_sem=lsr.at[i],
            device_id=(below, dp), device_id_type=MESH,
        )

    def first_term(p):
        cols = pl.ds(pl.multiple_of(p * 512, 512), 512)
        d_normed = dot(vg2[0], wf[p].reshape(512, E), NT)
        inv = jnp.concatenate([col[0]] * 4, axis=1)
        return cols, inv * (gain[:, cols] * d_normed)

    def leave_early(i):
        p = spot(*EARLY[i])

        @pl.when(gives_early)
        def _():
            cols, term = first_term(p)
            lg[:, cols] = term.astype(BF16)
            passing(p).start()

    def fixing():
        return pltpu.make_async_remote_copy(
            src_ref=col.at[1], dst_ref=fixr, send_sem=fx.at[0], recv_sem=fx.at[1],
            device_id=(below, dp), device_id_type=MESH,
        )

    def whole_term(p):
        cols, term = first_term(p)
        fix = jnp.concatenate([col[1]] * 4, axis=1)
        lg[:, cols] = (term - hid[:, cols].astype(F32) * fix).astype(BF16)

    def counting(i):
        return pltpu.make_async_remote_copy(
            src_ref=cbuf.at[0], dst_ref=cbuf.at[i], send_sem=cs.at[i - 1], recv_sem=cr.at[i - 1],
            device_id=(lax.rem(sec + i, NS), dp), device_id_type=MESH,
        )

    def hidden_ahead():
        for i in range(1, NS):
            counting(i).start()
        for load in loads[3:]:
            load.start()

        @pl.when(gives_early)
        def _():
            for i in range(len(EARLY)):
                ahead(i).start()

        for load in loads[:3]:
            load.wait()
        for g in range(HK):
            k_g = k[:, g * HD : (g + 1) * HD].astype(F32)
            krot[g] = turn(k_g, cosine[...], sine[...]).astype(BF16)

    cosine, sine = cos_ref, sin_ref

    def attend(g):
        for r in range(SHARE):
            h = g * SHARE + r
            qrot[g, r * T : (r + 1) * T] = turn(
                q[:, h * HD : (h + 1) * HD].astype(F32), cosine[...], sine[...]
            ).astype(BF16)
        total = jnp.zeros((T, HD), F32)
        for r in range(0, SHARE, 2):
            rows = slice(r * T, (r + 2) * T)
            scores = dot(qrot[g, rows], krot[g], NT) * SCALE
            row = lax.broadcasted_iota(jnp.int32, (2 * T, T), 0)
            row = jnp.where(row >= T, row - T, row)
            lane = lax.broadcasted_iota(jnp.int32, (2 * T, T), 1)
            scores = jnp.where(row >= lane, scores, -1e30)
            expo = jnp.exp(scores - jnp.max(scores, axis=-1, keepdims=True))
            p = expo / jnp.sum(expo, axis=-1, keepdims=True)
            probs[g, rows] = p
            h = g * SHARE + r
            d_out = jnp.concatenate(
                [og[:, h * HD : (h + 1) * HD], og[:, (h + 1) * HD : (h + 2) * HD]], axis=0
            )
            total = total + dot(p.astype(BF16), d_out, TN)
        vg2[0, :, g * HD : (g + 1) * HD] = total.astype(BF16)

    pair = pltpu.make_async_remote_copy(
        src_ref=normed.at[:, other], dst_ref=pnorm, send_sem=ps.at[0], recv_sem=pr.at[0],
        device_id=partner, device_id_type=MESH,
    )
    pair_vg = pltpu.make_async_remote_copy(
        src_ref=vg2.at[0], dst_ref=vg2.at[1], send_sem=ps.at[1], recv_sem=pr.at[1],
        device_id=partner, device_id_type=MESH,
    )

    def norm():
        pair_vg.start()
        for i in range(1, NS):
            counting(i).wait_recv()
        last = cbuf[0] - 1
        for i in range(1, NS):
            last = last + jnp.where(sec >= i, cbuf[i], 0)
        loads[3].wait()
        loads[4].wait()

        @pl.loop(0, 8)
        def _(i):
            cols = pl.ds(pl.multiple_of(i * 1024, 1024), 1024)
            rows = lax.broadcasted_iota(jnp.int32, (40, 1024), 0)
            table = gt[:, cols].astype(F32)
            same = rows == jnp.broadcast_to(last[0:1, 0:1], (40, 1024))
            gain[:, cols] = jnp.sum(jnp.where(same, table, 0.0), axis=0, keepdims=True)

        def squares(i, acc):
            x = hid[:, pl.ds(pl.multiple_of(i * SH, SH), SH)].astype(F32)
            return acc + x * x

        acc = lax.fori_loop(0, 32, squares, jnp.zeros((T, SH), F32))
        inverse = lax.rsqrt(jnp.sum(acc, axis=-1, keepdims=True) * (1.0 / D) + 1e-05)
        col[0] = jnp.broadcast_to(inverse, (T, 128))

        @pl.loop(0, 16)
        def _(i):
            for c in range(2):
                cols = pl.ds(pl.multiple_of(i * 512 + c * SH, SH), SH)
                x = hid[:, cols].astype(F32)
                inv = jnp.concatenate([col[0]] * 2, axis=1)
                normed[i, c] = (x * inv * gain[:, cols]).astype(BF16)

        pair.start()
        vals[...] = jnp.zeros((T, E), F32)
        loads[5].wait()

    def weight_part(p):
        left = jnp.concatenate([normed[p, core], pnorm[p]], axis=0)
        right = jnp.concatenate([vg2[0], vg2[1]], axis=0)
        stg[p] = dot(left, right, TN).astype(BF16)

    def weight_parts(yo):
        if not paired:
            paired.append(True)
            pair.wait_recv()
            pair_vg.wait_recv()

        @pl.loop(0, 4)
        def _(i):
            weight_part(lax.rem(y + yo, 4) * 4 + i)

    paired = []

    def rows_of(c, half):
        return pl.ds(SUMS[c][2] + half * (SUMS[c][3] // 2), SUMS[c][3] // 2)

    def part(c, fo, so, half):
        return stg.at[place(SUMS[c][0], fo, so), rows_of(c, half)]

    def free_sends(c, oi):
        so = RS_OFFS[oi]
        up1, down1 = near(SUMS[c][0], 1), near(SUMS[c][0], -1)
        for side, there in ((0, up1), (1, down1)):
            send(part(c, 2, so, side), rl.at[oi, side, rows_of(c, side)], rrl.at[c, oi, side], there)
        for side, fo, there in ((0, 1, up1), (1, 3, down1)):
            rows = rows_of(c, 1 - side)
            send(
                part(c, fo, so, 1 - side), fin.at[oi, side, rows], rfin.at[c, oi, side, 1 - side],
                there,
            )

    def relay(c, oi):
        for side, (fo, step) in enumerate(((1, 1), (3, -1))):
            rows = rows_of(c, side)
            arrived(rl.at[oi, side, rows], rrl.at[c, oi, side])
            p = place(SUMS[c][0], fo, RS_OFFS[oi])
            stg[p, rows] = (stg[p, rows].astype(F32) + rl[oi, side, rows].astype(F32)).astype(BF16)
            send(
                stg.at[p, rows], fin.at[oi, side, rows], rfin.at[c, oi, side, side],
                near(SUMS[c][0], step),
            )

    def finish(c, oi):
        so = RS_OFFS[oi]
        for side in range(2):
            for half in range(2):
                arrived(fin.at[oi, side, rows_of(c, half)], rfin.at[c, oi, side, half])
        p = place(SUMS[c][0], 0, so)
        rows = pl.ds(SUMS[c][2], SUMS[c][3])
        total = stg[p, rows].astype(F32)
        total = total + fin[oi, 0, rows].astype(F32) + fin[oi, 1, rows].astype(F32)
        if so == 0:
            wacc[rows] = total
            return
        stg[p, rows] = total.astype(BF16)
        up1, down1 = near(SUMS[c][1], 1), near(SUMS[c][1], -1)
        if so == 2:
            for side, there in ((0, up1), (1, down1)):
                send(part(c, 0, 2, side), rl2.at[side, rows_of(c, side)], rrl2.at[c, side], there)
        elif so == 1:
            send(part(c, 0, 1, 1), fin2.at[0, rows_of(c, 1)], rfin2.at[c, 0, 1], up1)
        else:
            send(part(c, 0, 3, 0), fin2.at[1, rows_of(c, 0)], rfin2.at[c, 1, 0], down1)

    def relay2(c, side):
        so, step = ((1, 1), (3, -1))[side]
        rows = rows_of(c, side)
        arrived(rl2.at[side, rows], rrl2.at[c, side])
        p = place(SUMS[c][0], 0, so)
        stg[p, rows] = (stg[p, rows].astype(F32) + rl2[side, rows].astype(F32)).astype(BF16)
        send(
            stg.at[p, rows], fin2.at[side, rows], rfin2.at[c, side, side], near(SUMS[c][1], step)
        )

    def finish2(c):
        for side in range(2):
            for half in range(2):
                arrived(fin2.at[side, rows_of(c, half)], rfin2.at[c, side, half])
        rows = pl.ds(SUMS[c][2], SUMS[c][3])
        total = wacc[rows] + fin2[0, rows].astype(F32) + fin2[1, rows].astype(F32)
        wgo[rows] = total.astype(BF16)

    def late_terms():
        inverse = col[0][:, 0:1]
        mean = jnp.sum(vg2[0].astype(F32) * vals[...], axis=-1, keepdims=True) * (1.0 / D)
        col[1] = jnp.broadcast_to(inverse * inverse * mean, (T, 128))

        @pl.when(gives_early)
        def _():
            fixing().start()

            for yo, zo in LATE:
                p = spot(yo, zo)
                whole_term(p)
                passing(p).start()

        @pl.when(sec == 4)
        def _():
            for n in range(16):
                p = spot(n // 4, n % 4)
                whole_term(p)
                slot = n // 2 + 4 * (n % 2) if n < 6 else (n - 6) // 2
                goal = 5 if n < 6 else 7 * (n % 2)
                pltpu.make_async_remote_copy(
                    src_ref=chunk(lg, p), dst_ref=rb.at[slot], send_sem=lss.at[p],
                    recv_sem=rbr.at[slot], device_id=(goal, dp), device_id_type=MESH,
                ).start()

        vlow[...] = vals[...].astype(BF16)

    HOPS = {
        0: [[(j, 3, 6 + 2 * j)] for j in range(5)],
        7: [[(j, 3, 7 + 2 * j)] for j in range(5)],
        5: [[(j, 1, None), (4 + j, 6, None)] for j in range(3)],
        1: [[(j, 2, None)] for j in range(3)],
        6: [[(4 + j, 2, None)] for j in range(3)],
        2: [[(j, 3, 2 * j), (4 + j, 3, 2 * j + 1)] for j in range(3)],
    }

    def handing(slot, goal, n):
        if n is None:
            dst, recv = rb.at[slot], rbr.at[slot]
        else:
            p = spot(n // 4, n % 4)
            dst, recv = chunk(up, p), lsr.at[p]
        return pltpu.make_async_remote_copy(
            src_ref=rb.at[slot], dst_ref=dst, send_sem=rbs.at[slot], recv_sem=recv,
            device_id=(goal, dp), device_id_type=MESH,
        )

    def hand_on(j, *sections):
        for one in sections:

            @pl.when(sec == one)
            def _():
                for hop in HOPS[one][j]:
                    arrived(rb.at[hop[0]], rbr.at[hop[0]])
                    handing(*hop).start()

    def attend_back(g):
        value = vlow[:, g * HD : (g + 1) * HD]
        total = jnp.zeros((T, HD), F32)
        for r in range(0, SHARE, 2):
            h = g * SHARE + r
            rows = slice(r * T, (r + 2) * T)
            d_out = jnp.concatenate(
                [og[:, h * HD : (h + 1) * HD], og[:, (h + 1) * HD : (h + 2) * HD]], axis=0
            )
            d_probs = dot(d_out, value, NT)
            p = probs[g, rows]
            low = p.astype(BF16).astype(F32)
            delta = jnp.sum(low * d_probs, axis=-1, keepdims=True)
            d_scores = (p * (d_probs - delta) * SCALE).astype(BF16)
            total = total + dot(d_scores, qrot[g, rows], TN)
            dq = dot(d_scores, krot[g])
            for i in range(2):
                one = turn(dq[i * T : (i + 1) * T], cosine[...], -sine[...])
                qgo[:, (h + i) * HD : (h + i + 1) * HD] = one.astype(BF16)
        kgo[:, g * HD : (g + 1) * HD] = turn(total, cosine[...], -sine[...]).astype(BF16)

    @pl.when(sec == NS - 1)
    def _():
        up[...] = jnp.zeros((T, D), BF16)

    steps = {
        "oF": first_own, "oS": lambda c: to_second(c, 0), "rF": first12, "sF": to_second,
        "f3": first3, "rS": second12, "s3": second3, "hid": hidden_ahead, "att": attend,
        "norm": norm, "wp": weight_parts, "mul": multiply, "le": leave_early, "lg": late_terms,
        "free": free_sends, "relay": relay, "fin": finish, "r2": relay2, "f2": finish2,
        "ab": attend_back, "hand": hand_on,
    }
    for step in ORDER:
        steps[step[0]](*step[1:])

    @pl.when(gets_early)
    def _():
        fixing().wait_recv()
        fix = jnp.concatenate([fixr[...]] * 4, axis=1)
        for i in range(len(EARLY)):
            p = spot(*EARLY[i])
            ahead(i).wait_recv()
            passing(p).wait_recv()
            cols = pl.ds(pl.multiple_of(p * 512, 512), 512)
            up[:, cols] = (up[:, cols].astype(F32) - hin[i].astype(F32) * fix).astype(BF16)

        for yo, zo in LATE:
            passing(spot(yo, zo)).wait_recv()

    @pl.when(sec == 3)
    def _():
        @pl.loop(0, 16)
        def _(i):
            passing(i).wait_recv()

    for one, hops in HOPS.items():

        @pl.when(sec == one)
        def _():
            for pair_of in hops:
                for hop in pair_of:
                    handing(*hop).wait_send()

    @pl.when(gives_early)
    def _():
        fixing().wait_send()
        for i in range(len(EARLY)):
            ahead(i).wait_send()

    @pl.when(sec > 0)
    def _():
        @pl.loop(0, 16)
        def _(i):
            passing(i).wait_send()

    for copy in sent:
        copy.wait_send()
    for i in range(1, NS):
        counting(i).wait_send()
    pair.wait_send()
    pair_vg.wait_send()


def shards(hidden, gain_table, layer_counts, positions, queries, keys, value_weight, out_grad):
    half = HD // 2
    freq = jnp.exp(jnp.arange(half, dtype=F32) * (-2.0 * math.log(500000.0) / HD))
    angle = positions[0].astype(F32)[:, None] * freq[None, :]
    cosine, sine = jnp.cos(angle), jnp.sin(angle)
    cosine = jnp.concatenate([cosine, cosine], axis=1)
    sine = jnp.concatenate([-sine, sine], axis=1)
    anywhere = pl.BlockSpec(memory_space=pl.ANY)
    vmem = pl.BlockSpec(memory_space=pltpu.VMEM)
    smem = pl.BlockSpec(memory_space=pltpu.SMEM)
    dma = pltpu.SemaphoreType.DMA
    scratch = [
        pltpu.VMEM((T, D), BF16),
        pltpu.VMEM((40, D), BF16),
        pltpu.VMEM((T, HQ * HD), BF16),
        pltpu.VMEM((T, HK * HD), BF16),
        pltpu.VMEM((T, HQ * HD), BF16),
        pltpu.VMEM((16, 2, SH, E), BF16),
        pltpu.VMEM((16, 2, T, SH), BF16),
        pltpu.VMEM((16, T, SH), BF16),
        pltpu.VMEM((1, D), F32),
        pltpu.VMEM((HK, T, HD), BF16),
        pltpu.VMEM((HK, SHARE * T, HD), BF16),
        pltpu.VMEM((HK, SHARE * T, T), F32),
        pltpu.VMEM((2, T, E), BF16),
        pltpu.VMEM((T, E), F32),
        pltpu.VMEM((T, D), BF16),
        pltpu.VMEM((16, SH, E), BF16),
    ]
    scratch += [
        pltpu.VMEM((4, 2, SH, E), BF16),
        pltpu.VMEM((4, 2, SH, E), BF16),
        pltpu.VMEM((2, SH, E), BF16),
        pltpu.VMEM((2, SH, E), BF16),
        pltpu.VMEM((SH, E), F32),
        pltpu.VMEM((NS, 8, 128), jnp.int32),
        pltpu.VMEM((2, T, 128), F32),
        pltpu.VMEM((len(EARLY), T, 512), BF16),
        pltpu.VMEM((T, 128), F32),
        pltpu.VMEM((8, T, 512), BF16),
        pltpu.VMEM((T, E), BF16),
        dma((6,)),
        dma((136,)),
        dma((2, 4)),
        dma((2, 4, 4)),
        dma((2, 4, 4)),
        dma((7,)),
        dma((7,)),
        dma((2,)),
        dma((2,)),
        dma((16,)),
        dma((16,)),
        dma((2, 4, 2)),
        dma((2, 4, 2, 2)),
        dma((2, 2)),
        dma((2, 2, 2)),
        dma((len(EARLY),)),
        dma((len(EARLY),)),
        dma((2,)),
        dma((8,)),
        dma((8,)),
    ]
    query_grad, key_grad, weight_grad, upstream = pl.pallas_call(
        kernel,
        out_shape=(
            pltpu.VMEM((T, HQ * HD), BF16),
            pltpu.VMEM((T, HK * HD), BF16),
            pltpu.VMEM((SH, E), BF16),
            pltpu.VMEM((T, D), BF16),
        ),
        in_specs=[anywhere, anywhere, smem, vmem, vmem] + [anywhere] * 4,
        out_specs=(vmem,) * 4,
        scratch_shapes=scratch,
        compiler_params=pltpu.CompilerParams(
            collective_id=0, has_side_effects=True, vmem_limit_bytes=56 << 20
        ),
    )(
        hidden[0], gain_table, layer_counts, cosine, sine, queries[0], keys[0], value_weight[0],
        out_grad[0],
    )
    return (query_grad[None], key_grad[None], weight_grad[None], upstream[None])


def solution(mesh):
    rows = P("section", "dp", None)
    in_specs = (rows, P(), P("section"), P("section", "dp"), rows, rows, rows, rows)
    return jax.shard_map(
        shards, mesh=mesh, in_specs=in_specs, out_specs=(rows,) * 4, check_vma=False
    )
```

```python
import functools
import math

import jax
import jax.numpy as jnp
from jax import lax
from jax.experimental import pallas as pl
from jax.experimental.pallas import tpu as pltpu
from jax.sharding import PartitionSpec as P

HQ = 32
HK = 4
HD = 128
SHARE = HQ // HK
SCALE = HD ** (-0.5)
T = 128
D = 8192
E = HK * HD
SH = 256
NS = 8
MESH = pl.DeviceIdType.MESH
F32 = jnp.float32
BF16 = jnp.bfloat16

COLOURS = (("z", "y", 0, 384), ("y", "z", 384, 128))
SUMS = (("y", "z", 0, 224), ("z", "y", 224, 32))
OFFS = (0, 3, 1, 2)
INDEX = {0: 0, 3: 1, 1: 2, 2: 3}
EARLY = ((0, 0), (1, 0), (3, 0), (0, 1), (0, 3), (2, 0), (0, 2))
LATE = tuple((i, j) for i in range(4) for j in range(4) if (i, j) not in EARLY)
ORDER = (
    ("oF", 0), ("oF", 1), ("oS", 0), ("hid",), ("att", 3), ("att", 0), ("att", 1), ("att", 2),
    ("rF", 1, 2), ("rF", 1, 1), ("norm",), ("rS", 0, 0), ("oS", 1), ("rF", 0, 1), ("sF", 0, 1),
    ("mul", 0, 0), ("le", 0), ("rF", 0, 2), ("rS", 1, 0), ("sF", 1, 2), ("sF", 0, 2), ("mul", 0, 1),
    ("le", 3), ("rS", 0, 1), ("sF", 1, 1), ("mul", 0, 3), ("le", 4), ("f3", 0), ("s3", 1, 0),
    ("s3", 0, 0), ("mul", 3, 0), ("le", 2), ("rS", 1, 2), ("s3", 0, 1), ("wp", 2), ("f3", 1),
    ("wp", 0), ("rS", 0, 2), ("wp", 1), ("rS", 1, 1), ("wp", 3), ("s3", 1, 2), ("rS", 0, 3),
    ("s3", 0, 2), ("rS", 1, 3), ("mul", 3, 1), ("mul", 1, 1), ("mul", 1, 0), ("le", 1),
    ("s3", 1, 1), ("mul", 2, 0), ("le", 5), ("free", 0, 0), ("free", 1, 0), ("s3", 0, 3),
    ("free", 0, 1), ("free", 1, 1), ("s3", 1, 3), ("mul", 3, 3), ("free", 0, 2), ("free", 1, 2),
    ("mul", 1, 3), ("mul", 0, 2), ("le", 6), ("mul", 3, 2), ("mul", 2, 1), ("mul", 2, 3),
    ("mul", 1, 2), ("mul", 2, 2), ("lg",), ("relay", 0, 0), ("relay", 1, 0), ("ab", 0),
    ("hand", 0, 5, 0, 7), ("free", 0, 3), ("free", 1, 3), ("relay", 0, 1), ("relay", 1, 1),
    ("hand", 1, 0, 7), ("ab", 1), ("fin", 0, 0), ("fin", 1, 0), ("hand", 0, 1, 6), ("relay", 0, 2),
    ("relay", 1, 2), ("hand", 1, 5), ("hand", 2, 0, 7), ("ab", 2), ("hand", 0, 2), ("fin", 0, 1),
    ("fin", 1, 1), ("hand", 1, 1, 6), ("hand", 3, 0, 7), ("r2", 0, 0), ("r2", 1, 0), ("hand", 2, 5),
    ("hand", 4, 0, 7), ("relay", 0, 3), ("relay", 1, 3), ("hand", 1, 2), ("ab", 3),
    ("hand", 2, 1, 6), ("fin", 0, 2), ("fin", 1, 2), ("r2", 0, 1), ("r2", 1, 1), ("hand", 2, 2),
    ("fin", 0, 3), ("fin", 1, 3), ("f2", 0), ("f2", 1),
)
RS_OFFS = (2, 1, 3, 0)
NT = (((1,), (1,)), ((), ()))
TN = (((0,), (0,)), ((), ()))


def dot(a, b, dims=(((1,), (0,)), ((), ()))):
    return lax.dot_general(a, b, dims, preferred_element_type=F32)


def turn(x, cosine, sine):
    return x * cosine + pltpu.roll(x, HD // 2, 1) * sine


def kernel(
    hid_hbm, gt_hbm, cnt_ref, pos_ref, q_hbm, k_hbm, w_hbm, og_hbm,
    qgo, kgo, wgo, up,
    hid, gt, q, k, og, wf, normed, pnorm, gain, krot, qrot, probs, vg2, vals, lg, stg,
    rl, fin, rl2, fin2, wacc, cbuf, col, hin, fixr, rb, vlow, cosine, sine,
    loc, ssem, rf, rs, rp, cs, cr, ps, pr, lss, lsr, rrl, rfin, rrl2, rfin2, hs, hr, fx, rbs, rbr,
):
    sec = lax.axis_index("section")
    dp = lax.axis_index("dp")
    core = lax.rem(dp, 2)
    y = dp // 8
    z = lax.rem(dp // 2, 4)
    other = 1 - core

    def at(yy, zz, cc):
        return (sec, (yy * 4 + zz) * 2 + cc)

    def near(axis, step):
        if axis == "y":
            return at(lax.rem(y + step + 4, 4), z, core)
        return at(y, lax.rem(z + step + 4, 4), core)

    partner = at(y, z, other)

    def spot(yo, zo):
        return lax.rem(y + yo, 4) * 4 + lax.rem(z + zo, 4)

    def place(first, fo, so):
        return spot(fo, so) if first == "y" else spot(so, fo)

    gives_early = jnp.logical_and(sec != 0, sec != 4)
    gets_early = jnp.logical_and(sec != NS - 1, sec != 3)
    below = lax.rem(sec + NS - 1, NS)

    here = y * 4 + z

    loads = [
        pltpu.make_async_copy(k_hbm, k, loc.at[0]),
        pltpu.make_async_copy(q_hbm, q, loc.at[1]),
        pltpu.make_async_copy(og_hbm, og, loc.at[2]),
        pltpu.make_async_copy(hid_hbm, hid, loc.at[3]),
        pltpu.make_async_copy(gt_hbm, gt, loc.at[4]),
        pltpu.make_async_copy(w_hbm, wf.at[here, core], loc.at[5]),
    ]
    loads[0].start()
    loads[1].start()
    loads[2].start()
    cbuf[0] = jnp.full((8, 128), cnt_ref[0], jnp.int32)

    barrier = pltpu.get_barrier_semaphore()
    ids = [near("y", 1), near("y", -1), near("z", 1), near("z", -1), partner]
    ids += [(lax.rem(sec + i, NS), dp) for i in range(1, NS)]
    for one in ids:
        pl.semaphore_signal(barrier, inc=1, device_id=one, device_id_type=MESH)
    pl.semaphore_wait(barrier, len(ids))

    sent = []

    def send(src, dst, recv, device):
        copy = pltpu.make_async_remote_copy(
            src_ref=src, dst_ref=dst, send_sem=ssem.at[len(sent)], recv_sem=recv,
            device_id=device, device_id_type=MESH,
        )
        sent.append(copy)
        copy.start()

    def arrived(dst, recv):
        pltpu.make_async_remote_copy(
            src_ref=dst, dst_ref=dst, send_sem=ssem.at[0], recv_sem=recv,
            device_id=partner, device_id_type=MESH,
        ).wait_recv()

    HALF = (pl.ds(0, 128), pl.ds(128, 128))
    FULL = pl.ds(0, SH)

    def piece(c, fo, so, rows):
        first, _, c0, cw = COLOURS[c]
        return wf.at[place(first, fo, so), core, rows, pl.ds(c0, cw)]

    def to_second(c, fi):
        first, second, c0, cw = COLOURS[c]
        src = w_hbm.at[:, pl.ds(c0, cw)] if fi == 0 else piece(c, OFFS[fi], 0, FULL)
        dst = piece(c, OFFS[fi], 0, FULL)
        send(src, dst, rs.at[c, fi, 0], near(second, 1))
        send(src, dst, rs.at[c, fi, 1], near(second, -1))

    def to_partner(c, fi, si):
        first, second, c0, cw = COLOURS[c]
        dst = piece(c, OFFS[fi], OFFS[si], FULL)
        src = w_hbm.at[:, pl.ds(c0, cw)] if fi == 0 and si == 0 else dst
        send(src, dst, rp.at[c, fi, si], partner)

    def first_own(c):
        _, _, c0, cw = COLOURS[c]
        first, src, dst = COLOURS[c][0], w_hbm.at[:, pl.ds(c0, cw)], piece(c, 0, 0, FULL)
        send(src, dst, rf.at[c, 0], near(first, 1))
        send(src, dst, rf.at[c, 1], near(first, -1))
        to_partner(c, 0, 0)

    def first12(c, fi):
        step, half = ((1, 0), (-1, 1))[fi - 1]
        arrived(piece(c, OFFS[fi], 0, FULL), rf.at[c, fi - 1])
        part = piece(c, OFFS[fi], 0, HALF[half])
        send(part, part, rf.at[c, 2 + half], near(COLOURS[c][0], step))
        to_partner(c, fi, 0)

    def first3(c):
        for half in (0, 1):
            arrived(piece(c, 2, 0, HALF[half]), rf.at[c, 2 + half])
        to_second(c, 3)
        to_partner(c, 3, 0)

    def second12(c, fi):
        second = COLOURS[c][1]
        for si, (step, half) in ((1, (1, 0)), (2, (-1, 1))):
            arrived(piece(c, OFFS[fi], OFFS[si], FULL), rs.at[c, fi, si - 1])
            part = piece(c, OFFS[fi], OFFS[si], HALF[half])
            send(part, part, rs.at[c, fi, 2 + half], near(second, step))
            to_partner(c, fi, si)

    def second3(c, fi):
        for half in (0, 1):
            arrived(piece(c, OFFS[fi], 2, HALF[half]), rs.at[c, fi, 2 + half])
        to_partner(c, fi, 3)

    def from_partner(c, fi, si):
        first, _, c0, cw = COLOURS[c]
        arrived(
            wf.at[place(first, OFFS[fi], OFFS[si]), other, FULL, pl.ds(c0, cw)], rp.at[c, fi, si]
        )

    def multiply(yo, zo):
        from_partner(0, INDEX[zo], INDEX[yo])
        from_partner(1, INDEX[yo], INDEX[zo])
        p = spot(yo, zo)
        vals[...] += dot(normed[p, 0], wf[p, 0]) + dot(normed[p, 1], wf[p, 1])

    def chunk(ref, i):
        return ref.at[:, pl.ds(pl.multiple_of(i * 512, 512), 512)]

    def ahead(i):
        p = spot(*EARLY[i])
        return pltpu.make_async_remote_copy(
            src_ref=chunk(hid_hbm, p), dst_ref=hin.at[i], send_sem=hs.at[i], recv_sem=hr.at[i],
            device_id=(below, dp), device_id_type=MESH,
        )

    def passing(i):
        return pltpu.make_async_remote_copy(
            src_ref=chunk(lg, i), dst_ref=chunk(up, i), send_sem=lss.at[i], recv_sem=lsr.at[i],
            device_id=(below, dp), device_id_type=MESH,
        )

    def first_term(p):
        cols = pl.ds(pl.multiple_of(p * 512, 512), 512)
        d_normed = dot(vg2[0], wf[p].reshape(512, E), NT)
        inv = jnp.concatenate([col[0]] * 4, axis=1)
        return cols, inv * (gain[:, cols] * d_normed)

    def leave_early(i):
        p = spot(*EARLY[i])

        @pl.when(gives_early)
        def _():
            cols, term = first_term(p)
            lg[:, cols] = term.astype(BF16)
            passing(p).start()

    def fixing():
        return pltpu.make_async_remote_copy(
            src_ref=col.at[1], dst_ref=fixr, send_sem=fx.at[0], recv_sem=fx.at[1],
            device_id=(below, dp), device_id_type=MESH,
        )

    def whole_term(p):
        cols, term = first_term(p)
        fix = jnp.concatenate([col[1]] * 4, axis=1)
        lg[:, cols] = (term - hid[:, cols].astype(F32) * fix).astype(BF16)

    def counting(i):
        return pltpu.make_async_remote_copy(
            src_ref=cbuf.at[0], dst_ref=cbuf.at[i], send_sem=cs.at[i - 1], recv_sem=cr.at[i - 1],
            device_id=(lax.rem(sec + i, NS), dp), device_id_type=MESH,
        )

    def hidden_ahead():
        for i in range(1, NS):
            counting(i).start()
        for load in loads[3:]:
            load.start()

        @pl.when(gives_early)
        def _():
            for i in range(len(EARLY)):
                ahead(i).start()

        places = jnp.broadcast_to(pos_ref[...].astype(F32), (T, HD)).T
        lane = lax.broadcasted_iota(jnp.int32, (T, HD), 1)
        entry = jnp.where(lane < HD // 2, lane, lane - HD // 2).astype(F32)
        angle = places * jnp.exp(entry * (-2.0 * math.log(500000.0) / HD))
        cosine[...] = jnp.cos(angle)
        sine[...] = jnp.where(lane < HD // 2, -1.0, 1.0) * jnp.sin(angle)
        for load in loads[:3]:
            load.wait()
        for g in range(HK):
            k_g = k[:, g * HD : (g + 1) * HD].astype(F32)
            krot[g] = turn(k_g, cosine[...], sine[...]).astype(BF16)

    def attend(g):
        for r in range(SHARE):
            h = g * SHARE + r
            qrot[g, r * T : (r + 1) * T] = turn(
                q[:, h * HD : (h + 1) * HD].astype(F32), cosine[...], sine[...]
            ).astype(BF16)
        total = jnp.zeros((T, HD), F32)
        for r in range(0, SHARE, 2):
            rows = slice(r * T, (r + 2) * T)
            scores = dot(qrot[g, rows], krot[g], NT) * SCALE
            row = lax.broadcasted_iota(jnp.int32, (2 * T, T), 0)
            row = jnp.where(row >= T, row - T, row)
            lane = lax.broadcasted_iota(jnp.int32, (2 * T, T), 1)
            scores = jnp.where(row >= lane, scores, -1e30)
            expo = jnp.exp(scores - jnp.max(scores, axis=-1, keepdims=True))
            p = expo / jnp.sum(expo, axis=-1, keepdims=True)
            probs[g, rows] = p
            h = g * SHARE + r
            d_out = jnp.concatenate(
                [og[:, h * HD : (h + 1) * HD], og[:, (h + 1) * HD : (h + 2) * HD]], axis=0
            )
            total = total + dot(p.astype(BF16), d_out, TN)
        vg2[0, :, g * HD : (g + 1) * HD] = total.astype(BF16)

    pair = pltpu.make_async_remote_copy(
        src_ref=normed.at[:, other], dst_ref=pnorm, send_sem=ps.at[0], recv_sem=pr.at[0],
        device_id=partner, device_id_type=MESH,
    )
    pair_vg = pltpu.make_async_remote_copy(
        src_ref=vg2.at[0], dst_ref=vg2.at[1], send_sem=ps.at[1], recv_sem=pr.at[1],
        device_id=partner, device_id_type=MESH,
    )

    def norm():
        pair_vg.start()
        for i in range(1, NS):
            counting(i).wait_recv()
        last = cbuf[0] - 1
        for i in range(1, NS):
            last = last + jnp.where(sec >= i, cbuf[i], 0)
        loads[3].wait()
        loads[4].wait()

        @pl.loop(0, 8)
        def _(i):
            cols = pl.ds(pl.multiple_of(i * 1024, 1024), 1024)
            rows = lax.broadcasted_iota(jnp.int32, (40, 1024), 0)
            table = gt[:, cols].astype(F32)
            same = rows == jnp.broadcast_to(last[0:1, 0:1], (40, 1024))
            gain[:, cols] = jnp.sum(jnp.where(same, table, 0.0), axis=0, keepdims=True)

        def squares(i, acc):
            x = hid[:, pl.ds(pl.multiple_of(i * SH, SH), SH)].astype(F32)
            return acc + x * x

        acc = lax.fori_loop(0, 32, squares, jnp.zeros((T, SH), F32))
        inverse = lax.rsqrt(jnp.sum(acc, axis=-1, keepdims=True) * (1.0 / D) + 1e-05)
        col[0] = jnp.broadcast_to(inverse, (T, 128))

        @pl.loop(0, 16)
        def _(i):
            for c in range(2):
                cols = pl.ds(pl.multiple_of(i * 512 + c * SH, SH), SH)
                x = hid[:, cols].astype(F32)
                inv = jnp.concatenate([col[0]] * 2, axis=1)
                normed[i, c] = (x * inv * gain[:, cols]).astype(BF16)

        pair.start()
        vals[...] = jnp.zeros((T, E), F32)
        loads[5].wait()

    def weight_part(p):
        left = jnp.concatenate([normed[p, core], pnorm[p]], axis=0)
        right = jnp.concatenate([vg2[0], vg2[1]], axis=0)
        stg[p] = dot(left, right, TN).astype(BF16)

    def weight_parts(yo):
        if not paired:
            paired.append(True)
            pair.wait_recv()
            pair_vg.wait_recv()

        @pl.loop(0, 4)
        def _(i):
            weight_part(lax.rem(y + yo, 4) * 4 + i)

    paired = []

    def rows_of(c, half):
        return pl.ds(SUMS[c][2] + half * (SUMS[c][3] // 2), SUMS[c][3] // 2)

    def part(c, fo, so, half):
        return stg.at[place(SUMS[c][0], fo, so), rows_of(c, half)]

    def free_sends(c, oi):
        so = RS_OFFS[oi]
        up1, down1 = near(SUMS[c][0], 1), near(SUMS[c][0], -1)
        for side, there in ((0, up1), (1, down1)):
            send(part(c, 2, so, side), rl.at[oi, side, rows_of(c, side)], rrl.at[c, oi, side], there)
        for side, fo, there in ((0, 1, up1), (1, 3, down1)):
            rows = rows_of(c, 1 - side)
            send(
                part(c, fo, so, 1 - side), fin.at[oi, side, rows], rfin.at[c, oi, side, 1 - side],
                there,
            )

    def relay(c, oi):
        for side, (fo, step) in enumerate(((1, 1), (3, -1))):
            rows = rows_of(c, side)
            arrived(rl.at[oi, side, rows], rrl.at[c, oi, side])
            p = place(SUMS[c][0], fo, RS_OFFS[oi])
            stg[p, rows] = (stg[p, rows].astype(F32) + rl[oi, side, rows].astype(F32)).astype(BF16)
            send(
                stg.at[p, rows], fin.at[oi, side, rows], rfin.at[c, oi, side, side],
                near(SUMS[c][0], step),
            )

    def finish(c, oi):
        so = RS_OFFS[oi]
        for side in range(2):
            for half in range(2):
                arrived(fin.at[oi, side, rows_of(c, half)], rfin.at[c, oi, side, half])
        p = place(SUMS[c][0], 0, so)
        rows = pl.ds(SUMS[c][2], SUMS[c][3])
        total = stg[p, rows].astype(F32)
        total = total + fin[oi, 0, rows].astype(F32) + fin[oi, 1, rows].astype(F32)
        if so == 0:
            wacc[rows] = total
            return
        stg[p, rows] = total.astype(BF16)
        up1, down1 = near(SUMS[c][1], 1), near(SUMS[c][1], -1)
        if so == 2:
            for side, there in ((0, up1), (1, down1)):
                send(part(c, 0, 2, side), rl2.at[side, rows_of(c, side)], rrl2.at[c, side], there)
        elif so == 1:
            send(part(c, 0, 1, 1), fin2.at[0, rows_of(c, 1)], rfin2.at[c, 0, 1], up1)
        else:
            send(part(c, 0, 3, 0), fin2.at[1, rows_of(c, 0)], rfin2.at[c, 1, 0], down1)

    def relay2(c, side):
        so, step = ((1, 1), (3, -1))[side]
        rows = rows_of(c, side)
        arrived(rl2.at[side, rows], rrl2.at[c, side])
        p = place(SUMS[c][0], 0, so)
        stg[p, rows] = (stg[p, rows].astype(F32) + rl2[side, rows].astype(F32)).astype(BF16)
        send(
            stg.at[p, rows], fin2.at[side, rows], rfin2.at[c, side, side], near(SUMS[c][1], step)
        )

    def finish2(c):
        for side in range(2):
            for half in range(2):
                arrived(fin2.at[side, rows_of(c, half)], rfin2.at[c, side, half])
        rows = pl.ds(SUMS[c][2], SUMS[c][3])
        total = wacc[rows] + fin2[0, rows].astype(F32) + fin2[1, rows].astype(F32)
        wgo[rows] = total.astype(BF16)

    def late_terms():
        inverse = col[0][:, 0:1]
        mean = jnp.sum(vg2[0].astype(F32) * vals[...], axis=-1, keepdims=True) * (1.0 / D)
        col[1] = jnp.broadcast_to(inverse * inverse * mean, (T, 128))

        @pl.when(gives_early)
        def _():
            fixing().start()

            for yo, zo in LATE:
                p = spot(yo, zo)
                whole_term(p)
                passing(p).start()

        @pl.when(sec == 4)
        def _():
            for n in range(16):
                p = spot(n // 4, n % 4)
                whole_term(p)
                slot = n // 2 + 4 * (n % 2) if n < 6 else (n - 6) // 2
                goal = 5 if n < 6 else 7 * (n % 2)
                pltpu.make_async_remote_copy(
                    src_ref=chunk(lg, p), dst_ref=rb.at[slot], send_sem=lss.at[p],
                    recv_sem=rbr.at[slot], device_id=(goal, dp), device_id_type=MESH,
                ).start()

        vlow[...] = vals[...].astype(BF16)

    HOPS = {
        0: [[(j, 3, 6 + 2 * j)] for j in range(5)],
        7: [[(j, 3, 7 + 2 * j)] for j in range(5)],
        5: [[(j, 1, None), (4 + j, 6, None)] for j in range(3)],
        1: [[(j, 2, None)] for j in range(3)],
        6: [[(4 + j, 2, None)] for j in range(3)],
        2: [[(j, 3, 2 * j), (4 + j, 3, 2 * j + 1)] for j in range(3)],
    }

    def handing(slot, goal, n):
        if n is None:
            dst, recv = rb.at[slot], rbr.at[slot]
        else:
            p = spot(n // 4, n % 4)
            dst, recv = chunk(up, p), lsr.at[p]
        return pltpu.make_async_remote_copy(
            src_ref=rb.at[slot], dst_ref=dst, send_sem=rbs.at[slot], recv_sem=recv,
            device_id=(goal, dp), device_id_type=MESH,
        )

    def hand_on(j, *sections):
        for one in sections:

            @pl.when(sec == one)
            def _():
                for hop in HOPS[one][j]:
                    arrived(rb.at[hop[0]], rbr.at[hop[0]])
                    handing(*hop).start()

    def attend_back(g):
        value = vlow[:, g * HD : (g + 1) * HD]
        total = jnp.zeros((T, HD), F32)
        for r in range(0, SHARE, 2):
            h = g * SHARE + r
            rows = slice(r * T, (r + 2) * T)
            d_out = jnp.concatenate(
                [og[:, h * HD : (h + 1) * HD], og[:, (h + 1) * HD : (h + 2) * HD]], axis=0
            )
            d_probs = dot(d_out, value, NT)
            p = probs[g, rows]
            low = p.astype(BF16).astype(F32)
            delta = jnp.sum(low * d_probs, axis=-1, keepdims=True)
            d_scores = (p * (d_probs - delta) * SCALE).astype(BF16)
            total = total + dot(d_scores, qrot[g, rows], TN)
            dq = dot(d_scores, krot[g])
            for i in range(2):
                one = turn(dq[i * T : (i + 1) * T], cosine[...], -sine[...])
                qgo[:, (h + i) * HD : (h + i + 1) * HD] = one.astype(BF16)
        kgo[:, g * HD : (g + 1) * HD] = turn(total, cosine[...], -sine[...]).astype(BF16)

    @pl.when(sec == NS - 1)
    def _():
        up[...] = jnp.zeros((T, D), BF16)

    steps = {
        "oF": first_own, "oS": lambda c: to_second(c, 0), "rF": first12, "sF": to_second,
        "f3": first3, "rS": second12, "s3": second3, "hid": hidden_ahead, "att": attend,
        "norm": norm, "wp": weight_parts, "mul": multiply, "le": leave_early, "lg": late_terms,
        "free": free_sends, "relay": relay, "fin": finish, "r2": relay2, "f2": finish2,
        "ab": attend_back, "hand": hand_on,
    }
    for step in ORDER:
        steps[step[0]](*step[1:])

    @pl.when(gets_early)
    def _():
        fixing().wait_recv()
        fix = jnp.concatenate([fixr[...]] * 4, axis=1)
        for i in range(len(EARLY)):
            p = spot(*EARLY[i])
            ahead(i).wait_recv()
            passing(p).wait_recv()
            cols = pl.ds(pl.multiple_of(p * 512, 512), 512)
            up[:, cols] = (up[:, cols].astype(F32) - hin[i].astype(F32) * fix).astype(BF16)

        for yo, zo in LATE:
            passing(spot(yo, zo)).wait_recv()

    @pl.when(sec == 3)
    def _():
        @pl.loop(0, 16)
        def _(i):
            passing(i).wait_recv()

    for one, hops in HOPS.items():

        @pl.when(sec == one)
        def _():
            for pair_of in hops:
                for hop in pair_of:
                    handing(*hop).wait_send()

    @pl.when(gives_early)
    def _():
        fixing().wait_send()
        for i in range(len(EARLY)):
            ahead(i).wait_send()

    @pl.when(sec > 0)
    def _():
        @pl.loop(0, 16)
        def _(i):
            passing(i).wait_send()

    for copy in sent:
        copy.wait_send()
    for i in range(1, NS):
        counting(i).wait_send()
    pair.wait_send()
    pair_vg.wait_send()


def store(*refs):
    copies = [
        pltpu.make_async_copy(refs[i], refs[4 + i].at[0], refs[8].at[i]) for i in (3, 0, 2, 1)
    ]
    for copy in copies:
        copy.start()
    for copy in copies:
        copy.wait()


def shards(hidden, gain_table, layer_counts, positions, queries, keys, value_weight, out_grad):
    anywhere = pl.BlockSpec(memory_space=pl.ANY)
    vmem = pl.BlockSpec(memory_space=pltpu.VMEM)
    smem = pl.BlockSpec(memory_space=pltpu.SMEM)
    dma = pltpu.SemaphoreType.DMA
    scratch = [
        pltpu.VMEM((T, D), BF16),
        pltpu.VMEM((40, D), BF16),
        pltpu.VMEM((T, HQ * HD), BF16),
        pltpu.VMEM((T, HK * HD), BF16),
        pltpu.VMEM((T, HQ * HD), BF16),
        pltpu.VMEM((16, 2, SH, E), BF16),
        pltpu.VMEM((16, 2, T, SH), BF16),
        pltpu.VMEM((16, T, SH), BF16),
        pltpu.VMEM((1, D), F32),
        pltpu.VMEM((HK, T, HD), BF16),
        pltpu.VMEM((HK, SHARE * T, HD), BF16),
        pltpu.VMEM((HK, SHARE * T, T), F32),
        pltpu.VMEM((2, T, E), BF16),
        pltpu.VMEM((T, E), F32),
        pltpu.VMEM((T, D), BF16),
        pltpu.VMEM((16, SH, E), BF16),
    ]
    scratch += [
        pltpu.VMEM((4, 2, SH, E), BF16),
        pltpu.VMEM((4, 2, SH, E), BF16),
        pltpu.VMEM((2, SH, E), BF16),
        pltpu.VMEM((2, SH, E), BF16),
        pltpu.VMEM((SH, E), F32),
        pltpu.VMEM((NS, 8, 128), jnp.int32),
        pltpu.VMEM((2, T, 128), F32),
        pltpu.VMEM((len(EARLY), T, 512), BF16),
        pltpu.VMEM((T, 128), F32),
        pltpu.VMEM((8, T, 512), BF16),
        pltpu.VMEM((T, E), BF16),
        pltpu.VMEM((T, HD), F32),
        pltpu.VMEM((T, HD), F32),
        dma((6,)),
        dma((136,)),
        dma((2, 4)),
        dma((2, 4, 4)),
        dma((2, 4, 4)),
        dma((7,)),
        dma((7,)),
        dma((2,)),
        dma((2,)),
        dma((16,)),
        dma((16,)),
        dma((2, 4, 2)),
        dma((2, 4, 2, 2)),
        dma((2, 2)),
        dma((2, 2, 2)),
        dma((len(EARLY),)),
        dma((len(EARLY),)),
        dma((2,)),
        dma((8,)),
        dma((8,)),
    ]
    query_grad, key_grad, weight_grad, upstream = pl.pallas_call(
        kernel,
        out_shape=(
            pltpu.VMEM((T, HQ * HD), BF16),
            pltpu.VMEM((T, HK * HD), BF16),
            pltpu.VMEM((SH, E), BF16),
            pltpu.VMEM((T, D), BF16),
        ),
        in_specs=[anywhere, anywhere, smem, vmem] + [anywhere] * 4,
        out_specs=(vmem,) * 4,
        scratch_shapes=scratch,
        compiler_params=pltpu.CompilerParams(
            collective_id=0, has_side_effects=True, vmem_limit_bytes=56 << 20
        ),
    )(
        hidden[0], gain_table, layer_counts, positions, queries[0], keys[0], value_weight[0],
        out_grad[0],
    )
    grads = (query_grad, key_grad, weight_grad, upstream)
    return pl.pallas_call(
        store,
        out_shape=tuple(jax.ShapeDtypeStruct((1, *one.shape), BF16) for one in grads),
        in_specs=[anywhere] * 4,
        out_specs=(anywhere,) * 4,
        scratch_shapes=[dma((4,))],
        compiler_params=pltpu.CompilerParams(vmem_limit_bytes=1 << 20),
    )(*grads)


def solution(mesh):
    rows = P("section", "dp", None)
    in_specs = (rows, P(), P("section"), P("section", "dp"), rows, rows, rows, rows)
    return jax.shard_map(
        shards, mesh=mesh, in_specs=in_specs, out_specs=(rows,) * 4, check_vma=False
    )
```

```python
import functools
import math

import jax
import jax.numpy as jnp
from jax import lax
from jax.experimental import pallas as pl
from jax.experimental.pallas import tpu as pltpu
from jax.sharding import PartitionSpec as P

HQ = 32
HK = 4
HD = 128
SHARE = HQ // HK
SCALE = HD ** (-0.5)
T = 128
D = 8192
E = HK * HD
SH = 256
NS = 8
MESH = pl.DeviceIdType.MESH
F32 = jnp.float32
BF16 = jnp.bfloat16

COLOURS = (("z", "y", 0, 384), ("y", "z", 384, 128))
SUMS = (("y", "z", 0, 224), ("z", "y", 224, 32))
OFFS = (0, 3, 1, 2)
INDEX = {0: 0, 3: 1, 1: 2, 2: 3}
EARLY = ((0, 0), (1, 0), (3, 0), (0, 1), (0, 3), (2, 0), (0, 2))
LATE = tuple((i, j) for i in range(4) for j in range(4) if (i, j) not in EARLY)
ORDER = (
    ("oF", 0), ("oF", 1), ("oS", 0), ("hid",), ("att", 3), ("att", 0), ("att", 1), ("att", 2),
    ("rF", 1, 2), ("rF", 1, 1), ("norm",), ("rS", 0, 0), ("oS", 1), ("rF", 0, 1), ("sF", 0, 1),
    ("mul", 0, 0), ("le", 0), ("rF", 0, 2), ("rS", 1, 0), ("sF", 1, 2), ("sF", 0, 2), ("mul", 0, 1),
    ("le", 3), ("rS", 0, 1), ("sF", 1, 1), ("mul", 0, 3), ("le", 4), ("f3", 0), ("s3", 1, 0),
    ("s3", 0, 0), ("mul", 3, 0), ("le", 2), ("rS", 1, 2), ("s3", 0, 1), ("wp", 2), ("f3", 1),
    ("wp", 0), ("rS", 0, 2), ("wp", 1), ("rS", 1, 1), ("wp", 3), ("s3", 1, 2), ("rS", 0, 3),
    ("s3", 0, 2), ("rS", 1, 3), ("mul", 3, 1), ("mul", 1, 1), ("mul", 1, 0), ("le", 1),
    ("s3", 1, 1), ("mul", 2, 0), ("le", 5), ("free", 0, 0), ("free", 1, 0), ("s3", 0, 3),
    ("free", 0, 1), ("free", 1, 1), ("s3", 1, 3), ("mul", 3, 3), ("free", 0, 2), ("free", 1, 2),
    ("mul", 1, 3), ("mul", 0, 2), ("le", 6), ("mul", 3, 2), ("mul", 2, 1), ("mul", 2, 3),
    ("mul", 1, 2), ("mul", 2, 2), ("lg",), ("relay", 0, 0), ("relay", 1, 0), ("four", 8, 12),
    ("ab", 0), ("four", 12, 16), ("hand", 0, 5), ("free", 0, 3), ("free", 1, 3), ("relay", 0, 1),
    ("relay", 1, 1), ("hand", 0, 0, 7), ("ab", 1), ("hand", 1, 0, 7), ("fin", 0, 0), ("fin", 1, 0),
    ("hand", 0, 1, 6), ("relay", 0, 2), ("relay", 1, 2), ("hand", 1, 5), ("hand", 2, 0, 7),
    ("ab", 2), ("hand", 0, 2), ("fin", 0, 1), ("fin", 1, 1), ("hand", 1, 1, 6), ("hand", 3, 0, 7),
    ("r2", 0, 0), ("r2", 1, 0), ("hand", 2, 5), ("hand", 4, 0, 7), ("relay", 0, 3), ("relay", 1, 3),
    ("hand", 1, 2), ("ab", 3), ("close",), ("mean",), ("hand", 2, 1, 6), ("fin", 0, 2),
    ("fin", 1, 2), ("r2", 0, 1), ("r2", 1, 1), ("hand", 2, 2), ("fin", 0, 3), ("fin", 1, 3),
    ("f2", 0), ("f2", 1),
)
RS_OFFS = (2, 1, 3, 0)
NT = (((1,), (1,)), ((), ()))
TN = (((0,), (0,)), ((), ()))


def dot(a, b, dims=(((1,), (0,)), ((), ()))):
    return lax.dot_general(a, b, dims, preferred_element_type=F32)


def turn(x, cosine, sine):
    return x * cosine + pltpu.roll(x, HD // 2, 1) * sine


def kernel(
    hid_hbm, gt_hbm, cnt_ref, pos_ref, q_hbm, k_hbm, w_hbm, og_hbm,
    qgo, kgo, wgo, up,
    hid, gt, q, k, og, wf, normed, pnorm, gain, krot, qrot, probs, vg2, vals, lg, stg,
    rl, fin, rl2, fin2, wacc, cbuf, col, hin, fixr, rb, vlow, cosine, sine,
    loc, ssem, rf, rs, rp, cs, cr, ps, pr, lss, lsr, rrl, rfin, rrl2, rfin2, hs, hr, fx, rbs, rbr,
):
    sec = lax.axis_index("section")
    dp = lax.axis_index("dp")
    core = lax.rem(dp, 2)
    y = dp // 8
    z = lax.rem(dp // 2, 4)
    other = 1 - core

    def at(yy, zz, cc):
        return (sec, (yy * 4 + zz) * 2 + cc)

    def near(axis, step):
        if axis == "y":
            return at(lax.rem(y + step + 4, 4), z, core)
        return at(y, lax.rem(z + step + 4, 4), core)

    partner = at(y, z, other)

    def spot(yo, zo):
        return lax.rem(y + yo, 4) * 4 + lax.rem(z + zo, 4)

    def place(first, fo, so):
        return spot(fo, so) if first == "y" else spot(so, fo)

    gives_early = jnp.logical_and(sec != 0, sec != 4)
    gets_early = jnp.logical_and(sec != NS - 1, sec != 3)
    below = lax.rem(sec + NS - 1, NS)

    here = y * 4 + z

    loads = [
        pltpu.make_async_copy(k_hbm, k, loc.at[0]),
        pltpu.make_async_copy(q_hbm, q, loc.at[1]),
        pltpu.make_async_copy(og_hbm, og, loc.at[2]),
        pltpu.make_async_copy(hid_hbm, hid, loc.at[3]),
        pltpu.make_async_copy(gt_hbm, gt, loc.at[4]),
        pltpu.make_async_copy(w_hbm, wf.at[here, core], loc.at[5]),
    ]
    loads[0].start()
    loads[1].start()
    loads[2].start()
    cbuf[0] = jnp.full((8, 128), cnt_ref[0], jnp.int32)

    barrier = pltpu.get_barrier_semaphore()
    ids = [near("y", 1), near("y", -1), near("z", 1), near("z", -1), partner]
    ids += [(lax.rem(sec + i, NS), dp) for i in range(1, NS)]
    for one in ids:
        pl.semaphore_signal(barrier, inc=1, device_id=one, device_id_type=MESH)
    pl.semaphore_wait(barrier, len(ids))

    sent = []

    def send(src, dst, recv, device):
        copy = pltpu.make_async_remote_copy(
            src_ref=src, dst_ref=dst, send_sem=ssem.at[len(sent)], recv_sem=recv,
            device_id=device, device_id_type=MESH,
        )
        sent.append(copy)
        copy.start()

    def arrived(dst, recv):
        pltpu.make_async_remote_copy(
            src_ref=dst, dst_ref=dst, send_sem=ssem.at[0], recv_sem=recv,
            device_id=partner, device_id_type=MESH,
        ).wait_recv()

    HALF = (pl.ds(0, 128), pl.ds(128, 128))
    FULL = pl.ds(0, SH)

    def piece(c, fo, so, rows):
        first, _, c0, cw = COLOURS[c]
        return wf.at[place(first, fo, so), core, rows, pl.ds(c0, cw)]

    def to_second(c, fi):
        first, second, c0, cw = COLOURS[c]
        src = w_hbm.at[:, pl.ds(c0, cw)] if fi == 0 else piece(c, OFFS[fi], 0, FULL)
        dst = piece(c, OFFS[fi], 0, FULL)
        send(src, dst, rs.at[c, fi, 0], near(second, 1))
        send(src, dst, rs.at[c, fi, 1], near(second, -1))

    def to_partner(c, fi, si):
        first, second, c0, cw = COLOURS[c]
        dst = piece(c, OFFS[fi], OFFS[si], FULL)
        src = w_hbm.at[:, pl.ds(c0, cw)] if fi == 0 and si == 0 else dst
        send(src, dst, rp.at[c, fi, si], partner)

    def first_own(c):
        _, _, c0, cw = COLOURS[c]
        first, src, dst = COLOURS[c][0], w_hbm.at[:, pl.ds(c0, cw)], piece(c, 0, 0, FULL)
        send(src, dst, rf.at[c, 0], near(first, 1))
        send(src, dst, rf.at[c, 1], near(first, -1))
        to_partner(c, 0, 0)

    def first12(c, fi):
        step, half = ((1, 0), (-1, 1))[fi - 1]
        arrived(piece(c, OFFS[fi], 0, FULL), rf.at[c, fi - 1])
        part = piece(c, OFFS[fi], 0, HALF[half])
        send(part, part, rf.at[c, 2 + half], near(COLOURS[c][0], step))
        to_partner(c, fi, 0)

    def first3(c):
        for half in (0, 1):
            arrived(piece(c, 2, 0, HALF[half]), rf.at[c, 2 + half])
        to_second(c, 3)
        to_partner(c, 3, 0)

    def second12(c, fi):
        second = COLOURS[c][1]
        for si, (step, half) in ((1, (1, 0)), (2, (-1, 1))):
            arrived(piece(c, OFFS[fi], OFFS[si], FULL), rs.at[c, fi, si - 1])
            part = piece(c, OFFS[fi], OFFS[si], HALF[half])
            send(part, part, rs.at[c, fi, 2 + half], near(second, step))
            to_partner(c, fi, si)

    def second3(c, fi):
        for half in (0, 1):
            arrived(piece(c, OFFS[fi], 2, HALF[half]), rs.at[c, fi, 2 + half])
        to_partner(c, fi, 3)

    def from_partner(c, fi, si):
        first, _, c0, cw = COLOURS[c]
        arrived(
            wf.at[place(first, OFFS[fi], OFFS[si]), other, FULL, pl.ds(c0, cw)], rp.at[c, fi, si]
        )

    def multiply(yo, zo):
        from_partner(0, INDEX[zo], INDEX[yo])
        from_partner(1, INDEX[yo], INDEX[zo])
        p = spot(yo, zo)
        vals[...] += dot(normed[p, 0], wf[p, 0]) + dot(normed[p, 1], wf[p, 1])

    def chunk(ref, i):
        return ref.at[:, pl.ds(pl.multiple_of(i * 512, 512), 512)]

    def ahead(i):
        p = spot(*EARLY[i])
        return pltpu.make_async_remote_copy(
            src_ref=chunk(hid_hbm, p), dst_ref=hin.at[i], send_sem=hs.at[i], recv_sem=hr.at[i],
            device_id=(below, dp), device_id_type=MESH,
        )

    def passing(i):
        return pltpu.make_async_remote_copy(
            src_ref=chunk(lg, i), dst_ref=chunk(up, i), send_sem=lss.at[i], recv_sem=lsr.at[i],
            device_id=(below, dp), device_id_type=MESH,
        )

    def first_term(p):
        cols = pl.ds(pl.multiple_of(p * 512, 512), 512)
        d_normed = dot(vg2[0], wf[p].reshape(512, E), NT)
        inv = jnp.concatenate([col[0]] * 4, axis=1)
        return cols, inv * (gain[:, cols] * d_normed)

    def leave_early(i):
        p = spot(*EARLY[i])

        @pl.when(gives_early)
        def _():
            cols, term = first_term(p)
            lg[:, cols] = term.astype(BF16)
            passing(p).start()

    def fixing():
        return pltpu.make_async_remote_copy(
            src_ref=col.at[1], dst_ref=fixr, send_sem=fx.at[0], recv_sem=fx.at[1],
            device_id=(below, dp), device_id_type=MESH,
        )

    def whole_term(p):
        cols, term = first_term(p)
        fix = jnp.concatenate([col[1]] * 4, axis=1)
        lg[:, cols] = (term - hid[:, cols].astype(F32) * fix).astype(BF16)

    def counting(i):
        return pltpu.make_async_remote_copy(
            src_ref=cbuf.at[0], dst_ref=cbuf.at[i], send_sem=cs.at[i - 1], recv_sem=cr.at[i - 1],
            device_id=(lax.rem(sec + i, NS), dp), device_id_type=MESH,
        )

    def hidden_ahead():
        for i in range(1, NS):
            counting(i).start()
        for load in loads[3:]:
            load.start()

        @pl.when(gives_early)
        def _():
            for i in range(len(EARLY)):
                ahead(i).start()

        places = jnp.broadcast_to(pos_ref[...].astype(F32), (T, HD)).T
        lane = lax.broadcasted_iota(jnp.int32, (T, HD), 1)
        entry = jnp.where(lane < HD // 2, lane, lane - HD // 2).astype(F32)
        angle = places * jnp.exp(entry * (-2.0 * math.log(500000.0) / HD))
        cosine[...] = jnp.cos(angle)
        sine[...] = jnp.where(lane < HD // 2, -1.0, 1.0) * jnp.sin(angle)
        for load in loads[:3]:
            load.wait()
        for g in range(HK):
            k_g = k[:, g * HD : (g + 1) * HD].astype(F32)
            krot[g] = turn(k_g, cosine[...], sine[...]).astype(BF16)

    def attend(g):
        for r in range(SHARE):
            h = g * SHARE + r
            qrot[g, r * T : (r + 1) * T] = turn(
                q[:, h * HD : (h + 1) * HD].astype(F32), cosine[...], sine[...]
            ).astype(BF16)
        total = jnp.zeros((T, HD), F32)
        for r in range(0, SHARE, 2):
            rows = slice(r * T, (r + 2) * T)
            scores = dot(qrot[g, rows], krot[g], NT) * SCALE
            row = lax.broadcasted_iota(jnp.int32, (2 * T, T), 0)
            row = jnp.where(row >= T, row - T, row)
            lane = lax.broadcasted_iota(jnp.int32, (2 * T, T), 1)
            scores = jnp.where(row >= lane, scores, -1e30)
            expo = jnp.exp(scores - jnp.max(scores, axis=-1, keepdims=True))
            p = expo / jnp.sum(expo, axis=-1, keepdims=True)
            probs[g, rows] = p
            h = g * SHARE + r
            d_out = jnp.concatenate(
                [og[:, h * HD : (h + 1) * HD], og[:, (h + 1) * HD : (h + 2) * HD]], axis=0
            )
            total = total + dot(p.astype(BF16), d_out, TN)
        vg2[0, :, g * HD : (g + 1) * HD] = total.astype(BF16)

    pair = pltpu.make_async_remote_copy(
        src_ref=normed.at[:, other], dst_ref=pnorm, send_sem=ps.at[0], recv_sem=pr.at[0],
        device_id=partner, device_id_type=MESH,
    )
    pair_vg = pltpu.make_async_remote_copy(
        src_ref=vg2.at[0], dst_ref=vg2.at[1], send_sem=ps.at[1], recv_sem=pr.at[1],
        device_id=partner, device_id_type=MESH,
    )

    def norm():
        pair_vg.start()
        for i in range(1, NS):
            counting(i).wait_recv()
        last = cbuf[0] - 1
        for i in range(1, NS):
            last = last + jnp.where(sec >= i, cbuf[i], 0)
        loads[3].wait()
        loads[4].wait()

        @pl.loop(0, 8)
        def _(i):
            cols = pl.ds(pl.multiple_of(i * 1024, 1024), 1024)
            rows = lax.broadcasted_iota(jnp.int32, (40, 1024), 0)
            table = gt[:, cols].astype(F32)
            same = rows == jnp.broadcast_to(last[0:1, 0:1], (40, 1024))
            gain[:, cols] = jnp.sum(jnp.where(same, table, 0.0), axis=0, keepdims=True)

        def squares(i, acc):
            x = hid[:, pl.ds(pl.multiple_of(i * SH, SH), SH)].astype(F32)
            return acc + x * x

        acc = lax.fori_loop(0, 32, squares, jnp.zeros((T, SH), F32))
        inverse = lax.rsqrt(jnp.sum(acc, axis=-1, keepdims=True) * (1.0 / D) + 1e-05)
        col[0] = jnp.broadcast_to(inverse, (T, 128))

        @pl.loop(0, 16)
        def _(i):
            for c in range(2):
                cols = pl.ds(pl.multiple_of(i * 512 + c * SH, SH), SH)
                x = hid[:, cols].astype(F32)
                inv = jnp.concatenate([col[0]] * 2, axis=1)
                normed[i, c] = (x * inv * gain[:, cols]).astype(BF16)

        pair.start()
        vals[...] = jnp.zeros((T, E), F32)
        loads[5].wait()

    def weight_part(p):
        left = jnp.concatenate([normed[p, core], pnorm[p]], axis=0)
        right = jnp.concatenate([vg2[0], vg2[1]], axis=0)
        stg[p] = dot(left, right, TN).astype(BF16)

    def weight_parts(yo):
        if not paired:
            paired.append(True)
            pair.wait_recv()
            pair_vg.wait_recv()

        @pl.loop(0, 4)
        def _(i):
            weight_part(lax.rem(y + yo, 4) * 4 + i)

    paired = []

    def rows_of(c, half):
        return pl.ds(SUMS[c][2] + half * (SUMS[c][3] // 2), SUMS[c][3] // 2)

    def part(c, fo, so, half):
        return stg.at[place(SUMS[c][0], fo, so), rows_of(c, half)]

    def free_sends(c, oi):
        so = RS_OFFS[oi]
        up1, down1 = near(SUMS[c][0], 1), near(SUMS[c][0], -1)
        for side, there in ((0, up1), (1, down1)):
            send(part(c, 2, so, side), rl.at[oi, side, rows_of(c, side)], rrl.at[c, oi, side], there)
        for side, fo, there in ((0, 1, up1), (1, 3, down1)):
            rows = rows_of(c, 1 - side)
            send(
                part(c, fo, so, 1 - side), fin.at[oi, side, rows], rfin.at[c, oi, side, 1 - side],
                there,
            )

    def relay(c, oi):
        for side, (fo, step) in enumerate(((1, 1), (3, -1))):
            rows = rows_of(c, side)
            arrived(rl.at[oi, side, rows], rrl.at[c, oi, side])
            p = place(SUMS[c][0], fo, RS_OFFS[oi])
            stg[p, rows] = (stg[p, rows].astype(F32) + rl[oi, side, rows].astype(F32)).astype(BF16)
            send(
                stg.at[p, rows], fin.at[oi, side, rows], rfin.at[c, oi, side, side],
                near(SUMS[c][0], step),
            )

    def finish(c, oi):
        so = RS_OFFS[oi]
        for side in range(2):
            for half in range(2):
                arrived(fin.at[oi, side, rows_of(c, half)], rfin.at[c, oi, side, half])
        p = place(SUMS[c][0], 0, so)
        rows = pl.ds(SUMS[c][2], SUMS[c][3])
        total = stg[p, rows].astype(F32)
        total = total + fin[oi, 0, rows].astype(F32) + fin[oi, 1, rows].astype(F32)
        if so == 0:
            wacc[rows] = total
            return
        stg[p, rows] = total.astype(BF16)
        up1, down1 = near(SUMS[c][1], 1), near(SUMS[c][1], -1)
        if so == 2:
            for side, there in ((0, up1), (1, down1)):
                send(part(c, 0, 2, side), rl2.at[side, rows_of(c, side)], rrl2.at[c, side], there)
        elif so == 1:
            send(part(c, 0, 1, 1), fin2.at[0, rows_of(c, 1)], rfin2.at[c, 0, 1], up1)
        else:
            send(part(c, 0, 3, 0), fin2.at[1, rows_of(c, 0)], rfin2.at[c, 1, 0], down1)

    def relay2(c, side):
        so, step = ((1, 1), (3, -1))[side]
        rows = rows_of(c, side)
        arrived(rl2.at[side, rows], rrl2.at[c, side])
        p = place(SUMS[c][0], 0, so)
        stg[p, rows] = (stg[p, rows].astype(F32) + rl2[side, rows].astype(F32)).astype(BF16)
        send(
            stg.at[p, rows], fin2.at[side, rows], rfin2.at[c, side, side], near(SUMS[c][1], step)
        )

    def finish2(c):
        for side in range(2):
            for half in range(2):
                arrived(fin2.at[side, rows_of(c, half)], rfin2.at[c, side, half])
        rows = pl.ds(SUMS[c][2], SUMS[c][3])
        total = wacc[rows] + fin2[0, rows].astype(F32) + fin2[1, rows].astype(F32)
        wgo[rows] = total.astype(BF16)

    def from_four(start, stop):
        @pl.when(sec == 4)
        def _():
            for n in range(start, stop):
                p = spot(n // 4, n % 4)
                whole_term(p)
                slot = n // 2 + 4 * (n % 2) if n < 6 else (n - 6) // 2
                goal = 5 if n < 6 else 7 * (n % 2)
                pltpu.make_async_remote_copy(
                    src_ref=chunk(lg, p), dst_ref=rb.at[slot], send_sem=lss.at[p],
                    recv_sem=rbr.at[slot], device_id=(goal, dp), device_id_type=MESH,
                ).start()

    def late_terms():
        early_sends.extend(sent)
        inverse = col[0][:, 0:1]
        mean = jnp.sum(vg2[0].astype(F32) * vals[...], axis=-1, keepdims=True) * (1.0 / D)
        col[1] = jnp.broadcast_to(inverse * inverse * mean, (T, 128))

        @pl.when(gives_early)
        def _():
            fixing().start()

            for yo, zo in LATE:
                p = spot(yo, zo)
                whole_term(p)
                passing(p).start()

        from_four(0, 8)
        vlow[...] = vals[...].astype(BF16)

    HOPS = {
        0: [[(j, 3, 6 + 2 * j)] for j in range(5)],
        7: [[(j, 3, 7 + 2 * j)] for j in range(5)],
        5: [[(j, 1, None), (4 + j, 6, None)] for j in range(3)],
        1: [[(j, 2, None)] for j in range(3)],
        6: [[(4 + j, 2, None)] for j in range(3)],
        2: [[(j, 3, 2 * j), (4 + j, 3, 2 * j + 1)] for j in range(3)],
    }

    def handing(slot, goal, n):
        if n is None:
            dst, recv = rb.at[slot], rbr.at[slot]
        else:
            p = spot(n // 4, n % 4)
            dst, recv = chunk(up, p), lsr.at[p]
        return pltpu.make_async_remote_copy(
            src_ref=rb.at[slot], dst_ref=dst, send_sem=rbs.at[slot], recv_sem=recv,
            device_id=(goal, dp), device_id_type=MESH,
        )

    def hand_on(j, *sections):
        for one in sections:

            @pl.when(sec == one)
            def _():
                for hop in HOPS[one][j]:
                    arrived(rb.at[hop[0]], rbr.at[hop[0]])
                    handing(*hop).start()

    def attend_back(g):
        value = vlow[:, g * HD : (g + 1) * HD]
        total = jnp.zeros((T, HD), F32)
        for r in range(0, SHARE, 2):
            h = g * SHARE + r
            rows = slice(r * T, (r + 2) * T)
            d_out = jnp.concatenate(
                [og[:, h * HD : (h + 1) * HD], og[:, (h + 1) * HD : (h + 2) * HD]], axis=0
            )
            d_probs = dot(d_out, value, NT)
            p = probs[g, rows]
            low = p.astype(BF16).astype(F32)
            delta = jnp.sum(low * d_probs, axis=-1, keepdims=True)
            d_scores = (p * (d_probs - delta) * SCALE).astype(BF16)
            total = total + dot(d_scores, qrot[g, rows], TN)
            dq = dot(d_scores, krot[g])
            for i in range(2):
                one = turn(dq[i * T : (i + 1) * T], cosine[...], -sine[...])
                qgo[:, (h + i) * HD : (h + i + 1) * HD] = one.astype(BF16)
        kgo[:, g * HD : (g + 1) * HD] = turn(total, cosine[...], -sine[...]).astype(BF16)

    def take_off_mean():
        @pl.when(gets_early)
        def _():
            fixing().wait_recv()
            fix = jnp.concatenate([fixr[...]] * 4, axis=1)
            for i in range(len(EARLY)):
                p = spot(*EARLY[i])
                ahead(i).wait_recv()
                passing(p).wait_recv()
                cols = pl.ds(pl.multiple_of(p * 512, 512), 512)
                up[:, cols] = (up[:, cols].astype(F32) - hin[i].astype(F32) * fix).astype(BF16)

    early_sends = []

    def close_first_phase():
        for copy in early_sends:
            copy.wait_send()
        for i in range(1, NS):
            counting(i).wait_send()
        pair.wait_send()
        pair_vg.wait_send()

        @pl.when(sec == NS - 1)
        def _():
            up[...] = jnp.zeros((T, D), BF16)

        @pl.when(gives_early)
        def _():
            fixing().wait_send()
            for i in range(len(EARLY)):
                ahead(i).wait_send()

    steps = {
        "four": from_four, "mean": take_off_mean, "close": close_first_phase,
        "oF": first_own, "oS": lambda c: to_second(c, 0), "rF": first12, "sF": to_second,
        "f3": first3, "rS": second12, "s3": second3, "hid": hidden_ahead, "att": attend,
        "norm": norm, "wp": weight_parts, "mul": multiply, "le": leave_early, "lg": late_terms,
        "free": free_sends, "relay": relay, "fin": finish, "r2": relay2, "f2": finish2,
        "ab": attend_back, "hand": hand_on,
    }
    for step in ORDER:
        steps[step[0]](*step[1:])

    @pl.when(gets_early)
    def _():
        for yo, zo in LATE:
            passing(spot(yo, zo)).wait_recv()

    @pl.when(sec == 3)
    def _():
        @pl.loop(0, 16)
        def _(i):
            passing(i).wait_recv()

    for one, hops in HOPS.items():

        @pl.when(sec == one)
        def _():
            for pair_of in hops:
                for hop in pair_of:
                    handing(*hop).wait_send()

    @pl.when(sec > 0)
    def _():
        @pl.loop(0, 16)
        def _(i):
            passing(i).wait_send()

    for copy in sent[len(early_sends) :]:
        copy.wait_send()


def store(*refs):
    copies = [
        pltpu.make_async_copy(refs[i], refs[4 + i].at[0], refs[8].at[i]) for i in (3, 0, 2, 1)
    ]
    for copy in copies:
        copy.start()
    for copy in copies:
        copy.wait()


def shards(hidden, gain_table, layer_counts, positions, queries, keys, value_weight, out_grad):
    anywhere = pl.BlockSpec(memory_space=pl.ANY)
    vmem = pl.BlockSpec(memory_space=pltpu.VMEM)
    smem = pl.BlockSpec(memory_space=pltpu.SMEM)
    dma = pltpu.SemaphoreType.DMA
    scratch = [
        pltpu.VMEM((T, D), BF16),
        pltpu.VMEM((40, D), BF16),
        pltpu.VMEM((T, HQ * HD), BF16),
        pltpu.VMEM((T, HK * HD), BF16),
        pltpu.VMEM((T, HQ * HD), BF16),
        pltpu.VMEM((16, 2, SH, E), BF16),
        pltpu.VMEM((16, 2, T, SH), BF16),
        pltpu.VMEM((16, T, SH), BF16),
        pltpu.VMEM((1, D), F32),
        pltpu.VMEM((HK, T, HD), BF16),
        pltpu.VMEM((HK, SHARE * T, HD), BF16),
        pltpu.VMEM((HK, SHARE * T, T), F32),
        pltpu.VMEM((2, T, E), BF16),
        pltpu.VMEM((T, E), F32),
        pltpu.VMEM((T, D), BF16),
        pltpu.VMEM((16, SH, E), BF16),
    ]
    scratch += [
        pltpu.VMEM((4, 2, SH, E), BF16),
        pltpu.VMEM((4, 2, SH, E), BF16),
        pltpu.VMEM((2, SH, E), BF16),
        pltpu.VMEM((2, SH, E), BF16),
        pltpu.VMEM((SH, E), F32),
        pltpu.VMEM((NS, 8, 128), jnp.int32),
        pltpu.VMEM((2, T, 128), F32),
        pltpu.VMEM((len(EARLY), T, 512), BF16),
        pltpu.VMEM((T, 128), F32),
        pltpu.VMEM((8, T, 512), BF16),
        pltpu.VMEM((T, E), BF16),
        pltpu.VMEM((T, HD), F32),
        pltpu.VMEM((T, HD), F32),
        dma((6,)),
        dma((136,)),
        dma((2, 4)),
        dma((2, 4, 4)),
        dma((2, 4, 4)),
        dma((7,)),
        dma((7,)),
        dma((2,)),
        dma((2,)),
        dma((16,)),
        dma((16,)),
        dma((2, 4, 2)),
        dma((2, 4, 2, 2)),
        dma((2, 2)),
        dma((2, 2, 2)),
        dma((len(EARLY),)),
        dma((len(EARLY),)),
        dma((2,)),
        dma((8,)),
        dma((8,)),
    ]
    query_grad, key_grad, weight_grad, upstream = pl.pallas_call(
        kernel,
        out_shape=(
            pltpu.VMEM((T, HQ * HD), BF16),
            pltpu.VMEM((T, HK * HD), BF16),
            pltpu.VMEM((SH, E), BF16),
            pltpu.VMEM((T, D), BF16),
        ),
        in_specs=[anywhere, anywhere, smem, vmem] + [anywhere] * 4,
        out_specs=(vmem,) * 4,
        scratch_shapes=scratch,
        compiler_params=pltpu.CompilerParams(
            collective_id=0, has_side_effects=True, vmem_limit_bytes=56 << 20
        ),
    )(
        hidden[0], gain_table, layer_counts, positions, queries[0], keys[0], value_weight[0],
        out_grad[0],
    )
    grads = (query_grad, key_grad, weight_grad, upstream)
    return pl.pallas_call(
        store,
        out_shape=tuple(jax.ShapeDtypeStruct((1, *one.shape), BF16) for one in grads),
        in_specs=[anywhere] * 4,
        out_specs=(anywhere,) * 4,
        scratch_shapes=[dma((4,))],
        compiler_params=pltpu.CompilerParams(vmem_limit_bytes=1 << 20),
    )(*grads)


def solution(mesh):
    rows = P("section", "dp", None)
    in_specs = (rows, P(), P("section"), P("section", "dp"), rows, rows, rows, rows)
    return jax.shard_map(
        shards, mesh=mesh, in_specs=in_specs, out_specs=(rows,) * 4, check_vma=False
    )
```

```python
import functools
import math

import jax
import jax.numpy as jnp
from jax import lax
from jax.experimental import pallas as pl
from jax.experimental.pallas import tpu as pltpu
from jax.sharding import PartitionSpec as P

HQ = 32
HK = 4
HD = 128
SHARE = HQ // HK
SCALE = HD ** (-0.5)
T = 128
D = 8192
E = HK * HD
SH = 256
NS = 8
MESH = pl.DeviceIdType.MESH
F32 = jnp.float32
BF16 = jnp.bfloat16

COLOURS = (("z", "y", 0, 384), ("y", "z", 384, 128))
SUMS = (("y", "z", 0, 224), ("z", "y", 224, 32))
OFFS = (0, 3, 1, 2)
INDEX = {0: 0, 3: 1, 1: 2, 2: 3}
EARLY = ((0, 0), (1, 0), (3, 0), (0, 1), (0, 3), (2, 0), (0, 2))
LATE = tuple((i, j) for i in range(4) for j in range(4) if (i, j) not in EARLY)
ORDER = (
    ("oF", 0), ("oF", 1), ("oS", 0), ("hid",), ("att", 3), ("att", 0), ("att", 1), ("att", 2),
    ("rF", 1, 2), ("rF", 1, 1), ("rS", 0, 0), ("oS", 1), ("norm",), ("rF", 0, 1), ("sF", 0, 1),
    ("mul", 0, 0), ("le", 0), ("rF", 0, 2), ("rS", 1, 0), ("sF", 1, 2), ("sF", 0, 2), ("mul", 0, 1),
    ("le", 3), ("rS", 0, 1), ("sF", 1, 1), ("mul", 0, 3), ("le", 4), ("f3", 0), ("s3", 1, 0),
    ("s3", 0, 0), ("mul", 3, 0), ("le", 2), ("rS", 1, 2), ("s3", 0, 1), ("wp", 2), ("f3", 1),
    ("wp", 0), ("rS", 0, 2), ("wp", 1), ("rS", 1, 1), ("wp", 3), ("s3", 1, 2), ("rS", 0, 3),
    ("s3", 0, 2), ("rS", 1, 3), ("mul", 3, 1), ("mul", 1, 1), ("mul", 1, 0), ("le", 1),
    ("s3", 1, 1), ("mul", 2, 0), ("le", 5), ("free", 0, 0), ("free", 1, 0), ("s3", 0, 3),
    ("free", 0, 1), ("free", 1, 1), ("s3", 1, 3), ("mul", 3, 3), ("free", 0, 2), ("free", 1, 2),
    ("mul", 1, 3), ("mul", 0, 2), ("le", 6), ("mul", 3, 2), ("mul", 2, 1), ("mul", 2, 3),
    ("mul", 1, 2), ("mul", 2, 2), ("lg",), ("relay", 0, 0), ("relay", 1, 0), ("four", 8, 12),
    ("ab", 0), ("four", 12, 16), ("hand", 0, 5), ("free", 0, 3), ("free", 1, 3), ("relay", 0, 1),
    ("relay", 1, 1), ("hand", 0, 0, 7), ("ab", 1), ("hand", 1, 0, 7), ("fin", 0, 0), ("fin", 1, 0),
    ("hand", 0, 1, 6), ("relay", 0, 2), ("relay", 1, 2), ("hand", 1, 5), ("hand", 2, 0, 7),
    ("ab", 2), ("hand", 0, 2), ("fin", 0, 1), ("fin", 1, 1), ("hand", 1, 1, 6), ("hand", 3, 0, 7),
    ("r2", 0, 0), ("r2", 1, 0), ("hand", 2, 5), ("hand", 4, 0), ("hand", 5, 0), ("relay", 0, 3), ("relay", 1, 3),
    ("hand", 1, 2), ("ab", 3), ("close",), ("mean",), ("hand", 2, 1, 6), ("fin", 0, 2),
    ("fin", 1, 2), ("r2", 0, 1), ("r2", 1, 1), ("hand", 2, 2), ("fin", 0, 3), ("fin", 1, 3),
    ("f2", 0), ("f2", 1),
)
RS_OFFS = (2, 1, 3, 0)
NT = (((1,), (1,)), ((), ()))
TN = (((0,), (0,)), ((), ()))


def dot(a, b, dims=(((1,), (0,)), ((), ()))):
    return lax.dot_general(a, b, dims, preferred_element_type=F32)


def turn(x, cosine, sine):
    return x * cosine + pltpu.roll(x, HD // 2, 1) * sine


def kernel(
    hid_hbm, gt_hbm, cnt_ref, pos_ref, q_hbm, k_hbm, w_hbm, og_hbm,
    qgo, kgo, wgo, up,
    hid, gt, q, k, og, wf, normed, pnorm, gain, krot, qrot, probs, vg2, vals, lg, stg,
    rl, fin, rl2, fin2, wacc, cbuf, col, hin, fixr, rb, vlow, cosine, sine,
    loc, ssem, rf, rs, rp, cs, cr, ps, pr, lss, lsr, rrl, rfin, rrl2, rfin2, hs, hr, fx, rbs, rbr,
):
    sec = lax.axis_index("section")
    dp = lax.axis_index("dp")
    core = lax.rem(dp, 2)
    y = dp // 8
    z = lax.rem(dp // 2, 4)
    other = 1 - core

    def at(yy, zz, cc):
        return (sec, (yy * 4 + zz) * 2 + cc)

    def near(axis, step):
        if axis == "y":
            return at(lax.rem(y + step + 4, 4), z, core)
        return at(y, lax.rem(z + step + 4, 4), core)

    partner = at(y, z, other)

    def spot(yo, zo):
        return lax.rem(y + yo, 4) * 4 + lax.rem(z + zo, 4)

    def place(first, fo, so):
        return spot(fo, so) if first == "y" else spot(so, fo)

    gives_early = jnp.logical_and(sec != 0, sec != 4)
    gets_early = jnp.logical_and(sec != NS - 1, sec != 3)
    below = lax.rem(sec + NS - 1, NS)

    here = y * 4 + z

    loads = [
        pltpu.make_async_copy(k_hbm, k, loc.at[0]),
        pltpu.make_async_copy(q_hbm, q, loc.at[1]),
        pltpu.make_async_copy(og_hbm, og, loc.at[2]),
        pltpu.make_async_copy(hid_hbm, hid, loc.at[3]),
        pltpu.make_async_copy(gt_hbm, gt, loc.at[4]),
        pltpu.make_async_copy(w_hbm, wf.at[here, core], loc.at[5]),
    ]
    loads[0].start()
    loads[1].start()
    loads[2].start()
    cbuf[0] = jnp.full((8, 128), cnt_ref[0], jnp.int32)

    barrier = pltpu.get_barrier_semaphore()
    ids = [near("y", 1), near("y", -1), near("z", 1), near("z", -1), partner]
    ids += [(lax.rem(sec + i, NS), dp) for i in range(1, NS)]
    for one in ids:
        pl.semaphore_signal(barrier, inc=1, device_id=one, device_id_type=MESH)
    pl.semaphore_wait(barrier, len(ids))

    sent = []

    def send(src, dst, recv, device):
        copy = pltpu.make_async_remote_copy(
            src_ref=src, dst_ref=dst, send_sem=ssem.at[len(sent)], recv_sem=recv,
            device_id=device, device_id_type=MESH,
        )
        sent.append(copy)
        copy.start()

    def arrived(dst, recv):
        pltpu.make_async_remote_copy(
            src_ref=dst, dst_ref=dst, send_sem=ssem.at[0], recv_sem=recv,
            device_id=partner, device_id_type=MESH,
        ).wait_recv()

    HALF = (pl.ds(0, 128), pl.ds(128, 128))
    FULL = pl.ds(0, SH)

    def piece(c, fo, so, rows):
        first, _, c0, cw = COLOURS[c]
        return wf.at[place(first, fo, so), core, rows, pl.ds(c0, cw)]

    def to_second(c, fi):
        first, second, c0, cw = COLOURS[c]
        src = w_hbm.at[:, pl.ds(c0, cw)] if fi == 0 else piece(c, OFFS[fi], 0, FULL)
        dst = piece(c, OFFS[fi], 0, FULL)
        send(src, dst, rs.at[c, fi, 0], near(second, 1))
        send(src, dst, rs.at[c, fi, 1], near(second, -1))

    def to_partner(c, fi, si):
        first, second, c0, cw = COLOURS[c]
        dst = piece(c, OFFS[fi], OFFS[si], FULL)
        src = w_hbm.at[:, pl.ds(c0, cw)] if fi == 0 and si == 0 else dst
        send(src, dst, rp.at[c, fi, si], partner)

    def first_own(c):
        _, _, c0, cw = COLOURS[c]
        first, src, dst = COLOURS[c][0], w_hbm.at[:, pl.ds(c0, cw)], piece(c, 0, 0, FULL)
        send(src, dst, rf.at[c, 0], near(first, 1))
        send(src, dst, rf.at[c, 1], near(first, -1))
        to_partner(c, 0, 0)

    def first12(c, fi):
        step, half = ((1, 0), (-1, 1))[fi - 1]
        arrived(piece(c, OFFS[fi], 0, FULL), rf.at[c, fi - 1])
        part = piece(c, OFFS[fi], 0, HALF[half])
        send(part, part, rf.at[c, 2 + half], near(COLOURS[c][0], step))
        to_partner(c, fi, 0)

    def first3(c):
        for half in (0, 1):
            arrived(piece(c, 2, 0, HALF[half]), rf.at[c, 2 + half])
        to_second(c, 3)
        to_partner(c, 3, 0)

    def second12(c, fi):
        second = COLOURS[c][1]
        for si, (step, half) in ((1, (1, 0)), (2, (-1, 1))):
            arrived(piece(c, OFFS[fi], OFFS[si], FULL), rs.at[c, fi, si - 1])
            part = piece(c, OFFS[fi], OFFS[si], HALF[half])
            send(part, part, rs.at[c, fi, 2 + half], near(second, step))
            to_partner(c, fi, si)

    def second3(c, fi):
        for half in (0, 1):
            arrived(piece(c, OFFS[fi], 2, HALF[half]), rs.at[c, fi, 2 + half])
        to_partner(c, fi, 3)

    def from_partner(c, fi, si):
        first, _, c0, cw = COLOURS[c]
        arrived(
            wf.at[place(first, OFFS[fi], OFFS[si]), other, FULL, pl.ds(c0, cw)], rp.at[c, fi, si]
        )

    def multiply(yo, zo):
        from_partner(0, INDEX[zo], INDEX[yo])
        from_partner(1, INDEX[yo], INDEX[zo])
        p = spot(yo, zo)
        vals[...] += dot(normed[p, 0], wf[p, 0]) + dot(normed[p, 1], wf[p, 1])

    def chunk(ref, i):
        return ref.at[:, pl.ds(pl.multiple_of(i * 512, 512), 512)]

    def ahead(i):
        p = spot(*EARLY[i])
        return pltpu.make_async_remote_copy(
            src_ref=chunk(hid_hbm, p), dst_ref=hin.at[i], send_sem=hs.at[i], recv_sem=hr.at[i],
            device_id=(below, dp), device_id_type=MESH,
        )

    def passing(i):
        return pltpu.make_async_remote_copy(
            src_ref=chunk(lg, i), dst_ref=chunk(up, i), send_sem=lss.at[i], recv_sem=lsr.at[i],
            device_id=(below, dp), device_id_type=MESH,
        )

    def first_term(p):
        cols = pl.ds(pl.multiple_of(p * 512, 512), 512)
        d_normed = dot(vg2[0], wf[p].reshape(512, E), NT)
        inv = jnp.concatenate([col[0]] * 4, axis=1)
        return cols, inv * (gain[:, cols] * d_normed)

    def leave_early(i):
        p = spot(*EARLY[i])

        @pl.when(gives_early)
        def _():
            cols, term = first_term(p)
            lg[:, cols] = term.astype(BF16)
            passing(p).start()

    def fixing():
        return pltpu.make_async_remote_copy(
            src_ref=col.at[1], dst_ref=fixr, send_sem=fx.at[0], recv_sem=fx.at[1],
            device_id=(below, dp), device_id_type=MESH,
        )

    def whole_term(p):
        cols, term = first_term(p)
        fix = jnp.concatenate([col[1]] * 4, axis=1)
        lg[:, cols] = (term - hid[:, cols].astype(F32) * fix).astype(BF16)

    def counting(i):
        return pltpu.make_async_remote_copy(
            src_ref=cbuf.at[0], dst_ref=cbuf.at[i], send_sem=cs.at[i - 1], recv_sem=cr.at[i - 1],
            device_id=(lax.rem(sec + i, NS), dp), device_id_type=MESH,
        )

    def hidden_ahead():
        for i in range(1, NS):
            counting(i).start()
        for load in loads[3:]:
            load.start()

        @pl.when(gives_early)
        def _():
            for i in range(len(EARLY)):
                ahead(i).start()

        places = jnp.broadcast_to(pos_ref[...].astype(F32), (T, HD)).T
        lane = lax.broadcasted_iota(jnp.int32, (T, HD), 1)
        entry = jnp.where(lane < HD // 2, lane, lane - HD // 2).astype(F32)
        angle = places * jnp.exp(entry * (-2.0 * math.log(500000.0) / HD))
        cosine[...] = jnp.cos(angle)
        sine[...] = jnp.where(lane < HD // 2, -1.0, 1.0) * jnp.sin(angle)
        for load in loads[:3]:
            load.wait()
        for g in range(HK):
            k_g = k[:, g * HD : (g + 1) * HD].astype(F32)
            krot[g] = turn(k_g, cosine[...], sine[...]).astype(BF16)

    def attend(g):
        for r in range(SHARE):
            h = g * SHARE + r
            qrot[g, r * T : (r + 1) * T] = turn(
                q[:, h * HD : (h + 1) * HD].astype(F32), cosine[...], sine[...]
            ).astype(BF16)
        total = jnp.zeros((T, HD), F32)
        for r in range(0, SHARE, 2):
            rows = slice(r * T, (r + 2) * T)
            scores = dot(qrot[g, rows], krot[g], NT) * SCALE
            row = lax.broadcasted_iota(jnp.int32, (2 * T, T), 0)
            row = jnp.where(row >= T, row - T, row)
            lane = lax.broadcasted_iota(jnp.int32, (2 * T, T), 1)
            scores = jnp.where(row >= lane, scores, -1e30)
            expo = jnp.exp(scores - jnp.max(scores, axis=-1, keepdims=True))
            p = expo / jnp.sum(expo, axis=-1, keepdims=True)
            probs[g, rows] = p
            h = g * SHARE + r
            d_out = jnp.concatenate(
                [og[:, h * HD : (h + 1) * HD], og[:, (h + 1) * HD : (h + 2) * HD]], axis=0
            )
            total = total + dot(p.astype(BF16), d_out, TN)
        vg2[0, :, g * HD : (g + 1) * HD] = total.astype(BF16)

    pair = pltpu.make_async_remote_copy(
        src_ref=normed.at[:, other], dst_ref=pnorm, send_sem=ps.at[0], recv_sem=pr.at[0],
        device_id=partner, device_id_type=MESH,
    )
    pair_vg = pltpu.make_async_remote_copy(
        src_ref=vg2.at[0], dst_ref=vg2.at[1], send_sem=ps.at[1], recv_sem=pr.at[1],
        device_id=partner, device_id_type=MESH,
    )

    def norm():
        pair_vg.start()
        for i in range(1, NS):
            counting(i).wait_recv()
        last = cbuf[0] - 1
        for i in range(1, NS):
            last = last + jnp.where(sec >= i, cbuf[i], 0)
        loads[3].wait()
        loads[4].wait()

        @pl.loop(0, 8)
        def _(i):
            cols = pl.ds(pl.multiple_of(i * 1024, 1024), 1024)
            rows = lax.broadcasted_iota(jnp.int32, (40, 1024), 0)
            table = gt[:, cols].astype(F32)
            same = rows == jnp.broadcast_to(last[0:1, 0:1], (40, 1024))
            gain[:, cols] = jnp.sum(jnp.where(same, table, 0.0), axis=0, keepdims=True)

        def squares(i, acc):
            x = hid[:, pl.ds(pl.multiple_of(i * SH, SH), SH)].astype(F32)
            return acc + x * x

        acc = lax.fori_loop(0, 32, squares, jnp.zeros((T, SH), F32))
        inverse = lax.rsqrt(jnp.sum(acc, axis=-1, keepdims=True) * (1.0 / D) + 1e-05)
        col[0] = jnp.broadcast_to(inverse, (T, 128))

        @pl.loop(0, 16)
        def _(i):
            for c in range(2):
                cols = pl.ds(pl.multiple_of(i * 512 + c * SH, SH), SH)
                x = hid[:, cols].astype(F32)
                inv = jnp.concatenate([col[0]] * 2, axis=1)
                normed[i, c] = (x * inv * gain[:, cols]).astype(BF16)

        pair.start()
        vals[...] = jnp.zeros((T, E), F32)
        loads[5].wait()

    def weight_part(p):
        left = jnp.concatenate([normed[p, core], pnorm[p]], axis=0)
        right = jnp.concatenate([vg2[0], vg2[1]], axis=0)
        stg[p] = dot(left, right, TN).astype(BF16)

    def weight_parts(yo):
        if not paired:
            paired.append(True)
            pair.wait_recv()
            pair_vg.wait_recv()

        @pl.loop(0, 4)
        def _(i):
            weight_part(lax.rem(y + yo, 4) * 4 + i)

    paired = []

    def rows_of(c, half):
        return pl.ds(SUMS[c][2] + half * (SUMS[c][3] // 2), SUMS[c][3] // 2)

    def part(c, fo, so, half):
        return stg.at[place(SUMS[c][0], fo, so), rows_of(c, half)]

    def free_sends(c, oi):
        so = RS_OFFS[oi]
        up1, down1 = near(SUMS[c][0], 1), near(SUMS[c][0], -1)
        for side, there in ((0, up1), (1, down1)):
            send(part(c, 2, so, side), rl.at[oi, side, rows_of(c, side)], rrl.at[c, oi, side], there)
        for side, fo, there in ((0, 1, up1), (1, 3, down1)):
            rows = rows_of(c, 1 - side)
            send(
                part(c, fo, so, 1 - side), fin.at[oi, side, rows], rfin.at[c, oi, side, 1 - side],
                there,
            )

    def relay(c, oi):
        for side, (fo, step) in enumerate(((1, 1), (3, -1))):
            rows = rows_of(c, side)
            arrived(rl.at[oi, side, rows], rrl.at[c, oi, side])
            p = place(SUMS[c][0], fo, RS_OFFS[oi])
            stg[p, rows] = (stg[p, rows].astype(F32) + rl[oi, side, rows].astype(F32)).astype(BF16)
            send(
                stg.at[p, rows], fin.at[oi, side, rows], rfin.at[c, oi, side, side],
                near(SUMS[c][0], step),
            )

    def finish(c, oi):
        so = RS_OFFS[oi]
        for side in range(2):
            for half in range(2):
                arrived(fin.at[oi, side, rows_of(c, half)], rfin.at[c, oi, side, half])
        p = place(SUMS[c][0], 0, so)
        rows = pl.ds(SUMS[c][2], SUMS[c][3])
        total = stg[p, rows].astype(F32)
        total = total + fin[oi, 0, rows].astype(F32) + fin[oi, 1, rows].astype(F32)
        if so == 0:
            wacc[rows] = total
            return
        stg[p, rows] = total.astype(BF16)
        up1, down1 = near(SUMS[c][1], 1), near(SUMS[c][1], -1)
        if so == 2:
            for side, there in ((0, up1), (1, down1)):
                send(part(c, 0, 2, side), rl2.at[side, rows_of(c, side)], rrl2.at[c, side], there)
        elif so == 1:
            send(part(c, 0, 1, 1), fin2.at[0, rows_of(c, 1)], rfin2.at[c, 0, 1], up1)
        else:
            send(part(c, 0, 3, 0), fin2.at[1, rows_of(c, 0)], rfin2.at[c, 1, 0], down1)

    def relay2(c, side):
        so, step = ((1, 1), (3, -1))[side]
        rows = rows_of(c, side)
        arrived(rl2.at[side, rows], rrl2.at[c, side])
        p = place(SUMS[c][0], 0, so)
        stg[p, rows] = (stg[p, rows].astype(F32) + rl2[side, rows].astype(F32)).astype(BF16)
        send(
            stg.at[p, rows], fin2.at[side, rows], rfin2.at[c, side, side], near(SUMS[c][1], step)
        )

    def finish2(c):
        for side in range(2):
            for half in range(2):
                arrived(fin2.at[side, rows_of(c, half)], rfin2.at[c, side, half])
        rows = pl.ds(SUMS[c][2], SUMS[c][3])
        total = wacc[rows] + fin2[0, rows].astype(F32) + fin2[1, rows].astype(F32)
        wgo[rows] = total.astype(BF16)

    def from_four(start, stop):
        @pl.when(sec == 4)
        def _():
            for n in range(start, stop):
                p = spot(n // 4, n % 4)
                whole_term(p)
                slot = n // 2 + 4 * (n % 2) if n < 6 else (n - 5) // 2 if n == 15 else (n - 6) // 2
                goal = 5 if n < 6 else 0 if n == 15 else 7 * (n % 2)
                pltpu.make_async_remote_copy(
                    src_ref=chunk(lg, p), dst_ref=rb.at[slot], send_sem=lss.at[p],
                    recv_sem=rbr.at[slot], device_id=(goal, dp), device_id_type=MESH,
                ).start()

    def late_terms():
        early_sends.extend(sent)
        inverse = col[0][:, 0:1]
        mean = jnp.sum(vg2[0].astype(F32) * vals[...], axis=-1, keepdims=True) * (1.0 / D)
        col[1] = jnp.broadcast_to(inverse * inverse * mean, (T, 128))

        @pl.when(gives_early)
        def _():
            fixing().start()

            for yo, zo in LATE:
                p = spot(yo, zo)
                whole_term(p)
                passing(p).start()

        from_four(0, 8)
        vlow[...] = vals[...].astype(BF16)

    HOPS = {
        0: [[(j, 3, min(6 + 2 * j, 15))] for j in range(6)],
        7: [[(j, 3, 7 + 2 * j)] for j in range(4)],
        5: [[(j, 1, None), (4 + j, 6, None)] for j in range(3)],
        1: [[(j, 2, None)] for j in range(3)],
        6: [[(4 + j, 2, None)] for j in range(3)],
        2: [[(j, 3, 2 * j), (4 + j, 3, 2 * j + 1)] for j in range(3)],
    }

    def handing(slot, goal, n):
        if n is None:
            dst, recv = rb.at[slot], rbr.at[slot]
        else:
            p = spot(n // 4, n % 4)
            dst, recv = chunk(up, p), lsr.at[p]
        return pltpu.make_async_remote_copy(
            src_ref=rb.at[slot], dst_ref=dst, send_sem=rbs.at[slot], recv_sem=recv,
            device_id=(goal, dp), device_id_type=MESH,
        )

    def hand_on(j, *sections):
        for one in sections:

            @pl.when(sec == one)
            def _():
                for hop in HOPS[one][j]:
                    arrived(rb.at[hop[0]], rbr.at[hop[0]])
                    handing(*hop).start()

    def attend_back(g):
        value = vlow[:, g * HD : (g + 1) * HD]
        total = jnp.zeros((T, HD), F32)
        for r in range(0, SHARE, 2):
            h = g * SHARE + r
            rows = slice(r * T, (r + 2) * T)
            d_out = jnp.concatenate(
                [og[:, h * HD : (h + 1) * HD], og[:, (h + 1) * HD : (h + 2) * HD]], axis=0
            )
            d_probs = dot(d_out, value, NT)
            p = probs[g, rows]
            low = p.astype(BF16).astype(F32)
            delta = jnp.sum(low * d_probs, axis=-1, keepdims=True)
            d_scores = (p * (d_probs - delta) * SCALE).astype(BF16)
            total = total + dot(d_scores, qrot[g, rows], TN)
            dq = dot(d_scores, krot[g])
            for i in range(2):
                one = turn(dq[i * T : (i + 1) * T], cosine[...], -sine[...])
                qgo[:, (h + i) * HD : (h + i + 1) * HD] = one.astype(BF16)
        kgo[:, g * HD : (g + 1) * HD] = turn(total, cosine[...], -sine[...]).astype(BF16)

    def take_off_mean():
        @pl.when(gets_early)
        def _():
            fixing().wait_recv()
            fix = jnp.concatenate([fixr[...]] * 4, axis=1)
            for i in range(len(EARLY)):
                p = spot(*EARLY[i])
                ahead(i).wait_recv()
                passing(p).wait_recv()
                cols = pl.ds(pl.multiple_of(p * 512, 512), 512)
                up[:, cols] = (up[:, cols].astype(F32) - hin[i].astype(F32) * fix).astype(BF16)

    early_sends = []

    def close_first_phase():
        for copy in early_sends:
            copy.wait_send()
        for i in range(1, NS):
            counting(i).wait_send()
        pair.wait_send()
        pair_vg.wait_send()

        @pl.when(sec == NS - 1)
        def _():
            up[...] = jnp.zeros((T, D), BF16)

        @pl.when(gives_early)
        def _():
            fixing().wait_send()
            for i in range(len(EARLY)):
                ahead(i).wait_send()

    steps = {
        "four": from_four, "mean": take_off_mean, "close": close_first_phase,
        "oF": first_own, "oS": lambda c: to_second(c, 0), "rF": first12, "sF": to_second,
        "f3": first3, "rS": second12, "s3": second3, "hid": hidden_ahead, "att": attend,
        "norm": norm, "wp": weight_parts, "mul": multiply, "le": leave_early, "lg": late_terms,
        "free": free_sends, "relay": relay, "fin": finish, "r2": relay2, "f2": finish2,
        "ab": attend_back, "hand": hand_on,
    }
    for step in ORDER:
        steps[step[0]](*step[1:])

    @pl.when(gets_early)
    def _():
        for yo, zo in LATE:
            passing(spot(yo, zo)).wait_recv()

    @pl.when(sec == 3)
    def _():
        @pl.loop(0, 16)
        def _(i):
            passing(i).wait_recv()

    for one, hops in HOPS.items():

        @pl.when(sec == one)
        def _():
            for pair_of in hops:
                for hop in pair_of:
                    handing(*hop).wait_send()

    @pl.when(sec > 0)
    def _():
        @pl.loop(0, 16)
        def _(i):
            passing(i).wait_send()

    for copy in sent[len(early_sends) :]:
        copy.wait_send()


def store(*refs):
    copies = [
        pltpu.make_async_copy(refs[i], refs[4 + i].at[0], refs[8].at[i]) for i in (3, 0, 2, 1)
    ]
    for copy in copies:
        copy.start()
    for copy in copies:
        copy.wait()


def shards(hidden, gain_table, layer_counts, positions, queries, keys, value_weight, out_grad):
    anywhere = pl.BlockSpec(memory_space=pl.ANY)
    vmem = pl.BlockSpec(memory_space=pltpu.VMEM)
    smem = pl.BlockSpec(memory_space=pltpu.SMEM)
    dma = pltpu.SemaphoreType.DMA
    scratch = [
        pltpu.VMEM((T, D), BF16),
        pltpu.VMEM((40, D), BF16),
        pltpu.VMEM((T, HQ * HD), BF16),
        pltpu.VMEM((T, HK * HD), BF16),
        pltpu.VMEM((T, HQ * HD), BF16),
        pltpu.VMEM((16, 2, SH, E), BF16),
        pltpu.VMEM((16, 2, T, SH), BF16),
        pltpu.VMEM((16, T, SH), BF16),
        pltpu.VMEM((1, D), F32),
        pltpu.VMEM((HK, T, HD), BF16),
        pltpu.VMEM((HK, SHARE * T, HD), BF16),
        pltpu.VMEM((HK, SHARE * T, T), F32),
        pltpu.VMEM((2, T, E), BF16),
        pltpu.VMEM((T, E), F32),
        pltpu.VMEM((T, D), BF16),
        pltpu.VMEM((16, SH, E), BF16),
    ]
    scratch += [
        pltpu.VMEM((4, 2, SH, E), BF16),
        pltpu.VMEM((4, 2, SH, E), BF16),
        pltpu.VMEM((2, SH, E), BF16),
        pltpu.VMEM((2, SH, E), BF16),
        pltpu.VMEM((SH, E), F32),
        pltpu.VMEM((NS, 8, 128), jnp.int32),
        pltpu.VMEM((2, T, 128), F32),
        pltpu.VMEM((len(EARLY), T, 512), BF16),
        pltpu.VMEM((T, 128), F32),
        pltpu.VMEM((8, T, 512), BF16),
        pltpu.VMEM((T, E), BF16),
        pltpu.VMEM((T, HD), F32),
        pltpu.VMEM((T, HD), F32),
        dma((6,)),
        dma((136,)),
        dma((2, 4)),
        dma((2, 4, 4)),
        dma((2, 4, 4)),
        dma((7,)),
        dma((7,)),
        dma((2,)),
        dma((2,)),
        dma((16,)),
        dma((16,)),
        dma((2, 4, 2)),
        dma((2, 4, 2, 2)),
        dma((2, 2)),
        dma((2, 2, 2)),
        dma((len(EARLY),)),
        dma((len(EARLY),)),
        dma((2,)),
        dma((8,)),
        dma((8,)),
    ]
    query_grad, key_grad, weight_grad, upstream = pl.pallas_call(
        kernel,
        out_shape=(
            pltpu.VMEM((T, HQ * HD), BF16),
            pltpu.VMEM((T, HK * HD), BF16),
            pltpu.VMEM((SH, E), BF16),
            pltpu.VMEM((T, D), BF16),
        ),
        in_specs=[anywhere, anywhere, smem, vmem] + [anywhere] * 4,
        out_specs=(vmem,) * 4,
        scratch_shapes=scratch,
        compiler_params=pltpu.CompilerParams(
            collective_id=0, has_side_effects=True, vmem_limit_bytes=56 << 20
        ),
    )(
        hidden[0], gain_table, layer_counts, positions, queries[0], keys[0], value_weight[0],
        out_grad[0],
    )
    grads = (query_grad, key_grad, weight_grad, upstream)
    return pl.pallas_call(
        store,
        out_shape=tuple(jax.ShapeDtypeStruct((1, *one.shape), BF16) for one in grads),
        in_specs=[anywhere] * 4,
        out_specs=(anywhere,) * 4,
        scratch_shapes=[dma((4,))],
        compiler_params=pltpu.CompilerParams(vmem_limit_bytes=1 << 20),
    )(*grads)


def solution(mesh):
    rows = P("section", "dp", None)
    in_specs = (rows, P(), P("section"), P("section", "dp"), rows, rows, rows, rows)
    return jax.shard_map(
        shards, mesh=mesh, in_specs=in_specs, out_specs=(rows,) * 4, check_vma=False
    )
```
